32 devices in a mesh: groups: 2 (over y), tm: 4 (over x, core), tensor: 4 (over z).
Axes of the slice: x: 2, y: 2, z: 4, core: 2. Of those that a mesh axis runs over, the one named last changes fastest.
Arguments:
- start_latent: float32 [256, 128], P(('groups', 'tensor')), parts along dimension 0, may hold values from -6 to 6
- time_index: int32 [8], P(('groups', 'tm')), parts along dimension 0, may hold values from 39 to 998, as said below
- step_weight: int32 [8], P(('groups', 'tm')), parts along dimension 0, may hold values from 1 to 16
- in_weight: bfloat16 [128, 3072], P('tm'), may hold values from -0.5 to 0.5
- mod_weight: bfloat16 [256, 9216], P(None, 'tensor'), may hold values from -0.375 to 0.375
- qkv_weight: bfloat16 [3072, 6144], P(None, 'tensor'), as said below
- out_weight: bfloat16 [2048, 3072], P('tensor'), may hold values from -0.125 to 0.125
- head_weight: bfloat16 [3072, 128], P('tm'), may hold values from -0.109375 to 0.109375
Outputs:
- window_latents: float32 [8, 128, 128], P(('groups', 'tm'), 'tensor'), parts along dimension 0
The draws below stay inside these ranges and needn't reach their ends.
There are 2 independent parts, one for each index of `groups`. The reference program is written for one: setup_inputs(seed, part) draws one part's arguments, and reference() takes and returns one part's arrays. A program takes and returns all parts, laid end to end along the dimension named above; an argument that names none is the same for every part. Nothing has to cross between parts.
Inputs may be any that keep to these rules, and one draw needn't show every extreme that they name: `time_index`: strictly decreasing indices of a 1000-step plan. `qkv_weight`: entries at most 24 / sqrt(3072) in magnitude.
All inputs are finite; a program needn't handle non-finite values.
Results may differ from the reference program's by a relative error of at most 0.0075.
Values may be sent and summed in bfloat16 or wider, within the bound.
No kernel may reach another device: no remote copies, remote signals or barrier semaphores. Data moves between devices by JAX's collectives and lax.ppermute only.
A program may use at most 64 MiB of HBM per device.

```python
import math
import jax
import jax.numpy as jnp
from jax import lax

D = 3072
HEADS = 16
HD = 128
C = 128
FREQ = 256
ITERS = 2
TOK = 128
TW = 4


def draw_time_index(key, part):
    spacing = jax.random.randint(jax.random.fold_in(key, 11), (TW,), 1, 960 // TW + 1)
    return (999 - jnp.cumsum(spacing)).astype(jnp.int32)


def draw_qkv_weight(key, part):
    columns = 3 * HEADS * HD
    base_key = jax.random.fold_in(key, 21)
    base = jax.random.truncated_normal(base_key, -4.0, 4.0, (D, columns), jnp.float32)
    chosen = jax.random.permutation(jax.random.fold_in(key, 22), HEADS)[:3]
    column_ids = jnp.arange(columns, dtype=jnp.int32)
    head_of_column = column_ids // (3 * HD)
    role_of_column = column_ids // HD % 3
    factor = jnp.ones((columns,), jnp.float32)
    factor = factor + 2.0 * (head_of_column == chosen[0]).astype(jnp.float32)
    factor = factor + 3.5 * (head_of_column == chosen[1]).astype(jnp.float32)
    factor = factor + 5.0 * (head_of_column == chosen[2]).astype(jnp.float32)
    factor = jnp.where(role_of_column < 2, factor, 1.0)
    return (base * factor[None, :] * float(D) ** (-0.5)).astype(jnp.bfloat16)


def place_ends(result, own_key, smallest, top_value):
    index_at = [jax.random.randint(jax.random.fold_in(own_key, axis), (), 0, length) for axis, length in enumerate(result.shape)]
    main_axis = result.shape.index(max(result.shape))
    neighbour = index_at[:main_axis] + [(index_at[main_axis] + 1) % result.shape[main_axis]] + index_at[main_axis + 1:]
    return result.at[tuple(index_at)].set(smallest).at[tuple(neighbour)].set(top_value)


def block_levels(rng, shape, shards, least, top_value):
    def one(axis_at, parts):
        steps = jax.random.uniform(jax.random.fold_in(jax.random.fold_in(rng, 6), axis_at), (parts,), jnp.float32, least / len(shards), top_value / len(shards))
        return jnp.repeat(jnp.exp(steps), shape[axis_at] // parts).reshape((-1,) + (1,) * (len(shape) - axis_at - 1))

    gain = one(*shards[0])
    for cut in shards[1:]:
        gain = gain * one(*cut)
    return gain


def normal_values(rng, shape, scale, bound, cuts=(), held_as=jnp.bfloat16):
    array = scale * jax.random.normal(rng, shape, jnp.float32)
    if cuts:
        array = array * block_levels(rng, shape, cuts, -0.22, 0.18)
    return jnp.clip(array, -bound, bound).astype(held_as)


def setup_inputs(seed: int = 0, part: int = 0) -> dict:
    keys = jax.random.split(jax.random.key(seed), 9)
    own_keys = jax.random.split(jax.random.fold_in(keys[8], part), 9)
    start_latent = normal_values(own_keys[0], (TOK, C), 1.0, 6.0, ((0, 4),), jnp.float32)
    time_index = draw_time_index(jax.random.fold_in(jax.random.fold_in(keys[8], part), 71), part)
    step_weight = place_ends(jax.random.randint(own_keys[2], (TW,), 1, 17), jax.random.fold_in(own_keys[2], 1), 1, 16).astype(jnp.int32)
    in_weight = normal_values(keys[3], (C, D), C ** -0.5, 0.5, ((0, 4),))
    mod_weight = normal_values(keys[4], (FREQ, 3 * D), FREQ ** -0.5, 0.375, ((1, 4),))
    qkv_weight = draw_qkv_weight(jax.random.fold_in(keys[8], 71), part)
    out_weight = normal_values(keys[6], (HEADS * HD, D), (HEADS * HD) ** -0.5, 0.125, ((0, 4),))
    head_weight = normal_values(keys[7], (D, C), D ** -0.5, 0.109375, ((0, 4),))
    return {"start_latent": start_latent, "time_index": time_index, "step_weight": step_weight, "in_weight": in_weight, "mod_weight": mod_weight, "qkv_weight": qkv_weight, "out_weight": out_weight, "head_weight": head_weight}


NORM_EPS = 1e-06
STEP_DIVISOR = 64.0

def embedding_of(time_index, width):
    half_width = width // 2
    frequency = jnp.exp(-math.log(10000.0) * jnp.arange(half_width).astype(jnp.float32) / half_width)
    angles = time_index.astype(jnp.float32)[:, None] * frequency[None, :]
    return jnp.concatenate([jnp.cos(angles), jnp.sin(angles)], axis=1)

def velocity_of(latents, modulation, in_weight, qkv_weight, out_weight, head_weight):
    shifts = modulation[:D]
    scales = modulation[D:2 * D]
    gate_rows = modulation[2 * D:]
    widened = jnp.dot(latents, in_weight, preferred_element_type=jnp.float32)
    row_mean = lax.optimization_barrier(jnp.mean(widened, axis=1, keepdims=True))
    centered = widened - row_mean
    spread = lax.optimization_barrier(jnp.mean(centered * centered, axis=1, keepdims=True))
    normed = (centered * lax.rsqrt(spread + NORM_EPS) * (1.0 + scales) + shifts).astype(jnp.bfloat16)
    qkv_rows = jnp.dot(normed, qkv_weight, preferred_element_type=jnp.float32).astype(jnp.bfloat16)
    packed = qkv_rows.reshape(TOK, HEADS, 3, HD).astype(jnp.float32)
    scores = jnp.einsum('qhe,khe->hqk', packed[:, :, 0], packed[:, :, 1]) * (1.0 / math.sqrt(HD))
    attention_weights = jax.nn.softmax(scores, axis=-1).astype(jnp.bfloat16)
    attention_weights = lax.optimization_barrier(attention_weights).astype(jnp.float32)
    attended = jnp.einsum('hqk,khe->qhe', attention_weights, packed[:, :, 2]).astype(jnp.bfloat16).reshape(TOK, HEADS * HD)
    scaled_out = (out_weight.astype(jnp.float32) * gate_rows[None, :]).astype(jnp.bfloat16)
    folded = jnp.dot(scaled_out, head_weight, preferred_element_type=jnp.float32).astype(jnp.bfloat16)
    residual = jnp.dot(widened.astype(jnp.bfloat16), head_weight, preferred_element_type=jnp.float32)
    return residual + jnp.dot(attended, folded, preferred_element_type=jnp.float32)

def reference(start_latent, time_index, step_weight, in_weight, mod_weight, qkv_weight, out_weight, head_weight):
    embedding = embedding_of(time_index, FREQ).astype(jnp.bfloat16)
    modulation = jnp.dot(embedding, mod_weight, preferred_element_type=jnp.float32)
    step_size = step_weight.astype(jnp.float32) / STEP_DIVISOR
    guesses = jnp.broadcast_to(start_latent.astype(jnp.bfloat16)[None], (TW, TOK, C))

    def one_timestep(pair):
        return velocity_of(pair[0], pair[1], in_weight, qkv_weight, out_weight, head_weight)
    window_end = start_latent[None]
    for iteration in range(ITERS):
        velocity = lax.map(one_timestep, (guesses, modulation))
        drifts = step_size[:, None, None] * velocity
        window_end = start_latent[None] + jnp.cumsum(drifts, axis=0)
        guesses = (window_end - drifts).astype(jnp.bfloat16)
    return window_end
```

```python
import functools
import math

import jax
import jax.numpy as jnp
from jax import lax
from jax.experimental import pallas as pl
from jax.experimental.pallas import tpu as pltpu
from jax.sharding import PartitionSpec as P

HD = 128
LANES = 128
ITERS = 2
NORM_EPS = 1e-06
STEP_DIVISOR = 64.0
F32 = jnp.float32
BF16 = jnp.bfloat16
VMEM = pl.BlockSpec(memory_space=pltpu.VMEM)
SMEM = pl.BlockSpec(memory_space=pltpu.SMEM)


def embedding_of(time_index, width):
    half_width = width // 2
    frequency = jnp.exp(
        -math.log(10000.0) * jnp.arange(half_width).astype(F32) / half_width
    )
    angles = time_index.astype(F32)[:, None] * frequency[None, :]
    return jnp.concatenate([jnp.cos(angles), jnp.sin(angles)], axis=1)


def is_small(axis):
    return lax.axis_size(axis) in (2, 4)


def swap(value, axis, k):
    n = lax.axis_size(axis)
    return lax.ppermute(value, axis, [(i, i ^ k) for i in range(n)])


def gather_parts(value, axis):
    if is_small(axis):
        return [value] + [swap(value, axis, k) for k in range(1, lax.axis_size(axis))]
    return [lax.all_gather(value, axis, axis=0, tiled=True)]


def gather_weight_parts(value, axis):
    n = lax.axis_size(axis)
    if n != 4:
        return gather_parts(value, axis)
    far = swap(value, axis, 2)
    near = swap(value, axis, 1)
    return [value, near, far, swap(far, axis, 1)]


def place(axis, parts, k):
    if parts == 1:
        return 0
    return lax.axis_index(axis) ^ k


def bdot(a, b):
    return jnp.dot(a, b, preferred_element_type=F32)


def bdot_t(a, b):
    return lax.dot_general(a, b, (((1,), (1,)), ((), ())), preferred_element_type=F32)


def split_terms(value, terms):
    out = []
    for _ in range(terms):
        piece = value.astype(BF16)
        out.append(piece)
        value = value - piece.astype(F32)
    return out


def modulation_kernel(emb_ref, weight_ref, start_ref, out_ref):
    rows = start_ref.shape[0]
    result = bdot(jnp.broadcast_to(emb_ref[...], (16, emb_ref.shape[1])), weight_ref[...])
    out_ref[0:rows, :] = start_ref[...]
    for r in range(weight_ref.shape[1] // LANES):
        out_ref[rows + r : rows + r + 1, :] = result[0:1, r * LANES : (r + 1) * LANES]


def attend(x, factors, base, gram, head_count):
    twice = jnp.concatenate([x, x], axis=1)
    thrice = jnp.concatenate([twice, x], axis=1)
    spread = jnp.sum(bdot(thrice, gram[...]) * x.astype(F32), axis=1, keepdims=True)
    scale = lax.rsqrt(jnp.maximum(spread, 0.0) + NORM_EPS)
    outs = []
    for h in range(head_count):
        cols = slice(h * 3 * HD, (h + 1) * 3 * HD)
        qkv = (bdot(twice, factors[:, cols]) * scale + base[0:1, cols]).astype(BF16)
        scores = bdot_t(qkv[:, :HD], qkv[:, HD : 2 * HD]) * (1.0 / math.sqrt(HD))
        top = jnp.max(scores, axis=1, keepdims=True)
        weights = jnp.exp(scores - top)
        weights = weights / jnp.sum(weights, axis=1, keepdims=True)
        outs.append(bdot(weights.astype(BF16), qkv[:, 2 * HD :]).astype(BF16))
    return outs[0] if head_count == 1 else jnp.concatenate(outs, axis=1)


def setup_kernel(nt, nm, rows, head_count, *refs):
    msgs, refs = refs[:nt], refs[nt:]
    inws, refs = refs[:nm], refs[nm:]
    qkv_ref, refs = refs[0], refs[1:]
    factor_ref, base_ref, gram_ref, start_ref, inw_ref, gate_ref, att_ref = refs[:7]
    start_s, mod_s, inw_s, z_s = refs[7:]
    for k in range(nt):
        at = place("tensor", nt, k)
        start_s[at] = msgs[k][0 : start_s.shape[1], :]
        mod_s[at, 0 : msgs[k].shape[0] - start_s.shape[1], :] = msgs[k][start_s.shape[1] :, :]
    for k in range(nm):
        inw_s[place("tm", nm, k)] = inws[k][...]
    channels, width = inw_ref.shape
    chunks = width // LANES
    per = 3 * chunks // nt

    def mod_row(r):
        return mod_s[r // per, r % per : r % per + 1, :]

    inw = inw_s[...].reshape(channels, width)
    inw_ref[...] = inw
    total = jnp.zeros((channels, LANES), F32)
    for c in range(chunks):
        total = total + inw[:, c * LANES : (c + 1) * LANES].astype(F32)
    mean = jnp.sum(total, axis=1, keepdims=True) * (1.0 / width)
    for c in range(chunks):
        cols = slice(c * LANES, (c + 1) * LANES)
        centered = inw[:, cols].astype(F32) - mean
        z_s[0:channels, cols] = (centered * (1.0 + mod_row(chunks + c))).astype(BF16)
        z_s[channels : channels + 16, cols] = jnp.broadcast_to(mod_row(c), (16, LANES)).astype(BF16)
        gate_ref[c : c + 1, :] = mod_row(2 * chunks + c)
    mean_b = jnp.broadcast_to(mean, (channels, channels))
    gram = bdot_t(inw, inw) * (1.0 / width) - mean_b * mean_b.T
    for i, piece in enumerate(split_terms(gram, 3)):
        gram_ref[i * channels : (i + 1) * channels, :] = piece
    start = start_s[...].reshape(start_ref.shape)
    start_ref[...] = start

    block = 3 * HD

    def columns(n, carry):
        at = pl.ds(pl.multiple_of(n * block, block), block)
        result = bdot(z_s[...], qkv_ref[:, at])
        high, low = split_terms(result[0:channels], 2)
        factor_ref[0:channels, at] = high
        factor_ref[channels : 2 * channels, at] = low
        base_ref[:, at] = result[channels : channels + 8]
        return carry

    lax.fori_loop(0, head_count, columns, 0)
    att_ref[...] = attend(start.astype(BF16), factor_ref, base_ref, gram_ref, head_count)


def add_own_rows(result, residual, rows):
    first = lax.axis_index("tensor") * rows
    at = lax.broadcasted_iota(jnp.int32, result.shape, 0)
    return result + jnp.where((at >= first) & (at < first + rows), residual, 0.0)


def step_size(step_ref):
    return step_ref[0].astype(F32) * (1.0 / STEP_DIVISOR)


def fold_kernel(nm, rows, *refs):
    heads, refs = refs[:nm], refs[nm:]
    step_ref, out_w_ref, gate_ref, inw_ref, att_ref, start_ref = refs[:6]
    fold_ref, resid_ref, vel_ref = refs[6:9]
    head_s, s_s = refs[9:]
    for k in range(nm):
        head_s[place("tm", nm, k)] = heads[k][...]
    span, width = out_w_ref.shape
    channels = inw_ref.shape[0]
    for c in range(width // LANES):
        cols = slice(c * LANES, (c + 1) * LANES)
        s_s[0:span, cols] = (out_w_ref[:, cols].astype(F32) * gate_ref[c : c + 1, :]).astype(BF16)
    s_s[span:, :] = inw_ref[...]
    head = head_s[...].reshape(width, head_s.shape[2])
    result = bdot(s_s[...], head)
    folded = result[0:span].astype(BF16)
    fold_ref[...] = folded
    for i, piece in enumerate(split_terms(result[span:], 2)):
        resid_ref[i * channels : (i + 1) * channels, :] = piece
    x = start_ref[...].astype(BF16)
    vel = bdot(att_ref[...], folded)
    residual = bdot(jnp.concatenate([x, x], axis=1), resid_ref[...])
    vel_ref[...] = (add_own_rows(vel, residual, rows) * step_size(step_ref)).astype(vel_ref.dtype)


def iterate_kernel(nparts, rows, head_count, split, *refs):
    parts, refs = refs[:nparts], refs[nparts:]
    step_ref, start_ref, factor_ref, base_ref, gram_ref, fold_ref, resid_ref = refs[:7]
    outs = refs[7:-1]
    vel_s = refs[-1]
    guess = start_ref[...]
    for part in parts:
        guess = guess + part[...].astype(F32)
    x = guess.astype(BF16)
    attended = attend(x, factor_ref, base_ref, gram_ref, head_count)
    vel = bdot(attended, fold_ref[...])
    residual = bdot(jnp.concatenate([x, x], axis=1), resid_ref[...])
    vel = add_own_rows(vel, residual, rows) * step_size(step_ref)
    if not split:
        outs[0][...] = vel.astype(outs[0].dtype)
        return
    vel_s[...] = vel.reshape(vel_s.shape)
    for k in range(len(outs)):
        outs[k][...] = vel_s[lax.axis_index("tensor") ^ k]


def shape_of(shape, dtype):
    return jax.ShapeDtypeStruct(shape, dtype)


PARAMS = pltpu.CompilerParams(vmem_limit_bytes=40 * 2**20)


def call(kernel, name, outs, in_specs, scratch, *args):
    return pl.pallas_call(
        kernel,
        name=name,
        out_shape=outs,
        in_specs=in_specs,
        out_specs=[VMEM] * len(outs),
        scratch_shapes=scratch,
        compiler_params=PARAMS,
    )(*args)


def sum_earlier(parts, inclusive):
    me = lax.axis_index("tm")
    total = parts[0].astype(F32) if inclusive else jnp.zeros(parts[0].shape, F32)
    for k in range(1, len(parts)):
        total = total + jnp.where((me ^ k) < me, parts[k].astype(F32), 0.0)
    return total


def earlier_sum(value, inclusive):
    if is_small("tm"):
        return sum_earlier(gather_parts(value, "tm"), inclusive)
    everything = lax.all_gather(value, "tm").astype(F32)
    index = jnp.arange(everything.shape[0]).reshape((-1,) + (1,) * value.ndim)
    me = lax.axis_index("tm")
    keep = index <= me if inclusive else index < me
    return jnp.sum(jnp.where(keep, everything, 0.0), axis=0)


def local(
    start_latent,
    time_index,
    step_weight,
    in_weight,
    mod_weight,
    qkv_weight,
    out_weight,
    head_weight,
):
    rows, channels = start_latent.shape
    n_tensor = lax.axis_size("tensor")
    tokens = rows * n_tensor
    width = in_weight.shape[1]
    chunks = width // LANES
    head_count = qkv_weight.shape[1] // (3 * HD)
    span = out_weight.shape[0]

    inw_parts = gather_weight_parts(in_weight, "tm")
    embedding = embedding_of(time_index, mod_weight.shape[0]).astype(BF16)
    small = is_small("tensor") and mod_weight.shape[1] % LANES == 0
    if small:
        mod_rows = mod_weight.shape[1] // LANES
        message = call(
            modulation_kernel,
            "modulation",
            [shape_of((rows + mod_rows, LANES), F32)],
            [VMEM] * 3,
            [],
            embedding,
            mod_weight,
            start_latent,
        )[0]
        messages = gather_parts(message, "tensor")
        block_rows = rows
    else:
        mod_part = jnp.dot(embedding, mod_weight, preferred_element_type=F32)
        modulation = lax.all_gather(mod_part, "tensor", axis=1, tiled=True)
        start_all = lax.all_gather(start_latent, "tensor", axis=0, tiled=True)
        messages = [jnp.concatenate([start_all, modulation.reshape(-1, LANES)], axis=0)]
        block_rows = tokens
    nt, nm = len(messages), len(inw_parts)
    mod_rows = messages[0].shape[0] - block_rows
    padded = -(-mod_rows // 8) * 8
    factor, base, gram, start_all, inw_all, gate, attended = call(
        functools.partial(setup_kernel, nt, nm, rows, head_count),
        "setup",
        [
            shape_of((2 * channels, qkv_weight.shape[1]), BF16),
            shape_of((8, qkv_weight.shape[1]), F32),
            shape_of((3 * channels, channels), BF16),
            shape_of((tokens, channels), F32),
            shape_of((channels, width), BF16),
            shape_of((chunks, LANES), F32),
            shape_of((tokens, head_count * HD), BF16),
        ],
        [VMEM] * (nt + nm + 1),
        [
            pltpu.VMEM((nt, block_rows, channels), F32),
            pltpu.VMEM((nt, padded, LANES), F32),
            pltpu.VMEM((nm, channels // nm, width), BF16),
            pltpu.VMEM((channels + 16, width), BF16),
        ],
        *messages,
        *inw_parts,
        qkv_weight,
    )
    head_parts = gather_weight_parts(head_weight, "tm")
    folded, resid, vel = call(
        functools.partial(fold_kernel, nm, rows),
        "fold",
        [
            shape_of((span, channels), BF16),
            shape_of((2 * channels, channels), BF16),
            shape_of((tokens, channels), BF16),
        ],
        [VMEM] * nm + [SMEM] + [VMEM] * 5,
        [
            pltpu.VMEM((nm, width // nm, channels), BF16),
            pltpu.VMEM((span + channels, width), BF16),
        ],
        *head_parts,
        step_weight,
        out_weight,
        gate,
        inw_all,
        attended,
        start_all,
    )
    small = is_small("tensor")
    for iteration in range(1, ITERS):
        last = iteration + 1 == ITERS
        earlier = earlier_sum(vel, False)
        if small:
            pieces = gather_parts(earlier.astype(BF16), "tensor")
        else:
            pieces = [lax.psum(earlier, "tensor")]
        split = last and small
        if split:
            outs = [shape_of((rows, channels), F32)] * n_tensor
        else:
            outs = [shape_of((tokens, channels), F32 if last else BF16)]
        vels = call(
            functools.partial(iterate_kernel, len(pieces), rows, head_count, split),
            "iterate",
            outs,
            [VMEM] * len(pieces) + [SMEM] + [VMEM] * 6,
            [pltpu.VMEM((n_tensor, rows, channels), F32)],
            *pieces,
            step_weight,
            start_all,
            factor,
            base,
            gram,
            folded,
            resid,
        )
        vel = vels[0]
    if small:
        drift = vels[0]
        for k in range(1, n_tensor):
            drift = drift + swap(vels[k], "tensor", k)
    else:
        drift = lax.psum_scatter(vel, "tensor", scatter_dimension=0, tiled=True)
    return (start_latent + earlier_sum(drift, True))[None]


def solution(mesh):
    return jax.shard_map(
        local,
        mesh=mesh,
        in_specs=(
            P(("groups", "tensor"), None),
            P(("groups", "tm")),
            P(("groups", "tm")),
            P("tm", None),
            P(None, "tensor"),
            P(None, "tensor"),
            P("tensor", None),
            P("tm", None),
        ),
        out_specs=P(("groups", "tm"), "tensor", None),
        check_vma=False,
    )
```

```python
import functools
import math

import jax
import jax.numpy as jnp
from jax import lax
from jax.experimental import pallas as pl
from jax.experimental.pallas import tpu as pltpu
from jax.sharding import PartitionSpec as P


HD = 128
LANES = 128
ITERS = 2
NORM_EPS = 1e-06
STEP_DIVISOR = 64.0
F32 = jnp.float32
BF16 = jnp.bfloat16
VMEM = pl.BlockSpec(memory_space=pltpu.VMEM)
SMEM = pl.BlockSpec(memory_space=pltpu.SMEM)


def embedding_of(time_index, width):
    half_width = width // 2
    frequency = jnp.exp(
        -math.log(10000.0) * jnp.arange(half_width).astype(F32) / half_width
    )
    angles = time_index.astype(F32)[:, None] * frequency[None, :]
    return jnp.concatenate([jnp.cos(angles), jnp.sin(angles)], axis=1)


def is_small(axis):
    return lax.axis_size(axis) in (2, 4)


def swap(value, axis, k):
    n = lax.axis_size(axis)
    return lax.ppermute(value, axis, [(i, i ^ k) for i in range(n)])


def gather_parts(value, axis):
    if is_small(axis):
        return [value] + [swap(value, axis, k) for k in range(1, lax.axis_size(axis))]
    return [lax.all_gather(value, axis, axis=0, tiled=True)]


def gather_weight_parts(value, axis):
    n = lax.axis_size(axis)
    if n != 4:
        return gather_parts(value, axis)
    far = swap(value, axis, 2)
    near = swap(value, axis, 1)
    return [value, near, far, swap(far, axis, 1)]


def place(axis, parts, k):
    if parts == 1:
        return 0
    return lax.axis_index(axis) ^ k


def bdot(a, b):
    return jnp.dot(a, b, preferred_element_type=F32)


def bdot_t(a, b):
    return lax.dot_general(a, b, (((1,), (1,)), ((), ())), preferred_element_type=F32)


def split_terms(value, terms):
    out = []
    for _ in range(terms):
        piece = value.astype(BF16)
        out.append(piece)
        value = value - piece.astype(F32)
    return out


def modulation_kernel(emb_ref, weight_hbm, start_hbm, out_ref, weight_ref, start_ref, sems):
    rows = start_ref.shape[0]
    copies = [
        pltpu.make_async_copy(weight_hbm, weight_ref, sems.at[0]),
        pltpu.make_async_copy(start_hbm, start_ref, sems.at[1]),
    ]
    for copy in copies:
        copy.start()
    for copy in copies:
        copy.wait()
    result = bdot(jnp.broadcast_to(emb_ref[...], (16, emb_ref.shape[1])), weight_ref[...])
    out_ref[0:rows, :] = start_ref[...]
    for r in range(weight_ref.shape[1] // LANES):
        out_ref[rows + r : rows + r + 1, :] = result[0:1, r * LANES : (r + 1) * LANES]


def load_kernel(source, out_ref, sems):
    n = sems.shape[0]
    rows = source.shape[0] // n
    copies = [
        pltpu.make_async_copy(
            source.at[pl.ds(i * rows, rows)], out_ref.at[pl.ds(i * rows, rows)], sems.at[i]
        )
        for i in range(n)
    ]
    for copy in copies:
        copy.start()
    for copy in copies:
        copy.wait()


def attend(x, factors, base, gram, head_count):
    twice = jnp.concatenate([x, x], axis=1)
    thrice = jnp.concatenate([twice, x], axis=1)
    spread = jnp.sum(bdot(thrice, gram[...]) * x.astype(F32), axis=1, keepdims=True)
    scale = lax.rsqrt(jnp.maximum(spread, 0.0) + NORM_EPS)
    outs = []
    for h in range(head_count):
        cols = slice(h * 3 * HD, (h + 1) * 3 * HD)
        qkv = (bdot(twice, factors[:, cols]) * scale + base[0:1, cols]).astype(BF16)
        scores = bdot_t(qkv[:, :HD], qkv[:, HD : 2 * HD]) * (1.0 / math.sqrt(HD))
        top = jnp.max(scores, axis=1, keepdims=True)
        weights = jnp.exp(scores - top)
        weights = weights / jnp.sum(weights, axis=1, keepdims=True)
        outs.append(bdot(weights.astype(BF16), qkv[:, 2 * HD :]).astype(BF16))
    return outs[0] if head_count == 1 else jnp.concatenate(outs, axis=1)


def setup_kernel(nt, nm, head_count, *refs):
    msgs, refs = refs[:nt], refs[nt:]
    inws, refs = refs[:nm], refs[nm:]
    qkv_ref, refs = refs[0], refs[1:]
    factor_ref, base_ref, gram_ref, start_ref, inw_ref, gate_ref = refs[:6]
    start_s, mod_s, inw_s, z_s = refs[6:]
    for k in range(nt):
        at = place("tensor", nt, k)
        start_s[at] = msgs[k][0 : start_s.shape[1], :]
        mod_s[at, 0 : msgs[k].shape[0] - start_s.shape[1], :] = msgs[k][start_s.shape[1] :, :]
    for k in range(nm):
        inw_s[place("tm", nm, k)] = inws[k][...]
    channels, width = inw_ref.shape
    chunks = width // LANES
    per = 3 * chunks // nt

    def mod_row(r):
        return mod_s[r // per, r % per : r % per + 1, :]

    inw = inw_s[...].reshape(channels, width)
    inw_ref[...] = inw
    total = jnp.zeros((channels, LANES), F32)
    for c in range(chunks):
        total = total + inw[:, c * LANES : (c + 1) * LANES].astype(F32)
    mean = jnp.sum(total, axis=1, keepdims=True) * (1.0 / width)
    for c in range(chunks):
        cols = slice(c * LANES, (c + 1) * LANES)
        centered = inw[:, cols].astype(F32) - mean
        z_s[0:channels, cols] = (centered * (1.0 + mod_row(chunks + c))).astype(BF16)
        z_s[channels : channels + 16, cols] = jnp.broadcast_to(mod_row(c), (16, LANES)).astype(BF16)
        gate_ref[c : c + 1, :] = mod_row(2 * chunks + c)
    mean_b = jnp.broadcast_to(mean, (channels, channels))
    gram = bdot_t(inw, inw) * (1.0 / width) - mean_b * mean_b.T
    for i, piece in enumerate(split_terms(gram, 3)):
        gram_ref[i * channels : (i + 1) * channels, :] = piece
    start = start_s[...].reshape(start_ref.shape)
    start_ref[...] = start

    block = 3 * HD

    def columns(n, carry):
        at = pl.ds(pl.multiple_of(n * block, block), block)
        result = bdot(z_s[...], qkv_ref[:, at])
        high, low = split_terms(result[0:channels], 2)
        factor_ref[0:channels, at] = high
        factor_ref[channels : 2 * channels, at] = low
        base_ref[:, at] = result[channels : channels + 8]
        return carry

    lax.fori_loop(0, head_count, columns, 0)


def attend_kernel(head_count, start_ref, factor_ref, base_ref, gram_ref, out_ref):
    x = start_ref[...].astype(BF16)
    out_ref[...] = attend(x, factor_ref, base_ref, gram_ref, head_count)


def add_own_rows(result, residual, rows):
    first = lax.axis_index("tensor") * rows
    at = lax.broadcasted_iota(jnp.int32, result.shape, 0)
    return result + jnp.where((at >= first) & (at < first + rows), residual, 0.0)


def step_size(step_ref):
    return step_ref[0].astype(F32) * (1.0 / STEP_DIVISOR)


def fold_kernel(nm, rows, *refs):
    heads, refs = refs[:nm], refs[nm:]
    step_ref, out_w_ref, gate_ref, inw_ref, att_ref, start_ref = refs[:6]
    fold_ref, resid_ref, vel_ref = refs[6:9]
    head_s, s_s = refs[9:]
    for k in range(nm):
        head_s[place("tm", nm, k)] = heads[k][...]
    span, width = out_w_ref.shape
    channels = inw_ref.shape[0]
    for c in range(width // LANES):
        cols = slice(c * LANES, (c + 1) * LANES)
        s_s[0:span, cols] = (out_w_ref[:, cols].astype(F32) * gate_ref[c : c + 1, :]).astype(BF16)
    s_s[span:, :] = inw_ref[...]
    head = head_s[...].reshape(width, head_s.shape[2])
    result = bdot(s_s[...], head)
    folded = result[0:span].astype(BF16)
    fold_ref[...] = folded
    for i, piece in enumerate(split_terms(result[span:], 2)):
        resid_ref[i * channels : (i + 1) * channels, :] = piece
    x = start_ref[...].astype(BF16)
    vel = bdot(att_ref[...], folded)
    residual = bdot(jnp.concatenate([x, x], axis=1), resid_ref[...])
    vel_ref[...] = (add_own_rows(vel, residual, rows) * step_size(step_ref)).astype(vel_ref.dtype)


def iterate_kernel(nparts, rows, head_count, split, *refs):
    parts, refs = refs[:nparts], refs[nparts:]
    step_ref, start_ref, factor_ref, base_ref, gram_ref, fold_ref, resid_ref = refs[:7]
    outs = refs[7:-1]
    vel_s = refs[-1]
    guess = start_ref[...]
    for part in parts:
        guess = guess + part[...].astype(F32)
    x = guess.astype(BF16)
    attended = attend(x, factor_ref, base_ref, gram_ref, head_count)
    vel = bdot(attended, fold_ref[...])
    residual = bdot(jnp.concatenate([x, x], axis=1), resid_ref[...])
    vel = add_own_rows(vel, residual, rows) * step_size(step_ref)
    if not split:
        outs[0][...] = vel.astype(outs[0].dtype)
        return
    vel_s[...] = vel.reshape(vel_s.shape)
    for k in range(len(outs)):
        outs[k][...] = vel_s[lax.axis_index("tensor") ^ k]


def shape_of(shape, dtype):
    return jax.ShapeDtypeStruct(shape, dtype)


def call(kernel, outs, in_specs, scratch, *args, cost=4 * 2**20, limit=8):
    return pl.pallas_call(
        kernel,
        out_shape=outs,
        in_specs=in_specs,
        out_specs=[VMEM] * len(outs),
        scratch_shapes=scratch,
        compiler_params=pltpu.CompilerParams(vmem_limit_bytes=limit * 2**20),
        cost_estimate=pl.CostEstimate(flops=0, bytes_accessed=cost, transcendentals=0),
    )(*args)


def sum_earlier(parts, inclusive):
    me = lax.axis_index("tm")
    total = parts[0].astype(F32) if inclusive else jnp.zeros(parts[0].shape, F32)
    for k in range(1, len(parts)):
        total = total + jnp.where((me ^ k) < me, parts[k].astype(F32), 0.0)
    return total


def earlier_sum(value, inclusive):
    if is_small("tm"):
        return sum_earlier(gather_parts(value, "tm"), inclusive)
    everything = lax.all_gather(value, "tm").astype(F32)
    index = jnp.arange(everything.shape[0]).reshape((-1,) + (1,) * value.ndim)
    me = lax.axis_index("tm")
    keep = index <= me if inclusive else index < me
    return jnp.sum(jnp.where(keep, everything, 0.0), axis=0)


def local(
    start_latent,
    time_index,
    step_weight,
    in_weight,
    mod_weight,
    qkv_weight,
    out_weight,
    head_weight,
):
    rows, channels = start_latent.shape
    n_tensor = lax.axis_size("tensor")
    tokens = rows * n_tensor
    width = in_weight.shape[1]
    chunks = width // LANES
    head_count = qkv_weight.shape[1] // (3 * HD)
    span = out_weight.shape[0]

    inw_parts = gather_weight_parts(in_weight, "tm")
    embedding = embedding_of(time_index, mod_weight.shape[0]).astype(BF16)
    small = is_small("tensor") and mod_weight.shape[1] % LANES == 0
    if small:
        mod_rows = mod_weight.shape[1] // LANES
        message = call(
            modulation_kernel,
            [shape_of((rows + mod_rows, LANES), F32)],
            [VMEM] + [pl.BlockSpec(memory_space=pltpu.HBM)] * 2,
            [
                pltpu.VMEM(mod_weight.shape, BF16),
                pltpu.VMEM(start_latent.shape, F32),
                pltpu.SemaphoreType.DMA((2,)),
            ],
            embedding,
            mod_weight,
            start_latent,
            limit=62,
        )[0]
        messages = gather_parts(message, "tensor")
        block_rows = rows
    else:
        mod_part = jnp.dot(embedding, mod_weight, preferred_element_type=F32)
        modulation = lax.all_gather(mod_part, "tensor", axis=1, tiled=True)
        start_all = lax.all_gather(start_latent, "tensor", axis=0, tiled=True)
        messages = [jnp.concatenate([start_all, modulation.reshape(-1, LANES)], axis=0)]
        block_rows = tokens
    nt, nm = len(messages), len(inw_parts)
    qkv_near = call(
        load_kernel,
        [shape_of(qkv_weight.shape, BF16)],
        [pl.BlockSpec(memory_space=pltpu.HBM)],
        [pltpu.SemaphoreType.DMA((4,))],
        qkv_weight,
        limit=40,
    )[0]
    mod_rows = messages[0].shape[0] - block_rows
    padded = -(-mod_rows // 8) * 8
    factor, base, gram, start_all, inw_all, gate = call(
        functools.partial(setup_kernel, nt, nm, head_count),
        [
            shape_of((2 * channels, qkv_weight.shape[1]), BF16),
            shape_of((8, qkv_weight.shape[1]), F32),
            shape_of((3 * channels, channels), BF16),
            shape_of((tokens, channels), F32),
            shape_of((channels, width), BF16),
            shape_of((chunks, LANES), F32),
        ],
        [VMEM] * (nt + nm + 1),
        [
            pltpu.VMEM((nt, block_rows, channels), F32),
            pltpu.VMEM((nt, padded, LANES), F32),
            pltpu.VMEM((nm, channels // nm, width), BF16),
            pltpu.VMEM((channels + 16, width), BF16),
        ],
        *messages,
        *inw_parts,
        qkv_near,
        limit=24,
    )
    attended = call(
        functools.partial(attend_kernel, head_count),
        [shape_of((tokens, head_count * HD), BF16)],
        [VMEM] * 4,
        [],
        start_all,
        factor,
        base,
        gram,
    )[0]
    head_parts = gather_weight_parts(head_weight, "tm")
    folded, resid, vel = call(
        functools.partial(fold_kernel, nm, rows),
        [
            shape_of((span, channels), BF16),
            shape_of((2 * channels, channels), BF16),
            shape_of((tokens, channels), BF16),
        ],
        [VMEM] * nm + [SMEM] + [VMEM] * 5,
        [
            pltpu.VMEM((nm, width // nm, channels), BF16),
            pltpu.VMEM((span + channels, width), BF16),
        ],
        *head_parts,
        step_weight,
        out_weight,
        gate,
        inw_all,
        attended,
        start_all,
        limit=24,
    )
    small = is_small("tensor")
    for iteration in range(1, ITERS):
        last = iteration + 1 == ITERS
        earlier = earlier_sum(vel, False)
        if small:
            pieces = gather_parts(earlier.astype(BF16), "tensor")
        else:
            pieces = [lax.psum(earlier, "tensor")]
        split = last and small
        if split:
            outs = [shape_of((rows, channels), F32)] * n_tensor
        else:
            outs = [shape_of((tokens, channels), F32 if last else BF16)]
        vels = call(
            functools.partial(iterate_kernel, len(pieces), rows, head_count, split),
            outs,
            [VMEM] * len(pieces) + [SMEM] + [VMEM] * 6,
            [pltpu.VMEM((n_tensor, rows, channels), F32)],
            *pieces,
            step_weight,
            start_all,
            factor,
            base,
            gram,
            folded,
            resid,
        )
        vel = vels[0]
    if small:
        drift = vels[0]
        for k in range(1, n_tensor):
            drift = drift + swap(vels[k], "tensor", k)
    else:
        drift = lax.psum_scatter(vel, "tensor", scatter_dimension=0, tiled=True)
    return (start_latent + earlier_sum(drift, True))[None]


def solution(mesh):
    return jax.shard_map(
        local,
        mesh=mesh,
        in_specs=(
            P(("groups", "tensor"), None),
            P(("groups", "tm")),
            P(("groups", "tm")),
            P("tm", None),
            P(None, "tensor"),
            P(None, "tensor"),
            P("tensor", None),
            P("tm", None),
        ),
        out_specs=P(("groups", "tm"), "tensor", None),
        check_vma=False,
    )
```

```python
import functools
import math

import jax
import jax.numpy as jnp
from jax import lax
from jax.experimental import pallas as pl
from jax.experimental.pallas import tpu as pltpu
from jax.sharding import PartitionSpec as P


HD = 128
LANES = 128
ITERS = 2
NORM_EPS = 1e-06
STEP_DIVISOR = 64.0
F32 = jnp.float32
BF16 = jnp.bfloat16
VMEM = pl.BlockSpec(memory_space=pltpu.VMEM)
SMEM = pl.BlockSpec(memory_space=pltpu.SMEM)
HBM = pl.BlockSpec(memory_space=pltpu.HBM)


def embedding_of(time_index, width):
    half_width = width // 2
    frequency = jnp.exp(
        -math.log(10000.0) * jnp.arange(half_width).astype(F32) / half_width
    )
    angles = time_index.astype(F32)[:, None] * frequency[None, :]
    return jnp.concatenate([jnp.cos(angles), jnp.sin(angles)], axis=1)


def is_small(axis):
    return lax.axis_size(axis) in (2, 4)


def swap(value, axis, k):
    n = lax.axis_size(axis)
    return lax.ppermute(value, axis, [(i, i ^ k) for i in range(n)])


def gather_parts(value, axis):
    if is_small(axis):
        return [value] + [swap(value, axis, k) for k in range(1, lax.axis_size(axis))]
    return [lax.all_gather(value, axis, axis=0, tiled=True)]


def gather_weight_parts(value, axis):
    n = lax.axis_size(axis)
    if n != 4:
        return gather_parts(value, axis)
    far = swap(value, axis, 2)
    near = swap(value, axis, 1)
    return [value, near, far, swap(far, axis, 1)]


def place(axis, parts, k):
    if parts == 1:
        return 0
    return lax.axis_index(axis) ^ k


def bdot(a, b):
    return jnp.dot(a, b, preferred_element_type=F32)


def bdot_t(a, b):
    return lax.dot_general(a, b, (((1,), (1,)), ((), ())), preferred_element_type=F32)


def split_terms(value, terms):
    out = []
    for _ in range(terms):
        piece = value.astype(BF16)
        out.append(piece)
        value = value - piece.astype(F32)
    return out


def run_copies(copies):
    for copy in copies:
        copy.start()
    return copies


def wait_copies(copies):
    for copy in copies:
        copy.wait()


def modulation_kernel(time_ref, weight_hbm, start_hbm, out_ref, weight_ref, start_ref, sems):
    rows = start_ref.shape[0]
    half = weight_ref.shape[0] // 2
    copies = run_copies(
        [
            pltpu.make_async_copy(weight_hbm, weight_ref, sems.at[0]),
            pltpu.make_async_copy(start_hbm, start_ref, sems.at[1]),
        ]
    )
    index = lax.broadcasted_iota(jnp.int32, (16, half), 1).astype(F32)
    angles = time_ref[0].astype(F32) * jnp.exp(-math.log(10000.0) * index / half)
    embedding = jnp.concatenate([jnp.cos(angles), jnp.sin(angles)], axis=1).astype(BF16)
    wait_copies(copies)
    result = bdot(embedding, weight_ref[...])
    out_ref[0:rows, :] = start_ref[...]
    for r in range(weight_ref.shape[1] // LANES):
        out_ref[rows + r : rows + r + 1, :] = result[0:1, r * LANES : (r + 1) * LANES]


def attend(x, factors, base, gram, head_count):
    twice = jnp.concatenate([x, x], axis=1)
    thrice = jnp.concatenate([twice, x], axis=1)
    heads = [slice(h * 3 * HD, (h + 1) * 3 * HD) for h in range(head_count)]
    quadratic = bdot(thrice, gram[...])
    raw = [bdot(twice, factors[:, cols]) for cols in heads]
    spread = jnp.sum(quadratic * x.astype(F32), axis=1, keepdims=True)
    scale = lax.rsqrt(jnp.maximum(spread, 0.0) + NORM_EPS)
    qkv = [(r * scale + base[0:1, cols]).astype(BF16) for r, cols in zip(raw, heads)]
    scores = [bdot_t(p[:, :HD], p[:, HD : 2 * HD]) * (1.0 / math.sqrt(HD)) for p in qkv]
    tops = [jnp.max(s, axis=1, keepdims=True) for s in scores]
    weights = [jnp.exp(s - t) for s, t in zip(scores, tops)]
    sums = [jnp.sum(w, axis=1, keepdims=True) for w in weights]
    probs = [(w / n).astype(BF16) for w, n in zip(weights, sums)]
    outs = [bdot(w, p[:, 2 * HD :]).astype(BF16) for w, p in zip(probs, qkv)]
    return outs[0] if head_count == 1 else jnp.concatenate(outs, axis=1)


def setup_kernel(nt, nm, head_count, *refs):
    msgs, refs = refs[:nt], refs[nt:]
    inws, refs = refs[:nm], refs[nm:]
    qkv_hbm, out_w_hbm, refs = refs[0], refs[1], refs[2:]
    factor_ref, base_ref, gram_ref, start_ref, inw_ref, gate_ref, out_w_ref = refs[:7]
    start_s, mod_s, inw_s, z_s, qkv_s, sems = refs[7:]
    block = 3 * HD
    own = run_copies(
        [
            pltpu.make_async_copy(
                inws[0], inw_s.at[place("tm", nm, 0)], sems.at[head_count + 1]
            )
        ]
    )
    copies = run_copies(
        [
            pltpu.make_async_copy(
                qkv_hbm.at[:, pl.ds(h * block, block)],
                qkv_s.at[:, pl.ds(h * block, block)],
                sems.at[h],
            )
            for h in range(head_count)
        ]
        + [pltpu.make_async_copy(out_w_hbm, out_w_ref, sems.at[head_count])]
    )
    wait_copies(own)
    for k, msg in enumerate(msgs):
        at = place("tensor", nt, k)
        start_s[at] = msg[0 : start_s.shape[1], :]
        mod_s[at, 0 : msg.shape[0] - start_s.shape[1], :] = msg[start_s.shape[1] :, :]
    for k in range(1, nm):
        inw_s[place("tm", nm, k)] = inws[k][...]
    channels, width = inw_ref.shape
    chunks = width // LANES
    per = 3 * chunks // nt

    def mod_row(r):
        return mod_s[r // per, r % per : r % per + 1, :]

    inw = inw_s[...].reshape(channels, width)
    inw_ref[...] = inw
    total = jnp.zeros((channels, LANES), F32)
    for c in range(chunks):
        total = total + inw[:, c * LANES : (c + 1) * LANES].astype(F32)
    mean = jnp.sum(total, axis=1, keepdims=True) * (1.0 / width)
    for c in range(chunks):
        cols = slice(c * LANES, (c + 1) * LANES)
        centered = inw[:, cols].astype(F32) - mean
        z_s[0:channels, cols] = (centered * (1.0 + mod_row(chunks + c))).astype(BF16)
        z_s[channels : channels + 16, cols] = jnp.broadcast_to(mod_row(c), (16, LANES)).astype(BF16)
        gate_ref[c : c + 1, :] = mod_row(2 * chunks + c)
    mean_b = jnp.broadcast_to(mean, (channels, channels))
    gram = bdot_t(inw, inw) * (1.0 / width) - mean_b * mean_b.T
    for i, piece in enumerate(split_terms(gram, 3)):
        gram_ref[i * channels : (i + 1) * channels, :] = piece
    start = start_s[...].reshape(start_ref.shape)
    start_ref[...] = start

    for h in range(head_count):
        at = slice(h * block, (h + 1) * block)
        copies[h].wait()
        result = bdot(z_s[...], qkv_s[:, at])
        high, low = split_terms(result[0:channels], 2)
        factor_ref[0:channels, at] = high
        factor_ref[channels : 2 * channels, at] = low
        base_ref[:, at] = result[channels : channels + 8]
    copies[head_count].wait()


def attend_kernel(head_count, *refs):
    start_ref, factor_ref, base_ref, gram_ref, out_w_ref, gate_ref, att_ref, scaled_ref = refs
    x = start_ref[...].astype(BF16)
    att_ref[...] = attend(x, factor_ref, base_ref, gram_ref, head_count)
    for c in range(out_w_ref.shape[1] // LANES):
        cols = slice(c * LANES, (c + 1) * LANES)
        scaled_ref[:, cols] = (out_w_ref[:, cols].astype(F32) * gate_ref[c : c + 1, :]).astype(BF16)


def add_own_rows(result, residual, rows):
    first = lax.axis_index("tensor") * rows
    at = lax.broadcasted_iota(jnp.int32, result.shape, 0)
    return result + jnp.where((at >= first) & (at < first + rows), residual, 0.0)


def step_size(step_ref):
    return step_ref[0].astype(F32) * (1.0 / STEP_DIVISOR)


def fold_kernel(nm, rows, *refs):
    heads, refs = refs[:nm], refs[nm:]
    step_ref, scaled_ref, inw_ref, att_ref, start_ref = refs[:5]
    fold_ref, resid_ref, vel_ref, head_s = refs[5:]
    for k in range(nm):
        head_s[place("tm", nm, k)] = heads[k][...]
    _, width = scaled_ref.shape
    channels = inw_ref.shape[0]
    head = head_s[...].reshape(width, head_s.shape[2])
    resid = bdot(inw_ref[...], head)
    folded = bdot(scaled_ref[...], head).astype(BF16)
    fold_ref[...] = folded
    for i, term in enumerate(split_terms(resid, 2)):
        resid_ref[i * channels : (i + 1) * channels, :] = term
    x = start_ref[...].astype(BF16)
    vel = bdot(att_ref[...], folded)
    residual = bdot(jnp.concatenate([x, x], axis=1), resid_ref[...])
    vel_ref[...] = (add_own_rows(vel, residual, rows) * step_size(step_ref)).astype(vel_ref.dtype)


def iterate_kernel(nparts, rows, head_count, split, *refs):
    parts, refs = refs[:nparts], refs[nparts:]
    step_ref, start_ref, factor_ref, base_ref, gram_ref, fold_ref, resid_ref = refs[:7]
    outs = refs[7:-1]
    vel_s = refs[-1]
    guess = start_ref[...]
    for part in parts:
        guess = guess + part[...].astype(F32)
    x = guess.astype(BF16)
    attended = attend(x, factor_ref, base_ref, gram_ref, head_count)
    vel = bdot(attended, fold_ref[...])
    residual = bdot(jnp.concatenate([x, x], axis=1), resid_ref[...])
    vel = add_own_rows(vel, residual, rows) * step_size(step_ref)
    if not split:
        outs[0][...] = vel.astype(outs[0].dtype)
        return
    vel_s[...] = vel.reshape(vel_s.shape)
    for k in range(len(outs)):
        outs[k][...] = vel_s[lax.axis_index("tensor") ^ k]


def shape_of(shape, dtype):
    return jax.ShapeDtypeStruct(shape, dtype)


def call(kernel, outs, in_specs, scratch, *args, cost=4 * 2**20, limit=8):
    args = [
        pltpu.with_memory_space_constraint(arg, pltpu.HBM) if spec is HBM else arg
        for arg, spec in zip(args, in_specs)
    ]
    return pl.pallas_call(
        kernel,
        out_shape=outs,
        in_specs=in_specs,
        out_specs=[VMEM] * len(outs),
        scratch_shapes=scratch,
        compiler_params=pltpu.CompilerParams(vmem_limit_bytes=limit * 2**20),
        cost_estimate=pl.CostEstimate(flops=0, bytes_accessed=cost, transcendentals=0),
    )(*args)


def sum_earlier(parts, inclusive):
    me = lax.axis_index("tm")
    total = parts[0].astype(F32) if inclusive else jnp.zeros(parts[0].shape, F32)
    for k in range(1, len(parts)):
        total = total + jnp.where((me ^ k) < me, parts[k].astype(F32), 0.0)
    return total


def earlier_sum(value, inclusive):
    if is_small("tm"):
        return sum_earlier(gather_parts(value, "tm"), inclusive)
    everything = lax.all_gather(value, "tm").astype(F32)
    index = jnp.arange(everything.shape[0]).reshape((-1,) + (1,) * value.ndim)
    me = lax.axis_index("tm")
    keep = index <= me if inclusive else index < me
    return jnp.sum(jnp.where(keep, everything, 0.0), axis=0)


def local(
    start_latent,
    time_index,
    step_weight,
    in_weight,
    mod_weight,
    qkv_weight,
    out_weight,
    head_weight,
):
    rows, channels = start_latent.shape
    n_tensor = lax.axis_size("tensor")
    tokens = rows * n_tensor
    width = in_weight.shape[1]
    chunks = width // LANES
    head_count = qkv_weight.shape[1] // (3 * HD)
    span = out_weight.shape[0]

    inw_parts = gather_weight_parts(in_weight, "tm")
    small = is_small("tensor") and mod_weight.shape[1] % LANES == 0
    if small:
        mod_rows = mod_weight.shape[1] // LANES
        message = call(
            modulation_kernel,
            [shape_of((rows + mod_rows, LANES), F32)],
            [SMEM, HBM, HBM],
            [
                pltpu.VMEM(mod_weight.shape, BF16),
                pltpu.VMEM(start_latent.shape, F32),
                pltpu.SemaphoreType.DMA((2,)),
            ],
            time_index,
            mod_weight,
            start_latent,
            limit=8,
        )[0]
        messages = gather_parts(message, "tensor")
        block_rows = rows
    else:
        embedding = embedding_of(time_index, mod_weight.shape[0]).astype(BF16)
        mod_part = jnp.dot(embedding, mod_weight, preferred_element_type=F32)
        modulation = lax.all_gather(mod_part, "tensor", axis=1, tiled=True)
        start_all = lax.all_gather(start_latent, "tensor", axis=0, tiled=True)
        messages = [jnp.concatenate([start_all, modulation.reshape(-1, LANES)], axis=0)]
        block_rows = tokens
    nt, nm = len(messages), len(inw_parts)
    mod_rows = messages[0].shape[0] - block_rows
    padded = -(-mod_rows // 8) * 8
    factor, base, gram, start_all, inw_all, gate, out_near = call(
        functools.partial(setup_kernel, nt, nm, head_count),
        [
            shape_of((2 * channels, qkv_weight.shape[1]), BF16),
            shape_of((8, qkv_weight.shape[1]), F32),
            shape_of((3 * channels, channels), BF16),
            shape_of((tokens, channels), F32),
            shape_of((channels, width), BF16),
            shape_of((chunks, LANES), F32),
            shape_of(out_weight.shape, BF16),
        ],
        [VMEM] * nt + [HBM] + [VMEM] * (nm - 1) + [HBM, HBM],
        [
            pltpu.VMEM((nt, block_rows, channels), F32),
            pltpu.VMEM((nt, padded, LANES), F32),
            pltpu.VMEM((nm, channels // nm, width), BF16),
            pltpu.VMEM((channels + 16, width), BF16),
            pltpu.VMEM(qkv_weight.shape, BF16),
            pltpu.SemaphoreType.DMA((head_count + 2,)),
        ],
        *messages,
        *inw_parts,
        qkv_weight,
        out_weight,
        limit=32,
    )
    attended, scaled = call(
        functools.partial(attend_kernel, head_count),
        [shape_of((tokens, head_count * HD), BF16), shape_of(out_weight.shape, BF16)],
        [VMEM] * 6,
        [],
        start_all,
        factor,
        base,
        gram,
        out_near,
        gate,
        limit=16,
    )
    head_parts = gather_weight_parts(head_weight, "tm")
    folded, resid, vel = call(
        functools.partial(fold_kernel, nm, rows),
        [
            shape_of((span, channels), BF16),
            shape_of((2 * channels, channels), BF16),
            shape_of((tokens, channels), BF16),
        ],
        [VMEM] * nm + [SMEM] + [VMEM] * 4,
        [pltpu.VMEM((nm, width // nm, channels), BF16)],
        *head_parts,
        step_weight,
        scaled,
        inw_all,
        attended,
        start_all,
        limit=24,
    )
    small = is_small("tensor")
    for iteration in range(1, ITERS):
        last = iteration + 1 == ITERS
        earlier = earlier_sum(vel, False)
        if small:
            pieces = gather_parts(earlier.astype(BF16), "tensor")
        else:
            pieces = [lax.psum(earlier, "tensor")]
        split = last and small
        if split:
            outs = [shape_of((rows, channels), F32)] * n_tensor
        else:
            outs = [shape_of((tokens, channels), F32 if last else BF16)]
        vels = call(
            functools.partial(iterate_kernel, len(pieces), rows, head_count, split),
            outs,
            [VMEM] * len(pieces) + [SMEM] + [VMEM] * 6,
            [pltpu.VMEM((n_tensor, rows, channels), F32)],
            *pieces,
            step_weight,
            start_all,
            factor,
            base,
            gram,
            folded,
            resid,
        )
        vel = vels[0]
    if small:
        drift = vels[0]
        for k in range(1, n_tensor):
            drift = drift + swap(vels[k], "tensor", k)
    else:
        drift = lax.psum_scatter(vel, "tensor", scatter_dimension=0, tiled=True)
    return (start_latent + earlier_sum(drift, True))[None]


def solution(mesh):
    return jax.shard_map(
        local,
        mesh=mesh,
        in_specs=(
            P(("groups", "tensor"), None),
            P(("groups", "tm")),
            P(("groups", "tm")),
            P("tm", None),
            P(None, "tensor"),
            P(None, "tensor"),
            P("tensor", None),
            P("tm", None),
        ),
        out_specs=P(("groups", "tm"), "tensor", None),
        check_vma=False,
    )
```

```python
import functools
import math

import jax
import jax.numpy as jnp
from jax import lax
from jax.experimental import pallas as pl
from jax.experimental.pallas import tpu as pltpu
from jax.sharding import PartitionSpec as P


HD = 128
LANES = 128
ITERS = 2
NORM_EPS = 1e-06
STEP_DIVISOR = 64.0
F32 = jnp.float32
BF16 = jnp.bfloat16
VMEM = pl.BlockSpec(memory_space=pltpu.VMEM)
HBM = pl.BlockSpec(memory_space=pltpu.HBM)


def embedding_of(time_index, width):
    half_width = width // 2
    frequency = jnp.exp(
        -math.log(10000.0) * jnp.arange(half_width).astype(F32) / half_width
    )
    angles = time_index.astype(F32)[:, None] * frequency[None, :]
    return jnp.concatenate([jnp.cos(angles), jnp.sin(angles)], axis=1)


def is_small(axis):
    return lax.axis_size(axis) in (2, 4)


def swap(value, axis, k):
    n = lax.axis_size(axis)
    return lax.ppermute(value, axis, [(i, i ^ k) for i in range(n)])


def gather_parts(value, axis):
    if is_small(axis):
        return [value] + [swap(value, axis, k) for k in range(1, lax.axis_size(axis))]
    return [lax.all_gather(value, axis, axis=0, tiled=True)]


def gather_weight_parts(value, axis):
    n = lax.axis_size(axis)
    if n != 4:
        return gather_parts(value, axis)
    far = swap(value, axis, 2)
    near = swap(value, axis, 1)
    return [value, near, far, swap(far, axis, 1)]


def place(axis, parts, k):
    if parts == 1:
        return 0
    return lax.axis_index(axis) ^ k


def bdot(a, b):
    return jnp.dot(a, b, preferred_element_type=F32)


def bdot_t(a, b):
    return lax.dot_general(a, b, (((1,), (1,)), ((), ())), preferred_element_type=F32)


def split_terms(value, terms):
    out = []
    for _ in range(terms):
        piece = value.astype(BF16)
        out.append(piece)
        value = value - piece.astype(F32)
    return out


def run_copies(copies):
    for copy in copies:
        copy.start()
    return copies


def wait_copies(copies):
    for copy in copies:
        copy.wait()


def modulation_kernel(
    time_ref, weight_step_ref, weight_hbm, start_hbm, out_ref, step_ref, weight_ref, start_ref, sems
):
    rows = start_ref.shape[0]
    half = weight_ref.shape[0] // 2
    pairs = ((weight_hbm, weight_ref), (start_hbm, start_ref))
    copies = run_copies(
        [pltpu.make_async_copy(a, b, sems.at[i]) for i, (a, b) in enumerate(pairs)]
    )
    index = lax.broadcasted_iota(jnp.int32, (16, half), 1).astype(F32)
    frequency = jnp.exp(-math.log(10000.0) * index / half)
    time = jnp.broadcast_to(time_ref[...].astype(F32), frequency.shape)
    angles = time * frequency
    embedding = jnp.concatenate([jnp.cos(angles), jnp.sin(angles)], axis=1).astype(BF16)
    step = weight_step_ref[...].astype(F32) * (1.0 / STEP_DIVISOR)
    step_ref[...] = jnp.broadcast_to(step, step_ref.shape)
    wait_copies(copies)
    result = bdot(embedding, weight_ref[...])
    out_ref[0:rows, :] = start_ref[...]
    for r in range(weight_ref.shape[1] // LANES):
        out_ref[rows + r : rows + r + 1, :] = result[0:1, r * LANES : (r + 1) * LANES]


def load_kernel(qkv_hbm, inw_hbm, qkv_ref, inw_ref, sems):
    cols = qkv_ref.shape[1]
    wait_copies(
        run_copies(
            [
                pltpu.make_async_copy(inw_hbm, inw_ref, sems.at[0]),
                pltpu.make_async_copy(qkv_hbm.at[:, pl.ds(0, cols)], qkv_ref, sems.at[1]),
            ]
        )
    )


def attend(x, factors, base, gram, head_count):
    twice = jnp.concatenate([x, x], axis=1)
    thrice = jnp.concatenate([twice, x], axis=1)
    heads = [slice(h * 3 * HD, (h + 1) * 3 * HD) for h in range(head_count)]
    quadratic = bdot(thrice, gram[...])
    raw = [bdot(twice, factors[:, cols]) for cols in heads]
    spread = jnp.sum(quadratic * x.astype(F32), axis=1, keepdims=True)
    scale = lax.rsqrt(jnp.maximum(spread, 0.0) + NORM_EPS)
    qkv = [(r * scale + base[0:1, cols]).astype(BF16) for r, cols in zip(raw, heads)]
    scores = [bdot_t(p[:, :HD], p[:, HD : 2 * HD]) * (1.0 / math.sqrt(HD)) for p in qkv]
    tops = [jnp.max(s, axis=1, keepdims=True) for s in scores]
    weights = [jnp.exp(s - t) for s, t in zip(scores, tops)]
    sums = [jnp.sum(w, axis=1, keepdims=True) for w in weights]
    probs = [(w / n).astype(BF16) for w, n in zip(weights, sums)]
    outs = [bdot(w, p[:, 2 * HD :]).astype(BF16) for w, p in zip(probs, qkv)]
    return outs[0] if head_count == 1 else jnp.concatenate(outs, axis=1)


def setup_kernel(nt, nm, head_count, *refs):
    msgs, refs = refs[:nt], refs[nt:]
    inws, refs = refs[:nm], refs[nm:]
    near_ref, qkv_hbm, out_w_hbm, refs = refs[0], refs[1], refs[2], refs[3:]
    factor_ref, base_ref, gram_ref, start_ref, inw_ref, scaled_ref = refs[:6]
    start_s, mod_s, inw_s, z_s, qkv_s, out_w_s, sems = refs[6:]
    block = 3 * HD
    near = near_ref.shape[1] // block
    copies = run_copies(
        [pltpu.make_async_copy(out_w_hbm, out_w_s, sems.at[0])]
        + [
            pltpu.make_async_copy(
                qkv_hbm.at[:, pl.ds(h * block, block)],
                qkv_s.at[:, pl.ds((h - near) * block, block)],
                sems.at[1 + h - near],
            )
            for h in range(near, head_count)
        ]
    )
    for k, msg in enumerate(msgs):
        at = place("tensor", nt, k)
        start_s[at] = msg[0 : start_s.shape[1], :]
        mod_s[at, 0 : msg.shape[0] - start_s.shape[1], :] = msg[start_s.shape[1] :, :]
    for k in range(nm):
        inw_s[place("tm", nm, k)] = inws[k][...]
    channels, width = inw_ref.shape[1], z_s.shape[1]
    chunks = width // LANES
    per_part = chunks // nm
    per = 3 * chunks // nt

    def mod_row(r):
        return mod_s[r // per, r % per : r % per + 1, :]

    inw = inw_s[...].reshape(channels, width)
    total = jnp.zeros((channels, LANES), F32)
    for c in range(chunks):
        total = total + inw[:, c * LANES : (c + 1) * LANES].astype(F32)
    mean = jnp.sum(total, axis=1, keepdims=True) * (1.0 / width)
    for c in range(chunks):
        cols = slice(c * LANES, (c + 1) * LANES)
        centered = inw[:, cols].astype(F32) - mean
        z_s[0:channels, cols] = (centered * (1.0 + mod_row(chunks + c))).astype(BF16)
        z_s[channels : channels + 16, cols] = jnp.broadcast_to(mod_row(c), (16, LANES)).astype(BF16)
        at = slice(c % per_part * LANES, (c % per_part + 1) * LANES)
        inw_ref[c // per_part, :, at] = inw[:, cols]
    mean_b = jnp.broadcast_to(mean, (channels, channels))
    gram = bdot_t(inw, inw) * (1.0 / width) - mean_b * mean_b.T
    for i, piece in enumerate(split_terms(gram, 3)):
        gram_ref[i * channels : (i + 1) * channels, :] = piece
    start = start_s[...].reshape(start_ref.shape)
    start_ref[...] = start

    def scale_chunks(first, last):
        for c in range(first, last):
            at = slice(c % per_part * LANES, (c % per_part + 1) * LANES)
            scaled = out_w_s[:, c * LANES : (c + 1) * LANES].astype(F32) * mod_row(2 * chunks + c)
            scaled_ref[c // per_part, :, at] = scaled.astype(BF16)

    def project(h, weight):
        at = slice(h * block, (h + 1) * block)
        result = bdot(z_s[...], weight)
        high, low = split_terms(result[0:channels], 2)
        factor_ref[0:channels, at] = high
        factor_ref[channels : 2 * channels, at] = low
        base_ref[:, at] = result[channels : channels + 8]

    for h in range(near):
        project(h, near_ref[:, h * block : (h + 1) * block])
    copies[0].wait()
    far = head_count - near
    for h in range(far):
        copies[1 + h].wait()
        project(near + h, qkv_s[:, h * block : (h + 1) * block])
        scale_chunks(h * chunks // far, (h + 1) * chunks // far)
    if far == 0:
        scale_chunks(0, chunks)


def attend_kernel(nm, early, head_count, *refs):
    heads, refs = refs[:early], refs[early:]
    start_ref, factor_ref, base_ref, gram_ref, scaled_ref, inw_ref = refs[:6]
    att_ref, fold_ref, resid_ref = refs[6:]
    x = start_ref[...].astype(BF16)
    folded = jnp.zeros(fold_ref.shape, F32)
    resid = jnp.zeros(resid_ref.shape, F32)
    for k in range(early):
        at = place("tm", nm, k)
        folded = folded + bdot(scaled_ref[at], heads[k][...])
        resid = resid + bdot(inw_ref[at], heads[k][...])
    fold_ref[...] = folded
    resid_ref[...] = resid
    att_ref[...] = attend(x, factor_ref, base_ref, gram_ref, head_count)


def add_own_rows(result, residual, rows):
    first = lax.axis_index("tensor") * rows
    at = lax.broadcasted_iota(jnp.int32, result.shape, 0)
    return result + jnp.where((at >= first) & (at < first + rows), residual, 0.0)


def fold_kernel(nm, late, rows, *refs):
    heads, refs = refs[:late], refs[late:]
    step_ref, scaled_ref, inw_ref, fold_in, resid_in, att_ref, start_ref = refs[:7]
    fold_ref, resid_ref, vel_ref = refs[7:]
    channels = inw_ref.shape[1]
    total, resid = fold_in[...], resid_in[...]
    for k in range(late):
        at = place("tm", nm, nm - late + k)
        total = total + bdot(scaled_ref[at], heads[k][...])
        resid = resid + bdot(inw_ref[at], heads[k][...])
    folded = total.astype(BF16)
    fold_ref[...] = folded
    for i, term in enumerate(split_terms(resid, 2)):
        resid_ref[i * channels : (i + 1) * channels, :] = term
    x = start_ref[...].astype(BF16)
    vel = bdot(att_ref[...], folded)
    residual = bdot(jnp.concatenate([x, x], axis=1), resid_ref[...])
    vel_ref[...] = (add_own_rows(vel, residual, rows) * step_ref[0:1, :]).astype(vel_ref.dtype)


def iterate_kernel(nparts, rows, head_count, split, *refs):
    parts, refs = refs[:nparts], refs[nparts:]
    step_ref, start_ref, factor_ref, base_ref, gram_ref, fold_ref, resid_ref = refs[:7]
    outs = refs[7:-1]
    vel_s = refs[-1]
    guess = start_ref[...]
    for part in parts:
        guess = guess + part[...].astype(F32)
    x = guess.astype(BF16)
    attended = attend(x, factor_ref, base_ref, gram_ref, head_count)
    vel = bdot(attended, fold_ref[...])
    residual = bdot(jnp.concatenate([x, x], axis=1), resid_ref[...])
    vel = add_own_rows(vel, residual, rows) * step_ref[0:1, :]
    if not split:
        outs[0][...] = vel.astype(outs[0].dtype)
        return
    vel_s[...] = vel.reshape(vel_s.shape)
    for k in range(len(outs)):
        outs[k][...] = vel_s[lax.axis_index("tensor") ^ k]


def shape_of(shape, dtype):
    return jax.ShapeDtypeStruct(shape, dtype)


def call(kernel, outs, in_specs, scratch, *args, cost=4 * 2**20, limit=8):
    args = [
        pltpu.with_memory_space_constraint(arg, pltpu.HBM) if spec is HBM else arg
        for arg, spec in zip(args, in_specs)
    ]
    return pl.pallas_call(
        kernel,
        out_shape=outs,
        in_specs=in_specs,
        out_specs=[VMEM] * len(outs),
        scratch_shapes=scratch,
        compiler_params=pltpu.CompilerParams(vmem_limit_bytes=limit * 2**20),
        cost_estimate=pl.CostEstimate(flops=0, bytes_accessed=cost, transcendentals=0),
    )(*args)


def sum_earlier(parts, inclusive):
    me = lax.axis_index("tm")
    total = parts[0].astype(F32) if inclusive else jnp.zeros(parts[0].shape, F32)
    for k in range(1, len(parts)):
        total = total + jnp.where((me ^ k) < me, parts[k].astype(F32), 0.0)
    return total


def earlier_sum(value, inclusive):
    if is_small("tm"):
        return sum_earlier(gather_parts(value, "tm"), inclusive)
    everything = lax.all_gather(value, "tm").astype(F32)
    index = jnp.arange(everything.shape[0]).reshape((-1,) + (1,) * value.ndim)
    me = lax.axis_index("tm")
    keep = index <= me if inclusive else index < me
    return jnp.sum(jnp.where(keep, everything, 0.0), axis=0)


def local(
    start_latent,
    time_index,
    step_weight,
    in_weight,
    mod_weight,
    qkv_weight,
    out_weight,
    head_weight,
):
    rows, channels = start_latent.shape
    n_tensor = lax.axis_size("tensor")
    tokens = rows * n_tensor
    width = in_weight.shape[1]
    head_count = qkv_weight.shape[1] // (3 * HD)
    span = out_weight.shape[0]

    inw_parts = gather_weight_parts(in_weight, "tm")
    small = is_small("tensor") and mod_weight.shape[1] % LANES == 0
    if small:
        mod_rows = mod_weight.shape[1] // LANES
        message, step = call(
            modulation_kernel,
            [shape_of((rows + mod_rows, LANES), F32), shape_of((8, LANES), F32)],
            [VMEM, VMEM, HBM, HBM],
            [
                pltpu.VMEM(mod_weight.shape, BF16),
                pltpu.VMEM(start_latent.shape, F32),
                pltpu.SemaphoreType.DMA((2,)),
            ],
            time_index.reshape(1, 1),
            step_weight.reshape(1, 1),
            mod_weight,
            start_latent,
        )
        messages = gather_parts(message, "tensor")
        block_rows = rows
    else:
        step = jnp.full((8, LANES), step_weight[0].astype(F32) / STEP_DIVISOR)
        embedding = embedding_of(time_index, mod_weight.shape[0]).astype(BF16)
        mod_part = jnp.dot(embedding, mod_weight, preferred_element_type=F32)
        modulation = lax.all_gather(mod_part, "tensor", axis=1, tiled=True)
        start_all = lax.all_gather(start_latent, "tensor", axis=0, tiled=True)
        messages = [jnp.concatenate([start_all, modulation.reshape(-1, LANES)], axis=0)]
        block_rows = tokens
    nt, nm = len(messages), len(inw_parts)
    mod_rows = messages[0].shape[0] - block_rows
    padded = -(-mod_rows // 8) * 8
    near = max(1, head_count // 2)
    far = max(1, head_count - near)
    qkv_near, inw_parts[0] = call(
        load_kernel,
        [shape_of((width, near * 3 * HD), BF16), shape_of(inw_parts[0].shape, BF16)],
        [HBM, HBM],
        [pltpu.SemaphoreType.DMA((2,))],
        qkv_weight,
        inw_parts[0],
    )
    scaled_shape = (nm, span, width // nm)
    factor, base, gram, start_all, inw_all, scaled = call(
        functools.partial(setup_kernel, nt, nm, head_count),
        [
            shape_of((2 * channels, qkv_weight.shape[1]), BF16),
            shape_of((8, qkv_weight.shape[1]), F32),
            shape_of((3 * channels, channels), BF16),
            shape_of((tokens, channels), F32),
            shape_of((nm, channels, width // nm), BF16),
            shape_of(scaled_shape, BF16),
        ],
        [VMEM] * (nt + nm + 1) + [HBM, HBM],
        [
            pltpu.VMEM((nt, block_rows, channels), F32),
            pltpu.VMEM((nt, padded, LANES), F32),
            pltpu.VMEM((nm, channels // nm, width), BF16),
            pltpu.VMEM((channels + 16, width), BF16),
            pltpu.VMEM((width, far * 3 * HD), BF16),
            pltpu.VMEM(out_weight.shape, BF16),
            pltpu.SemaphoreType.DMA((far + 1,)),
        ],
        *messages,
        *inw_parts,
        qkv_near,
        qkv_weight,
        out_weight,
        limit=32,
    )
    head_parts = gather_weight_parts(head_weight, "tm")
    late = 1 if nm > 1 else 0
    early = nm - late
    attended, fold_part, resid_part = call(
        functools.partial(attend_kernel, nm, early, head_count),
        [
            shape_of((tokens, head_count * HD), BF16),
            shape_of((span, channels), F32),
            shape_of((channels, channels), F32),
        ],
        [VMEM] * (early + 6),
        [],
        *head_parts[:early],
        start_all,
        factor,
        base,
        gram,
        scaled,
        inw_all,
        limit=16,
    )
    folded, resid, vel = call(
        functools.partial(fold_kernel, nm, late, rows),
        [
            shape_of((span, channels), BF16),
            shape_of((2 * channels, channels), BF16),
            shape_of((tokens, channels), BF16),
        ],
        [VMEM] * (late + 7),
        [],
        *head_parts[early:],
        step,
        scaled,
        inw_all,
        fold_part,
        resid_part,
        attended,
        start_all,
        limit=16,
    )
    small = is_small("tensor")
    for iteration in range(1, ITERS):
        last = iteration + 1 == ITERS
        earlier = earlier_sum(vel, False)
        if small:
            pieces = gather_parts(earlier.astype(BF16), "tensor")
        else:
            pieces = [lax.psum(earlier, "tensor")]
        split = last and small
        if split:
            outs = [shape_of((rows, channels), F32)] * n_tensor
        else:
            outs = [shape_of((tokens, channels), F32 if last else BF16)]
        vels = call(
            functools.partial(iterate_kernel, len(pieces), rows, head_count, split),
            outs,
            [VMEM] * (len(pieces) + 7),
            [pltpu.VMEM((n_tensor, rows, channels), F32)],
            *pieces,
            step,
            start_all,
            factor,
            base,
            gram,
            folded,
            resid,
        )
        vel = vels[0]
    if small:
        drift = vels[0]
        for k in range(1, n_tensor):
            drift = drift + swap(vels[k], "tensor", k)
    else:
        drift = lax.psum_scatter(vel, "tensor", scatter_dimension=0, tiled=True)
    return (start_latent + earlier_sum(drift, True))[None]


def solution(mesh):
    return jax.shard_map(
        local,
        mesh=mesh,
        in_specs=(
            P(("groups", "tensor"), None),
            P(("groups", "tm")),
            P(("groups", "tm")),
            P("tm", None),
            P(None, "tensor"),
            P(None, "tensor"),
            P("tensor", None),
            P("tm", None),
        ),
        out_specs=P(("groups", "tm"), "tensor", None),
        check_vma=False,
    )
```

```python
import functools
import math

import jax
import jax.numpy as jnp
from jax import lax
from jax.experimental import pallas as pl
from jax.experimental.pallas import tpu as pltpu
from jax.sharding import PartitionSpec as P


HD = 128
LANES = 128
ITERS = 2
NORM_EPS = 1e-06
STEP_DIVISOR = 64.0
F32 = jnp.float32
BF16 = jnp.bfloat16
VMEM = pl.BlockSpec(memory_space=pltpu.VMEM)
HBM = pl.BlockSpec(memory_space=pltpu.HBM)


def embedding_of(time_index, width):
    half_width = width // 2
    frequency = jnp.exp(
        -math.log(10000.0) * jnp.arange(half_width).astype(F32) / half_width
    )
    angles = time_index.astype(F32)[:, None] * frequency[None, :]
    return jnp.concatenate([jnp.cos(angles), jnp.sin(angles)], axis=1)


def is_small(axis):
    return lax.axis_size(axis) in (2, 4)


def swap(value, axis, k):
    n = lax.axis_size(axis)
    return lax.ppermute(value, axis, [(i, i ^ k) for i in range(n)])


def gather_parts(value, axis):
    if is_small(axis):
        return [value] + [swap(value, axis, k) for k in range(1, lax.axis_size(axis))]
    return [lax.all_gather(value, axis, axis=0, tiled=True)]


def gather_weight_parts(value, axis):
    n = lax.axis_size(axis)
    if n != 4:
        return gather_parts(value, axis)
    far = swap(value, axis, 2)
    near = swap(value, axis, 1)
    return [value, near, far, swap(far, axis, 1)]


def place(axis, parts, k):
    if parts == 1:
        return 0
    return lax.axis_index(axis) ^ k


def bdot(a, b):
    return jnp.dot(a, b, preferred_element_type=F32)


def bdot_t(a, b):
    return lax.dot_general(a, b, (((1,), (1,)), ((), ())), preferred_element_type=F32)


def split_terms(value, terms):
    out = []
    for _ in range(terms):
        piece = value.astype(BF16)
        out.append(piece)
        value = value - piece.astype(F32)
    return out


def run_copies(copies):
    for copy in copies:
        copy.start()
    return copies


def wait_copies(copies):
    for copy in copies:
        copy.wait()


def modulation_kernel(
    time_ref, weight_step_ref, weight_hbm, start_hbm, out_ref, step_ref, weight_ref, start_ref, sems
):
    rows = start_ref.shape[0]
    half = weight_ref.shape[0] // 2
    pairs = ((weight_hbm, weight_ref), (start_hbm, start_ref))
    copies = run_copies(
        [pltpu.make_async_copy(a, b, sems.at[i]) for i, (a, b) in enumerate(pairs)]
    )
    index = lax.broadcasted_iota(jnp.int32, (16, half), 1).astype(F32)
    frequency = jnp.exp(-math.log(10000.0) * index / half)
    time = jnp.broadcast_to(time_ref[...].astype(F32), frequency.shape)
    angles = time * frequency
    embedding = jnp.concatenate([jnp.cos(angles), jnp.sin(angles)], axis=1).astype(BF16)
    step = weight_step_ref[...].astype(F32) * (1.0 / STEP_DIVISOR)
    step_ref[...] = jnp.broadcast_to(step, step_ref.shape)
    wait_copies(copies)
    result = bdot(embedding, weight_ref[...])
    out_ref[0:rows, :] = start_ref[...]
    for r in range(weight_ref.shape[1] // LANES):
        out_ref[rows + r : rows + r + 1, :] = result[0:1, r * LANES : (r + 1) * LANES]


def load_kernel(qkv_hbm, inw_hbm, qkv_ref, inw_ref, sems):
    cols = qkv_ref.shape[1]
    wait_copies(
        run_copies(
            [
                pltpu.make_async_copy(inw_hbm, inw_ref, sems.at[0]),
                pltpu.make_async_copy(qkv_hbm.at[:, pl.ds(0, cols)], qkv_ref, sems.at[1]),
            ]
        )
    )


def attend(x, factors, base, gram, head_count):
    twice = jnp.concatenate([x, x], axis=1)
    thrice = jnp.concatenate([twice, x], axis=1)
    heads = [slice(h * 3 * HD, (h + 1) * 3 * HD) for h in range(head_count)]
    quadratic = bdot(thrice, gram[...])
    raw = [bdot(twice, factors[:, cols]) for cols in heads]
    spread = jnp.sum(quadratic * x.astype(F32), axis=1, keepdims=True)
    scale = lax.rsqrt(jnp.maximum(spread, 0.0) + NORM_EPS)
    qkv = [(r * scale + base[0:1, cols]).astype(BF16) for r, cols in zip(raw, heads)]
    scores = [bdot_t(p[:, :HD], p[:, HD : 2 * HD]) * (1.0 / math.sqrt(HD)) for p in qkv]
    tops = [jnp.max(s, axis=1, keepdims=True) for s in scores]
    weights = [jnp.exp(s - t) for s, t in zip(scores, tops)]
    sums = [jnp.sum(w, axis=1, keepdims=True) for w in weights]
    probs = [(w / n).astype(BF16) for w, n in zip(weights, sums)]
    outs = [bdot(w, p[:, 2 * HD :]).astype(BF16) for w, p in zip(probs, qkv)]
    return outs[0] if head_count == 1 else jnp.concatenate(outs, axis=1)


def setup_kernel(nt, nm, block, *refs):
    msgs, refs = refs[:nt], refs[nt:]
    inws, refs = refs[:nm], refs[nm:]
    near_ref, qkv_hbm, out_w_hbm, refs = refs[0], refs[1], refs[2], refs[3:]
    factor_ref, base_ref, gram_ref, start_ref, inw_ref, gate_ref, out_w_ref = refs[:7]
    start_s, mod_s, gate_s, z_s, qkv_s, sems = refs[7:]
    near = near_ref.shape[1] // block
    count = factor_ref.shape[1] // block
    copies = run_copies(
        [
            pltpu.make_async_copy(
                qkv_hbm.at[:, pl.ds(n * block, block)],
                qkv_s.at[:, pl.ds((n - near) * block, block)],
                sems.at[n - near],
            )
            for n in range(near, count)
        ]
        + [pltpu.make_async_copy(out_w_hbm, out_w_ref, sems.at[count - near])]
    )
    for k, msg in enumerate(msgs):
        at = place("tensor", nt, k)
        start_s[at] = msg[0 : start_s.shape[1], :]
        mod_s[at, 0 : msg.shape[0] - start_s.shape[1], :] = msg[start_s.shape[1] :, :]
    for k in range(nm):
        inw_ref[place("tm", nm, k)] = inws[k][...]
    channels, width = gram_ref.shape[1], z_s.shape[1]
    chunks = width // LANES
    per = 3 * chunks // nt

    def mod_row(r):
        return mod_s[r // per, r % per : r % per + 1, :]

    def columns(c, n):
        return inw_ref[:, :, c * LANES : (c + n) * LANES].reshape(channels, n * LANES)

    total = jnp.zeros((channels, LANES), F32)
    for c in range(chunks):
        total = total + columns(c, 1).astype(F32)
    mean = jnp.sum(total, axis=1, keepdims=True) * (1.0 / width)
    for c in range(chunks):
        cols = slice(c * LANES, (c + 1) * LANES)
        centered = columns(c, 1).astype(F32) - mean
        z_s[0:channels, cols] = (centered * (1.0 + mod_row(chunks + c))).astype(BF16)
        z_s[channels : channels + 16, cols] = jnp.broadcast_to(mod_row(c), (16, LANES)).astype(BF16)
        gate_s[c // (chunks // nm), c % (chunks // nm) : c % (chunks // nm) + 1, :] = mod_row(
            2 * chunks + c
        )
    for p in range(nm):
        gate_ref[p] = gate_s[p].T
    gram = jnp.zeros((channels, channels), F32)
    for c in range(0, chunks, 6):
        gram = gram + bdot_t(columns(c, 6), columns(c, 6))
    mean_b = jnp.broadcast_to(mean, (channels, channels))
    gram = gram * (1.0 / width) - mean_b * mean_b.T
    for i, piece in enumerate(split_terms(gram, 3)):
        gram_ref[i * channels : (i + 1) * channels, :] = piece
    start_ref[...] = start_s[...].reshape(start_ref.shape)

    for n in range(count):
        at = slice(n * block, (n + 1) * block)
        if n < near:
            weight = near_ref[:, at]
        else:
            copies[n - near].wait()
            weight = qkv_s[:, (n - near) * block : (n - near + 1) * block]
        result = bdot(z_s[...], weight)
        high, low = split_terms(result[0:channels], 2)
        factor_ref[0:channels, at] = high
        factor_ref[channels : 2 * channels, at] = low
        base_ref[:, at] = result[channels : channels + 8]
    copies[count - near].wait()


def fold_parts(nm, first, heads, gate_ref, out_w_ref, inw_ref):
    folded, resid = 0.0, 0.0
    for i, head_ref in enumerate(heads):
        size, _ = head_ref.shape
        at = place("tm", nm, first + i)
        cols = pl.ds(pl.multiple_of(at * size, LANES), size)
        gate = gate_ref[at]
        gated = []
        for r in range(size // LANES):
            rows = head_ref[r * LANES : (r + 1) * LANES, :].astype(F32)
            gated.append((rows * gate[:, r : r + 1]).astype(BF16))
        folded = folded + bdot(out_w_ref[:, cols], jnp.concatenate(gated, axis=0))
        inw = inw_ref[:, :, cols].reshape(-1, size)
        resid = resid + bdot(inw, head_ref[...])
    return folded, resid


def attend_kernel(nm, early, head_count, *refs):
    heads, refs = refs[:early], refs[early:]
    start_ref, factor_ref, base_ref, gram_ref, gate_ref, out_w_ref, inw_ref = refs[:7]
    att_ref, fold_ref, resid_ref = refs[7:]
    x = start_ref[...].astype(BF16)
    fold_ref[...], resid_ref[...] = fold_parts(nm, 0, heads, gate_ref, out_w_ref, inw_ref)
    att_ref[...] = attend(x, factor_ref, base_ref, gram_ref, head_count)


def add_own_rows(result, residual, rows):
    first = lax.axis_index("tensor") * rows
    at = lax.broadcasted_iota(jnp.int32, result.shape, 0)
    return result + jnp.where((at >= first) & (at < first + rows), residual, 0.0)


def fold_kernel(nm, late, rows, *refs):
    heads, refs = refs[:late], refs[late:]
    step_ref, gate_ref, out_w_ref, inw_ref, fold_in, resid_in, att_ref, start_ref = refs[:8]
    fold_ref, resid_ref, vel_ref = refs[8:]
    channels = resid_in.shape[0]
    total, resid = fold_in[...], resid_in[...]
    if late:
        more = fold_parts(nm, nm - late, heads, gate_ref, out_w_ref, inw_ref)
        total, resid = total + more[0], resid + more[1]
    folded = total.astype(BF16)
    fold_ref[...] = folded
    for i, term in enumerate(split_terms(resid, 2)):
        resid_ref[i * channels : (i + 1) * channels, :] = term
    x = start_ref[...].astype(BF16)
    vel = bdot(att_ref[...], folded)
    residual = bdot(jnp.concatenate([x, x], axis=1), resid_ref[...])
    vel_ref[...] = (add_own_rows(vel, residual, rows) * step_ref[0:1, :]).astype(vel_ref.dtype)


def iterate_kernel(nparts, rows, head_count, split, *refs):
    parts, refs = refs[:nparts], refs[nparts:]
    step_ref, start_ref, factor_ref, base_ref, gram_ref, fold_ref, resid_ref = refs[:7]
    outs = refs[7:-1]
    vel_s = refs[-1]
    guess = start_ref[...]
    for part in parts:
        guess = guess + part[...].astype(F32)
    x = guess.astype(BF16)
    attended = attend(x, factor_ref, base_ref, gram_ref, head_count)
    vel = bdot(attended, fold_ref[...])
    residual = bdot(jnp.concatenate([x, x], axis=1), resid_ref[...])
    vel = add_own_rows(vel, residual, rows) * step_ref[0:1, :]
    if not split:
        outs[0][...] = vel.astype(outs[0].dtype)
        return
    vel_s[...] = vel.reshape(vel_s.shape)
    for k in range(len(outs)):
        outs[k][...] = vel_s[lax.axis_index("tensor") ^ k]


def shape_of(shape, dtype):
    return jax.ShapeDtypeStruct(shape, dtype)


def call(kernel, outs, in_specs, scratch, *args, cost=4 * 2**20, limit=8):
    args = [
        pltpu.with_memory_space_constraint(arg, pltpu.HBM) if spec is HBM else arg
        for arg, spec in zip(args, in_specs)
    ]
    return pl.pallas_call(
        kernel,
        out_shape=outs,
        in_specs=in_specs,
        out_specs=[VMEM] * len(outs),
        scratch_shapes=scratch,
        compiler_params=pltpu.CompilerParams(vmem_limit_bytes=limit * 2**20),
        cost_estimate=pl.CostEstimate(flops=0, bytes_accessed=cost, transcendentals=0),
    )(*args)


def sum_earlier(parts, inclusive):
    me = lax.axis_index("tm")
    total = parts[0].astype(F32) if inclusive else jnp.zeros(parts[0].shape, F32)
    for k in range(1, len(parts)):
        total = total + jnp.where((me ^ k) < me, parts[k].astype(F32), 0.0)
    return total


def earlier_sum(value, inclusive):
    if is_small("tm"):
        return sum_earlier(gather_parts(value, "tm"), inclusive)
    everything = lax.all_gather(value, "tm").astype(F32)
    index = jnp.arange(everything.shape[0]).reshape((-1,) + (1,) * value.ndim)
    me = lax.axis_index("tm")
    keep = index <= me if inclusive else index < me
    return jnp.sum(jnp.where(keep, everything, 0.0), axis=0)


def local(
    start_latent,
    time_index,
    step_weight,
    in_weight,
    mod_weight,
    qkv_weight,
    out_weight,
    head_weight,
):
    rows, channels = start_latent.shape
    n_tensor = lax.axis_size("tensor")
    tokens = rows * n_tensor
    width = in_weight.shape[1]
    chunks = width // LANES
    head_count = qkv_weight.shape[1] // (3 * HD)
    span = out_weight.shape[0]

    inw_parts = gather_weight_parts(in_weight, "tm")
    small = is_small("tensor") and mod_weight.shape[1] % LANES == 0
    if small:
        mod_rows = mod_weight.shape[1] // LANES
        message, step = call(
            modulation_kernel,
            [shape_of((rows + mod_rows, LANES), F32), shape_of((8, LANES), F32)],
            [VMEM, VMEM, HBM, HBM],
            [
                pltpu.VMEM(mod_weight.shape, BF16),
                pltpu.VMEM(start_latent.shape, F32),
                pltpu.SemaphoreType.DMA((2,)),
            ],
            time_index.reshape(1, 1),
            step_weight.reshape(1, 1),
            mod_weight,
            start_latent,
        )
        messages = gather_parts(message, "tensor")
        block_rows = rows
    else:
        step = jnp.full((8, LANES), step_weight[0].astype(F32) / STEP_DIVISOR)
        embedding = embedding_of(time_index, mod_weight.shape[0]).astype(BF16)
        mod_part = jnp.dot(embedding, mod_weight, preferred_element_type=F32)
        modulation = lax.all_gather(mod_part, "tensor", axis=1, tiled=True)
        start_all = lax.all_gather(start_latent, "tensor", axis=0, tiled=True)
        messages = [jnp.concatenate([start_all, modulation.reshape(-1, LANES)], axis=0)]
        block_rows = tokens
    nt, nm = len(messages), len(inw_parts)
    mod_rows = messages[0].shape[0] - block_rows
    padded = -(-mod_rows // 8) * 8
    span_cols = qkv_weight.shape[1]
    gate_rows = -(-(chunks // nm) // 8) * 8
    block = 4 * LANES if span_cols % (4 * LANES) == 0 else span_cols
    near = max(1, span_cols // block * 2 // 3)
    far = max(1, span_cols // block - near)
    qkv_near, inw_parts[0] = call(
        load_kernel,
        [shape_of((width, near * block), BF16), shape_of(inw_parts[0].shape, BF16)],
        [HBM, HBM],
        [pltpu.SemaphoreType.DMA((2,))],
        qkv_weight,
        inw_parts[0],
    )
    factor, base, gram, start_all, inw_all, gate, out_near = call(
        functools.partial(setup_kernel, nt, nm, block),
        [
            shape_of((2 * channels, span_cols), BF16),
            shape_of((8, span_cols), F32),
            shape_of((3 * channels, channels), BF16),
            shape_of((tokens, channels), F32),
            shape_of((nm, channels // nm, width), BF16),
            shape_of((nm, LANES, gate_rows), F32),
            shape_of(out_weight.shape, BF16),
        ],
        [VMEM] * (nt + nm + 1) + [HBM, HBM],
        [
            pltpu.VMEM((nt, block_rows, channels), F32),
            pltpu.VMEM((nt, padded, LANES), F32),
            pltpu.VMEM((nm, gate_rows, LANES), F32),
            pltpu.VMEM((channels + 16, width), BF16),
            pltpu.VMEM((width, far * block), BF16),
            pltpu.SemaphoreType.DMA((far + 1,)),
        ],
        *messages,
        *inw_parts,
        qkv_near,
        qkv_weight,
        out_weight,
        limit=32,
    )
    head_parts = gather_weight_parts(head_weight, "tm")
    late = 1 if nm > 1 else 0
    early = nm - late
    attended, fold_part, resid_part = call(
        functools.partial(attend_kernel, nm, early, head_count),
        [
            shape_of((tokens, head_count * HD), BF16),
            shape_of((span, channels), F32),
            shape_of((channels, channels), F32),
        ],
        [VMEM] * (early + 7),
        [],
        *head_parts[:early],
        start_all,
        factor,
        base,
        gram,
        gate,
        out_near,
        inw_all,
        limit=16,
    )
    folded, resid, vel = call(
        functools.partial(fold_kernel, nm, late, rows),
        [
            shape_of((span, channels), BF16),
            shape_of((2 * channels, channels), BF16),
            shape_of((tokens, channels), BF16),
        ],
        [VMEM] * (late + 8),
        [],
        *head_parts[early:],
        step,
        gate,
        out_near,
        inw_all,
        fold_part,
        resid_part,
        attended,
        start_all,
        limit=16,
    )
    small = is_small("tensor")
    for iteration in range(1, ITERS):
        last = iteration + 1 == ITERS
        earlier = earlier_sum(vel, False)
        if small:
            pieces = gather_parts(earlier.astype(BF16), "tensor")
        else:
            pieces = [lax.psum(earlier, "tensor")]
        split = last and small
        if split:
            outs = [shape_of((rows, channels), F32)] * n_tensor
        else:
            outs = [shape_of((tokens, channels), F32 if last else BF16)]
        vels = call(
            functools.partial(iterate_kernel, len(pieces), rows, head_count, split),
            outs,
            [VMEM] * (len(pieces) + 7),
            [pltpu.VMEM((n_tensor, rows, channels), F32)],
            *pieces,
            step,
            start_all,
            factor,
            base,
            gram,
            folded,
            resid,
        )
        vel = vels[0]
    if small:
        drift = vels[0]
        for k in range(1, n_tensor):
            drift = drift + swap(vels[k], "tensor", k)
    else:
        drift = lax.psum_scatter(vel, "tensor", scatter_dimension=0, tiled=True)
    return (start_latent + earlier_sum(drift, True))[None]


def solution(mesh):
    return jax.shard_map(
        local,
        mesh=mesh,
        in_specs=(
            P(("groups", "tensor"), None),
            P(("groups", "tm")),
            P(("groups", "tm")),
            P("tm", None),
            P(None, "tensor"),
            P(None, "tensor"),
            P("tensor", None),
            P("tm", None),
        ),
        out_specs=P(("groups", "tm"), "tensor", None),
        check_vma=False,
    )
```

```python
import functools
import math

import jax
import jax.numpy as jnp
from jax import lax
from jax.experimental import pallas as pl
from jax.experimental.pallas import tpu as pltpu
from jax.sharding import PartitionSpec as P


HD = 128
LANES = 128
ITERS = 2
NORM_EPS = 1e-06
STEP_DIVISOR = 64.0
F32 = jnp.float32
BF16 = jnp.bfloat16
VMEM = pl.BlockSpec(memory_space=pltpu.VMEM)
SMEM = pl.BlockSpec(memory_space=pltpu.SMEM)
HBM = pl.BlockSpec(memory_space=pltpu.HBM)


def embedding_of(time_index, width):
    half_width = width // 2
    frequency = jnp.exp(
        -math.log(10000.0) * jnp.arange(half_width).astype(F32) / half_width
    )
    angles = time_index.astype(F32)[:, None] * frequency[None, :]
    return jnp.concatenate([jnp.cos(angles), jnp.sin(angles)], axis=1)


def is_small(axis):
    return lax.axis_size(axis) in (2, 4)


def swap(value, axis, k):
    n = lax.axis_size(axis)
    return lax.ppermute(value, axis, [(i, i ^ k) for i in range(n)])


def gather_parts(value, axis):
    if is_small(axis):
        return [value] + [swap(value, axis, k) for k in range(1, lax.axis_size(axis))]
    return [lax.all_gather(value, axis, axis=0, tiled=True)]


def gather_weight_parts(value, axis):
    n = lax.axis_size(axis)
    if n != 4:
        return gather_parts(value, axis)
    far = swap(value, axis, 2)
    near = swap(value, axis, 1)
    return [value, near, far, swap(far, axis, 1)]


def place(axis, parts, k):
    if parts == 1:
        return 0
    return lax.axis_index(axis) ^ k


def bdot(a, b):
    return jnp.dot(a, b, preferred_element_type=F32)


def bdot_t(a, b):
    return lax.dot_general(a, b, (((1,), (1,)), ((), ())), preferred_element_type=F32)


def split_terms(value, terms):
    out = []
    for _ in range(terms):
        piece = value.astype(BF16)
        out.append(piece)
        value = value - piece.astype(F32)
    return out


def run_copies(copies):
    for copy in copies:
        copy.start()
    return copies


def wait_copies(copies):
    for copy in copies:
        copy.wait()


def modulation_kernel(time_ref, weight_hbm, start_hbm, out_ref, weight_ref, start_ref, sems):
    rows = start_ref.shape[0]
    half = weight_ref.shape[0] // 2
    pairs = ((weight_hbm, weight_ref), (start_hbm, start_ref))
    copies = run_copies(
        [pltpu.make_async_copy(a, b, sems.at[i]) for i, (a, b) in enumerate(pairs)]
    )
    index = lax.broadcasted_iota(jnp.int32, (16, half), 1).astype(F32)
    angles = time_ref[0].astype(F32) * jnp.exp(-math.log(10000.0) * index / half)
    embedding = jnp.concatenate([jnp.cos(angles), jnp.sin(angles)], axis=1).astype(BF16)
    wait_copies(copies)
    result = bdot(embedding, weight_ref[...])
    out_ref[0:rows, :] = start_ref[...]
    for r in range(weight_ref.shape[1] // LANES):
        out_ref[rows + r : rows + r + 1, :] = result[0:1, r * LANES : (r + 1) * LANES]


def load_kernel(weight_ref, qkv_hbm, inw_hbm, qkv_ref, inw_ref, step_ref, sems):
    cols = qkv_ref.shape[1]
    copies = run_copies(
        [
            pltpu.make_async_copy(inw_hbm, inw_ref, sems.at[0]),
            pltpu.make_async_copy(qkv_hbm.at[:, pl.ds(0, cols)], qkv_ref, sems.at[1]),
        ]
    )
    step_ref[...] = jnp.full(step_ref.shape, weight_ref[0].astype(F32) * (1.0 / STEP_DIVISOR))
    wait_copies(copies)


def attend(x, factors, base, gram, head_count):
    twice = jnp.concatenate([x, x], axis=1)
    thrice = jnp.concatenate([twice, x], axis=1)
    heads = [slice(h * 3 * HD, (h + 1) * 3 * HD) for h in range(head_count)]
    quadratic = bdot(thrice, gram[...])
    raw = [bdot(twice, factors[:, cols]) for cols in heads]
    spread = jnp.sum(quadratic * x.astype(F32), axis=1, keepdims=True)
    scale = lax.rsqrt(jnp.maximum(spread, 0.0) + NORM_EPS)
    qkv = [(r * scale + base[0:1, cols]).astype(BF16) for r, cols in zip(raw, heads)]
    scores = [bdot_t(p[:, :HD], p[:, HD : 2 * HD]) * (1.0 / math.sqrt(HD)) for p in qkv]
    tops = [jnp.max(s, axis=1, keepdims=True) for s in scores]
    weights = [jnp.exp(s - t) for s, t in zip(scores, tops)]
    sums = [jnp.sum(w, axis=1, keepdims=True) for w in weights]
    probs = [(w / n).astype(BF16) for w, n in zip(weights, sums)]
    outs = [bdot(w, p[:, 2 * HD :]).astype(BF16) for w, p in zip(probs, qkv)]
    return outs[0] if head_count == 1 else jnp.concatenate(outs, axis=1)


def setup_kernel(nt, nm, block, *refs):
    msgs, refs = refs[:nt], refs[nt:]
    inws, refs = refs[:nm], refs[nm:]
    near_ref, qkv_hbm, out_w_hbm, refs = refs[0], refs[1], refs[2], refs[3:]
    factor_ref, base_ref, gram_ref, start_ref, inw_ref, gate_ref, out_w_ref = refs[:7]
    start_s, mod_s, z_s, qkv_s, sems = refs[7:]
    near = near_ref.shape[1] // block
    count = factor_ref.shape[1] // block
    copies = run_copies(
        [
            pltpu.make_async_copy(
                qkv_hbm.at[:, pl.ds(n * block, block)],
                qkv_s.at[:, pl.ds((n - near) * block, block)],
                sems.at[n - near],
            )
            for n in range(near, count)
        ]
        + [pltpu.make_async_copy(out_w_hbm, out_w_ref, sems.at[count - near])]
    )
    for k, msg in enumerate(msgs):
        at = place("tensor", nt, k)
        start_s[at] = msg[0 : start_s.shape[1], :]
        mod_s[at, 0 : msg.shape[0] - start_s.shape[1], :] = msg[start_s.shape[1] :, :]
    for k in range(nm):
        inw_ref[place("tm", nm, k)] = inws[k][...]
    channels, width = gram_ref.shape[1], z_s.shape[1]
    chunks = width // LANES
    per = 3 * chunks // nt

    def mod_row(r):
        return mod_s[r // per, r % per : r % per + 1, :]

    def columns(c, n):
        return inw_ref[:, :, c * LANES : (c + n) * LANES].reshape(channels, n * LANES)

    total = jnp.zeros((channels, LANES), F32)
    for c in range(chunks):
        total = total + columns(c, 1).astype(F32)
    mean = jnp.sum(total, axis=1, keepdims=True) * (1.0 / width)
    first = jnp.zeros((channels + 16, block), F32)
    group = 6
    for g in range(0, chunks, group):
        for c in range(g, g + group):
            cols = slice(c * LANES, (c + 1) * LANES)
            centered = columns(c, 1).astype(F32) - mean
            z_s[0:channels, cols] = (centered * (1.0 + mod_row(chunks + c))).astype(BF16)
            shift = jnp.broadcast_to(mod_row(c), (16, LANES)).astype(BF16)
            z_s[channels : channels + 16, cols] = shift
        cols = slice(g * LANES, (g + group) * LANES)
        first = first + bdot(z_s[:, cols], near_ref[cols, 0:block])

    def keep(result, n):
        at = slice(n * block, (n + 1) * block)
        high, low = split_terms(result[0:channels], 2)
        factor_ref[0:channels, at] = high
        factor_ref[channels : 2 * channels, at] = low
        base_ref[:, at] = result[channels : channels + 8]

    keep(first, 0)
    for p in range(nm):
        for r in range(chunks // nm):
            gate_ref[p, r : r + 1, :] = mod_row(2 * chunks + p * (chunks // nm) + r)
    gram = jnp.zeros((channels, channels), F32)
    for c in range(0, chunks, 6):
        gram = gram + bdot_t(columns(c, 6), columns(c, 6))
    mean_b = jnp.broadcast_to(mean, (channels, channels))
    gram = gram * (1.0 / width) - mean_b * mean_b.T
    for i, piece in enumerate(split_terms(gram, 3)):
        gram_ref[i * channels : (i + 1) * channels, :] = piece
    start_ref[...] = start_s[...].reshape(start_ref.shape)

    for n in range(1, count):
        if n < near:
            weight = near_ref[:, n * block : (n + 1) * block]
        else:
            copies[n - near].wait()
            weight = qkv_s[:, (n - near) * block : (n - near + 1) * block]
        keep(bdot(z_s[...], weight), n)
    copies[count - near].wait()


def fold_parts(nm, first, heads, gate_ref, out_w_ref, inw_ref):
    folded, resid = 0.0, 0.0
    for i, head_ref in enumerate(heads):
        size = head_ref.shape[0]
        at = place("tm", nm, first + i)
        cols = pl.ds(pl.multiple_of(at * size, LANES), size)
        gate = gate_ref[at]
        gated = []
        for r in range(size // LANES):
            turned = head_ref[r * LANES : (r + 1) * LANES, :].astype(F32).T
            gated.append((turned * gate[r : r + 1, :]).astype(BF16))
        folded = folded + bdot_t(jnp.concatenate(gated, axis=1), out_w_ref[:, cols])
        inw = inw_ref[:, :, cols].reshape(-1, size)
        resid = resid + bdot(inw, head_ref[...])
    return folded, resid


def attend_kernel(nm, early, head_count, *refs):
    heads, refs = refs[:early], refs[early:]
    start_ref, factor_ref, base_ref, gram_ref, gate_ref, out_w_ref, inw_ref = refs[:7]
    att_ref, fold_ref, resid_ref = refs[7:]
    x = start_ref[...].astype(BF16)
    fold_ref[...], resid_ref[...] = fold_parts(nm, 0, heads, gate_ref, out_w_ref, inw_ref)
    att_ref[...] = attend(x, factor_ref, base_ref, gram_ref, head_count)


def add_own_rows(result, residual, rows):
    first = lax.axis_index("tensor") * rows
    at = lax.broadcasted_iota(jnp.int32, result.shape, 0)
    return result + jnp.where((at >= first) & (at < first + rows), residual, 0.0)


def fold_kernel(nm, late, rows, *refs):
    heads, refs = refs[:late], refs[late:]
    step_ref, gate_ref, out_w_ref, inw_ref, fold_in, resid_in, att_ref, start_ref = refs[:8]
    fold_ref, resid_ref, vel_ref = refs[8:]
    channels = resid_in.shape[0]
    total, resid = fold_in[...], resid_in[...]
    if late:
        more = fold_parts(nm, nm - late, heads, gate_ref, out_w_ref, inw_ref)
        total, resid = total + more[0], resid + more[1]
    folded = total.astype(BF16)
    fold_ref[...] = folded
    for i, term in enumerate(split_terms(resid, 2)):
        resid_ref[i * channels : (i + 1) * channels, :] = term
    x = start_ref[...].astype(BF16)
    vel = bdot_t(att_ref[...], folded)
    residual = bdot(jnp.concatenate([x, x], axis=1), resid_ref[...])
    vel_ref[...] = (add_own_rows(vel, residual, rows) * step_ref[0:1, :]).astype(vel_ref.dtype)


def iterate_kernel(nparts, rows, head_count, split, *refs):
    parts, refs = refs[:nparts], refs[nparts:]
    step_ref, start_ref, factor_ref, base_ref, gram_ref, fold_ref, resid_ref = refs[:7]
    outs = refs[7:-1]
    vel_s = refs[-1]
    guess = start_ref[...]
    for part in parts:
        guess = guess + part[...].astype(F32)
    x = guess.astype(BF16)
    attended = attend(x, factor_ref, base_ref, gram_ref, head_count)
    vel = bdot_t(attended, fold_ref[...])
    residual = bdot(jnp.concatenate([x, x], axis=1), resid_ref[...])
    vel = add_own_rows(vel, residual, rows) * step_ref[0:1, :]
    if not split:
        outs[0][...] = vel.astype(outs[0].dtype)
        return
    vel_s[...] = vel.reshape(vel_s.shape)
    for k in range(len(outs)):
        outs[k][...] = vel_s[lax.axis_index("tensor") ^ k]


def shape_of(shape, dtype):
    return jax.ShapeDtypeStruct(shape, dtype)


def call(kernel, outs, in_specs, scratch, *args, cost=4 * 2**20, limit=8):
    args = [
        pltpu.with_memory_space_constraint(arg, pltpu.HBM) if spec is HBM else arg
        for arg, spec in zip(args, in_specs)
    ]
    return pl.pallas_call(
        kernel,
        out_shape=outs,
        in_specs=in_specs,
        out_specs=[VMEM] * len(outs),
        scratch_shapes=scratch,
        compiler_params=pltpu.CompilerParams(vmem_limit_bytes=limit * 2**20),
        cost_estimate=pl.CostEstimate(flops=0, bytes_accessed=cost, transcendentals=0),
    )(*args)


def sum_earlier(parts, inclusive):
    me = lax.axis_index("tm")
    total = parts[0].astype(F32) if inclusive else jnp.zeros(parts[0].shape, F32)
    for k in range(1, len(parts)):
        total = total + jnp.where((me ^ k) < me, parts[k].astype(F32), 0.0)
    return total


def earlier_sum(value, inclusive):
    if is_small("tm"):
        return sum_earlier(gather_parts(value, "tm"), inclusive)
    everything = lax.all_gather(value, "tm").astype(F32)
    index = jnp.arange(everything.shape[0]).reshape((-1,) + (1,) * value.ndim)
    me = lax.axis_index("tm")
    keep = index <= me if inclusive else index < me
    return jnp.sum(jnp.where(keep, everything, 0.0), axis=0)


def local(
    start_latent,
    time_index,
    step_weight,
    in_weight,
    mod_weight,
    qkv_weight,
    out_weight,
    head_weight,
):
    rows, channels = start_latent.shape
    n_tensor = lax.axis_size("tensor")
    tokens = rows * n_tensor
    width = in_weight.shape[1]
    chunks = width // LANES
    head_count = qkv_weight.shape[1] // (3 * HD)
    span = out_weight.shape[0]

    inw_parts = gather_weight_parts(in_weight, "tm")
    small = is_small("tensor") and mod_weight.shape[1] % LANES == 0
    if small:
        mod_rows = mod_weight.shape[1] // LANES
        message = call(
            modulation_kernel,
            [shape_of((rows + mod_rows, LANES), F32)],
            [SMEM, HBM, HBM],
            [
                pltpu.VMEM(mod_weight.shape, BF16),
                pltpu.VMEM(start_latent.shape, F32),
                pltpu.SemaphoreType.DMA((2,)),
            ],
            time_index,
            mod_weight,
            start_latent,
        )[0]
        messages = gather_parts(message, "tensor")
        block_rows = rows
    else:
        embedding = embedding_of(time_index, mod_weight.shape[0]).astype(BF16)
        mod_part = jnp.dot(embedding, mod_weight, preferred_element_type=F32)
        modulation = lax.all_gather(mod_part, "tensor", axis=1, tiled=True)
        start_all = lax.all_gather(start_latent, "tensor", axis=0, tiled=True)
        messages = [jnp.concatenate([start_all, modulation.reshape(-1, LANES)], axis=0)]
        block_rows = tokens
    nt, nm = len(messages), len(inw_parts)
    mod_rows = messages[0].shape[0] - block_rows
    padded = -(-mod_rows // 8) * 8
    span_cols = qkv_weight.shape[1]
    gate_rows = -(-(chunks // nm) // 8) * 8
    block = 4 * LANES if span_cols % (4 * LANES) == 0 else span_cols
    near = max(1, span_cols // block // 3)
    far = max(1, span_cols // block - near)
    qkv_near, inw_parts[0], step = call(
        load_kernel,
        [
            shape_of((width, near * block), BF16),
            shape_of(inw_parts[0].shape, BF16),
            shape_of((8, LANES), F32),
        ],
        [SMEM, HBM, HBM],
        [pltpu.SemaphoreType.DMA((2,))],
        step_weight,
        qkv_weight,
        inw_parts[0],
    )
    factor, base, gram, start_all, inw_all, gate, out_near = call(
        functools.partial(setup_kernel, nt, nm, block),
        [
            shape_of((2 * channels, span_cols), BF16),
            shape_of((8, span_cols), F32),
            shape_of((3 * channels, channels), BF16),
            shape_of((tokens, channels), F32),
            shape_of((nm, channels // nm, width), BF16),
            shape_of((nm, gate_rows, LANES), F32),
            shape_of(out_weight.shape, BF16),
        ],
        [VMEM] * (nt + nm + 1) + [HBM, HBM],
        [
            pltpu.VMEM((nt, block_rows, channels), F32),
            pltpu.VMEM((nt, padded, LANES), F32),
            pltpu.VMEM((channels + 16, width), BF16),
            pltpu.VMEM((width, far * block), BF16),
            pltpu.SemaphoreType.DMA((far + 1,)),
        ],
        *messages,
        *inw_parts,
        qkv_near,
        qkv_weight,
        out_weight,
        limit=32,
    )
    head_parts = gather_weight_parts(head_weight, "tm")
    late = 1 if nm > 1 else 0
    early = nm - late
    attended, fold_part, resid_part = call(
        functools.partial(attend_kernel, nm, early, head_count),
        [
            shape_of((tokens, head_count * HD), BF16),
            shape_of((channels, span), F32),
            shape_of((channels, channels), F32),
        ],
        [VMEM] * (early + 7),
        [],
        *head_parts[:early],
        start_all,
        factor,
        base,
        gram,
        gate,
        out_near,
        inw_all,
        limit=16,
    )
    folded, resid, vel = call(
        functools.partial(fold_kernel, nm, late, rows),
        [
            shape_of((channels, span), BF16),
            shape_of((2 * channels, channels), BF16),
            shape_of((tokens, channels), BF16),
        ],
        [VMEM] * (late + 8),
        [],
        *head_parts[early:],
        step,
        gate,
        out_near,
        inw_all,
        fold_part,
        resid_part,
        attended,
        start_all,
        limit=16,
    )
    small = is_small("tensor")
    for iteration in range(1, ITERS):
        last = iteration + 1 == ITERS
        earlier = earlier_sum(vel, False)
        if small:
            pieces = gather_parts(earlier.astype(BF16), "tensor")
        else:
            pieces = [lax.psum(earlier, "tensor")]
        split = last and small
        if split:
            outs = [shape_of((rows, channels), F32)] * n_tensor
        else:
            outs = [shape_of((tokens, channels), F32 if last else BF16)]
        vels = call(
            functools.partial(iterate_kernel, len(pieces), rows, head_count, split),
            outs,
            [VMEM] * (len(pieces) + 7),
            [pltpu.VMEM((n_tensor, rows, channels), F32)],
            *pieces,
            step,
            start_all,
            factor,
            base,
            gram,
            folded,
            resid,
        )
        vel = vels[0]
    if small:
        drift = vels[0]
        for k in range(1, n_tensor):
            drift = drift + swap(vels[k], "tensor", k)
    else:
        drift = lax.psum_scatter(vel, "tensor", scatter_dimension=0, tiled=True)
    return (start_latent + earlier_sum(drift, True))[None]


def solution(mesh):
    return jax.shard_map(
        local,
        mesh=mesh,
        in_specs=(
            P(("groups", "tensor"), None),
            P(("groups", "tm")),
            P(("groups", "tm")),
            P("tm", None),
            P(None, "tensor"),
            P(None, "tensor"),
            P("tensor", None),
            P("tm", None),
        ),
        out_specs=P(("groups", "tm"), "tensor", None),
        check_vma=False,
    )
```

```python
import functools
import math

import jax
import jax.numpy as jnp
from jax import lax
from jax.experimental import pallas as pl
from jax.experimental.pallas import tpu as pltpu
from jax.sharding import PartitionSpec as P


HD = 128
LANES = 128
ITERS = 2
NORM_EPS = 1e-06
STEP_DIVISOR = 64.0
F32 = jnp.float32
BF16 = jnp.bfloat16
VMEM = pl.BlockSpec(memory_space=pltpu.VMEM)
SMEM = pl.BlockSpec(memory_space=pltpu.SMEM)
HBM = pl.BlockSpec(memory_space=pltpu.HBM)


def embedding_of(time_index, width):
    half_width = width // 2
    frequency = jnp.exp(
        -math.log(10000.0) * jnp.arange(half_width).astype(F32) / half_width
    )
    angles = time_index.astype(F32)[:, None] * frequency[None, :]
    return jnp.concatenate([jnp.cos(angles), jnp.sin(angles)], axis=1)


def is_small(axis):
    return lax.axis_size(axis) in (2, 4)


def swap(value, axis, k):
    n = lax.axis_size(axis)
    return lax.ppermute(value, axis, [(i, i ^ k) for i in range(n)])


def gather_parts(value, axis):
    if is_small(axis):
        return [value] + [swap(value, axis, k) for k in range(1, lax.axis_size(axis))]
    return [lax.all_gather(value, axis, axis=0, tiled=True)]


def gather_weight_parts(value, axis):
    n = lax.axis_size(axis)
    if n != 4:
        return gather_parts(value, axis)
    far = swap(value, axis, 2)
    near = swap(value, axis, 1)
    return [value, near, far, swap(far, axis, 1)]


def place(axis, parts, k):
    if parts == 1:
        return 0
    return lax.axis_index(axis) ^ k


def bdot(a, b):
    return jnp.dot(a, b, preferred_element_type=F32)


def bdot_t(a, b):
    return lax.dot_general(a, b, (((1,), (1,)), ((), ())), preferred_element_type=F32)


def split_terms(value, terms):
    out = []
    for _ in range(terms):
        piece = value.astype(BF16)
        out.append(piece)
        value = value - piece.astype(F32)
    return out


def run_copies(copies):
    for copy in copies:
        copy.start()
    return copies


def wait_copies(copies):
    for copy in copies:
        copy.wait()


def modulation_kernel(time_ref, weight_hbm, start_hbm, out_ref, weight_ref, start_ref, sems):
    rows = start_ref.shape[0]
    half = weight_ref.shape[0] // 2
    pairs = ((weight_hbm, weight_ref), (start_hbm, start_ref))
    copies = run_copies(
        [pltpu.make_async_copy(a, b, sems.at[i]) for i, (a, b) in enumerate(pairs)]
    )
    index = lax.broadcasted_iota(jnp.int32, (16, half), 1).astype(F32)
    angles = time_ref[0].astype(F32) * jnp.exp(-math.log(10000.0) * index / half)
    embedding = jnp.concatenate([jnp.cos(angles), jnp.sin(angles)], axis=1).astype(BF16)
    wait_copies(copies)
    result = bdot(embedding, weight_ref[...])
    out_ref[0:rows, :] = start_ref[...]
    for r in range(weight_ref.shape[1] // LANES):
        out_ref[rows + r : rows + r + 1, :] = result[0:1, r * LANES : (r + 1) * LANES]


def channel_columns(inw_ref, c, n):
    return inw_ref[:, :, c * LANES : (c + n) * LANES].reshape(-1, n * LANES)


def load_kernel(nm, weight_ref, qkv_hbm, inw_hbm, *refs):
    inws, refs = refs[: nm - 1], refs[nm - 1 :]
    qkv_ref, inw_ref, mean_ref, gram_ref, step_ref, sems = refs
    cols = qkv_ref.shape[1]
    copies = run_copies(
        [
            pltpu.make_async_copy(inw_hbm, inw_ref.at[place("tm", nm, 0)], sems.at[0]),
            pltpu.make_async_copy(qkv_hbm.at[:, pl.ds(0, cols)], qkv_ref, sems.at[1]),
        ]
    )
    step_ref[...] = jnp.full(step_ref.shape, weight_ref[0].astype(F32) * (1.0 / STEP_DIVISOR))
    for k in range(1, nm):
        inw_ref[place("tm", nm, k)] = inws[k - 1][...]
    copies[0].wait()
    channels, width = mean_ref.shape[0], inw_ref.shape[2]
    chunks = width // LANES
    total = jnp.zeros((channels, LANES), F32)
    for c in range(chunks):
        total = total + channel_columns(inw_ref, c, 1).astype(F32)
    mean = jnp.sum(total, axis=1, keepdims=True) * (1.0 / width)
    mean_b = jnp.broadcast_to(mean, mean_ref.shape)
    mean_ref[...] = mean_b
    gram = jnp.zeros((channels, channels), F32)
    for c in range(0, chunks, 6):
        piece = channel_columns(inw_ref, c, 6)
        gram = gram + bdot_t(piece, piece)
    mean_c = jnp.broadcast_to(mean, (channels, channels))
    gram = gram * (1.0 / width) - mean_c * mean_c.T
    for i, term in enumerate(split_terms(gram, 3)):
        gram_ref[i * channels : (i + 1) * channels, :] = term
    copies[1].wait()


def attend(x, factors, base, gram, head_count):
    twice = jnp.concatenate([x, x], axis=1)
    thrice = jnp.concatenate([twice, x], axis=1)
    heads = [slice(h * 3 * HD, (h + 1) * 3 * HD) for h in range(head_count)]
    quadratic = bdot(thrice, gram[...])
    raw = [bdot(twice, factors[:, cols]) for cols in heads]
    spread = jnp.sum(quadratic * x.astype(F32), axis=1, keepdims=True)
    scale = lax.rsqrt(jnp.maximum(spread, 0.0) + NORM_EPS)
    qkv = [(r * scale + base[0:1, cols]).astype(BF16) for r, cols in zip(raw, heads)]
    scores = [bdot_t(p[:, :HD], p[:, HD : 2 * HD]) * (1.0 / math.sqrt(HD)) for p in qkv]
    tops = [jnp.max(s, axis=1, keepdims=True) for s in scores]
    weights = [jnp.exp(s - t) for s, t in zip(scores, tops)]
    sums = [jnp.sum(w, axis=1, keepdims=True) for w in weights]
    probs = [(w / n).astype(BF16) for w, n in zip(weights, sums)]
    outs = [bdot(w, p[:, 2 * HD :]).astype(BF16) for w, p in zip(probs, qkv)]
    return outs[0] if head_count == 1 else jnp.concatenate(outs, axis=1)


def setup_kernel(nt, nm, block, *refs):
    msgs, refs = refs[:nt], refs[nt:]
    inw_ref, mean_ref, near_ref, qkv_hbm, out_w_hbm = refs[:5]
    refs = refs[5:]
    factor_ref, base_ref, start_ref, gate_ref, out_w_ref = refs[:5]
    start_s, mod_s, gate_s, z_s, qkv_s, sems = refs[5:]
    near = near_ref.shape[1] // block
    count = factor_ref.shape[1] // block
    copies = run_copies(
        [
            pltpu.make_async_copy(
                qkv_hbm.at[:, pl.ds(n * block, block)],
                qkv_s.at[:, pl.ds((n - near) * block, block)],
                sems.at[n - near],
            )
            for n in range(near, count)
        ]
        + [pltpu.make_async_copy(out_w_hbm, out_w_ref, sems.at[count - near])]
    )
    for k, msg in enumerate(msgs):
        at = place("tensor", nt, k)
        start_s[at] = msg[0 : start_s.shape[1], :]
        mod_s[at, 0 : msg.shape[0] - start_s.shape[1], :] = msg[start_s.shape[1] :, :]
    channels, width = mean_ref.shape[0], z_s.shape[1]
    chunks = width // LANES
    per = 3 * chunks // nt

    def mod_row(r):
        return mod_s[r // per, r % per : r % per + 1, :]

    mean = mean_ref[...]
    first = jnp.zeros((channels + 16, block), F32)
    group = 6
    for g in range(0, chunks, group):
        for c in range(g, g + group):
            cols = slice(c * LANES, (c + 1) * LANES)
            centered = channel_columns(inw_ref, c, 1).astype(F32) - mean
            z_s[0:channels, cols] = (centered * (1.0 + mod_row(chunks + c))).astype(BF16)
            shift = jnp.broadcast_to(mod_row(c), (16, LANES)).astype(BF16)
            z_s[channels : channels + 16, cols] = shift
        cols = slice(g * LANES, (g + group) * LANES)
        first = first + bdot(z_s[:, cols], near_ref[cols, 0:block])

    def keep(result, n):
        at = slice(n * block, (n + 1) * block)
        high, low = split_terms(result[0:channels], 2)
        factor_ref[0:channels, at] = high
        factor_ref[channels : 2 * channels, at] = low
        base_ref[:, at] = result[channels : channels + 8]

    keep(first, 0)
    for p in range(nm):
        for r in range(chunks // nm):
            gate_s[p, r : r + 1, :] = mod_row(2 * chunks + p * (chunks // nm) + r)
        gate_ref[p] = gate_s[p].T
    start_ref[...] = start_s[...].reshape(start_ref.shape)

    for n in range(1, count):
        if n < near:
            weight = near_ref[:, n * block : (n + 1) * block]
        else:
            copies[n - near].wait()
            weight = qkv_s[:, (n - near) * block : (n - near + 1) * block]
        keep(bdot(z_s[...], weight), n)
    copies[count - near].wait()


def fold_parts(nm, first, heads, gate_ref, out_w_ref, inw_ref):
    folded, resid = 0.0, 0.0
    for i, head_ref in enumerate(heads):
        size, _ = head_ref.shape
        at = place("tm", nm, first + i)
        cols = pl.ds(pl.multiple_of(at * size, LANES), size)
        gate = gate_ref[at]
        gated = []
        for r in range(size // LANES):
            rows = head_ref[r * LANES : (r + 1) * LANES, :].astype(F32)
            gated.append((rows * gate[:, r : r + 1]).astype(BF16))
        folded = folded + bdot(out_w_ref[:, cols], jnp.concatenate(gated, axis=0))
        inw = inw_ref[:, :, cols].reshape(-1, size)
        resid = resid + bdot(inw, head_ref[...])
    return folded, resid


def attend_kernel(nm, early, head_count, *refs):
    heads, refs = refs[:early], refs[early:]
    start_ref, factor_ref, base_ref, gram_ref, gate_ref, out_w_ref, inw_ref = refs[:7]
    att_ref, fold_ref, resid_ref = refs[7:]
    x = start_ref[...].astype(BF16)
    fold_ref[...], resid_ref[...] = fold_parts(nm, 0, heads, gate_ref, out_w_ref, inw_ref)
    att_ref[...] = attend(x, factor_ref, base_ref, gram_ref, head_count)


def add_own_rows(result, residual, rows):
    first = lax.axis_index("tensor") * rows
    at = lax.broadcasted_iota(jnp.int32, result.shape, 0)
    return result + jnp.where((at >= first) & (at < first + rows), residual, 0.0)


def fold_kernel(nm, late, rows, *refs):
    heads, refs = refs[:late], refs[late:]
    step_ref, gate_ref, out_w_ref, inw_ref, fold_in, resid_in, att_ref, start_ref = refs[:8]
    fold_ref, resid_ref, vel_ref = refs[8:]
    channels = resid_in.shape[0]
    total, resid = fold_in[...], resid_in[...]
    if late:
        more = fold_parts(nm, nm - late, heads, gate_ref, out_w_ref, inw_ref)
        total, resid = total + more[0], resid + more[1]
    folded = total.astype(BF16)
    fold_ref[...] = folded
    for i, term in enumerate(split_terms(resid, 2)):
        resid_ref[i * channels : (i + 1) * channels, :] = term
    x = start_ref[...].astype(BF16)
    vel = bdot(att_ref[...], folded)
    residual = bdot(jnp.concatenate([x, x], axis=1), resid_ref[...])
    vel_ref[...] = (add_own_rows(vel, residual, rows) * step_ref[0:1, :]).astype(vel_ref.dtype)


def iterate_kernel(nparts, rows, head_count, split, *refs):
    parts, refs = refs[:nparts], refs[nparts:]
    step_ref, start_ref, factor_ref, base_ref, gram_ref, fold_ref, resid_ref = refs[:7]
    outs = refs[7:-1]
    vel_s = refs[-1]
    guess = start_ref[...]
    for part in parts:
        guess = guess + part[...].astype(F32)
    x = guess.astype(BF16)
    attended = attend(x, factor_ref, base_ref, gram_ref, head_count)
    vel = bdot(attended, fold_ref[...])
    residual = bdot(jnp.concatenate([x, x], axis=1), resid_ref[...])
    vel = add_own_rows(vel, residual, rows) * step_ref[0:1, :]
    if not split:
        outs[0][...] = vel.astype(outs[0].dtype)
        return
    vel_s[...] = vel.reshape(vel_s.shape)
    for k in range(len(outs)):
        outs[k][...] = vel_s[lax.axis_index("tensor") ^ k]


def shape_of(shape, dtype):
    return jax.ShapeDtypeStruct(shape, dtype)


def call(kernel, outs, in_specs, scratch, *args, cost=4 * 2**20, limit=8):
    args = [
        pltpu.with_memory_space_constraint(arg, pltpu.HBM) if spec is HBM else arg
        for arg, spec in zip(args, in_specs)
    ]
    return pl.pallas_call(
        kernel,
        out_shape=outs,
        in_specs=in_specs,
        out_specs=[VMEM] * len(outs),
        scratch_shapes=scratch,
        compiler_params=pltpu.CompilerParams(vmem_limit_bytes=limit * 2**20),
        cost_estimate=pl.CostEstimate(flops=0, bytes_accessed=cost, transcendentals=0),
    )(*args)


def sum_earlier(parts, inclusive):
    me = lax.axis_index("tm")
    total = parts[0].astype(F32) if inclusive else jnp.zeros(parts[0].shape, F32)
    for k in range(1, len(parts)):
        total = total + jnp.where((me ^ k) < me, parts[k].astype(F32), 0.0)
    return total


def earlier_sum(value, inclusive):
    if is_small("tm"):
        return sum_earlier(gather_parts(value, "tm"), inclusive)
    everything = lax.all_gather(value, "tm").astype(F32)
    index = jnp.arange(everything.shape[0]).reshape((-1,) + (1,) * value.ndim)
    me = lax.axis_index("tm")
    keep = index <= me if inclusive else index < me
    return jnp.sum(jnp.where(keep, everything, 0.0), axis=0)


def local(
    start_latent,
    time_index,
    step_weight,
    in_weight,
    mod_weight,
    qkv_weight,
    out_weight,
    head_weight,
):
    rows, channels = start_latent.shape
    n_tensor = lax.axis_size("tensor")
    tokens = rows * n_tensor
    width = in_weight.shape[1]
    chunks = width // LANES
    head_count = qkv_weight.shape[1] // (3 * HD)
    span = out_weight.shape[0]

    inw_parts = gather_weight_parts(in_weight, "tm")
    small = is_small("tensor") and mod_weight.shape[1] % LANES == 0
    if small:
        mod_rows = mod_weight.shape[1] // LANES
        message = call(
            modulation_kernel,
            [shape_of((rows + mod_rows, LANES), F32)],
            [SMEM, HBM, HBM],
            [
                pltpu.VMEM(mod_weight.shape, BF16),
                pltpu.VMEM(start_latent.shape, F32),
                pltpu.SemaphoreType.DMA((2,)),
            ],
            time_index,
            mod_weight,
            start_latent,
        )[0]
        messages = gather_parts(message, "tensor")
        block_rows = rows
    else:
        embedding = embedding_of(time_index, mod_weight.shape[0]).astype(BF16)
        mod_part = jnp.dot(embedding, mod_weight, preferred_element_type=F32)
        modulation = lax.all_gather(mod_part, "tensor", axis=1, tiled=True)
        start_all = lax.all_gather(start_latent, "tensor", axis=0, tiled=True)
        messages = [jnp.concatenate([start_all, modulation.reshape(-1, LANES)], axis=0)]
        block_rows = tokens
    nt, nm = len(messages), len(inw_parts)
    mod_rows = messages[0].shape[0] - block_rows
    padded = -(-mod_rows // 8) * 8
    span_cols = qkv_weight.shape[1]
    gate_rows = -(-(chunks // nm) // 8) * 8
    block = 4 * LANES if span_cols % (4 * LANES) == 0 else span_cols
    near = max(1, span_cols // block // 3)
    far = max(1, span_cols // block - near)
    qkv_near, inw_all, mean, gram, step = call(
        functools.partial(load_kernel, nm),
        [
            shape_of((width, near * block), BF16),
            shape_of((nm, channels // nm, width), BF16),
            shape_of((channels, LANES), F32),
            shape_of((3 * channels, channels), BF16),
            shape_of((8, LANES), F32),
        ],
        [SMEM, HBM, HBM] + [VMEM] * (nm - 1),
        [pltpu.SemaphoreType.DMA((2,))],
        step_weight,
        qkv_weight,
        *inw_parts,
        limit=16,
    )
    factor, base, start_all, gate, out_near = call(
        functools.partial(setup_kernel, nt, nm, block),
        [
            shape_of((2 * channels, span_cols), BF16),
            shape_of((8, span_cols), F32),
            shape_of((tokens, channels), F32),
            shape_of((nm, LANES, gate_rows), F32),
            shape_of(out_weight.shape, BF16),
        ],
        [VMEM] * (nt + 3) + [HBM, HBM],
        [
            pltpu.VMEM((nt, block_rows, channels), F32),
            pltpu.VMEM((nt, padded, LANES), F32),
            pltpu.VMEM((nm, gate_rows, LANES), F32),
            pltpu.VMEM((channels + 16, width), BF16),
            pltpu.VMEM((width, far * block), BF16),
            pltpu.SemaphoreType.DMA((far + 1,)),
        ],
        *messages,
        inw_all,
        mean,
        qkv_near,
        qkv_weight,
        out_weight,
        limit=32,
    )
    head_parts = gather_weight_parts(head_weight, "tm")
    late = 1 if nm > 1 else 0
    early = nm - late
    attended, fold_part, resid_part = call(
        functools.partial(attend_kernel, nm, early, head_count),
        [
            shape_of((tokens, head_count * HD), BF16),
            shape_of((span, channels), F32),
            shape_of((channels, channels), F32),
        ],
        [VMEM] * (early + 7),
        [],
        *head_parts[:early],
        start_all,
        factor,
        base,
        gram,
        gate,
        out_near,
        inw_all,
        limit=16,
    )
    folded, resid, vel = call(
        functools.partial(fold_kernel, nm, late, rows),
        [
            shape_of((span, channels), BF16),
            shape_of((2 * channels, channels), BF16),
            shape_of((tokens, channels), BF16),
        ],
        [VMEM] * (late + 8),
        [],
        *head_parts[early:],
        step,
        gate,
        out_near,
        inw_all,
        fold_part,
        resid_part,
        attended,
        start_all,
        limit=16,
    )
    small = is_small("tensor")
    for iteration in range(1, ITERS):
        last = iteration + 1 == ITERS
        earlier = earlier_sum(vel, False)
        if small:
            pieces = gather_parts(earlier.astype(BF16), "tensor")
        else:
            pieces = [lax.psum(earlier, "tensor")]
        split = last and small
        if split:
            outs = [shape_of((rows, channels), F32)] * n_tensor
        else:
            outs = [shape_of((tokens, channels), F32 if last else BF16)]
        vels = call(
            functools.partial(iterate_kernel, len(pieces), rows, head_count, split),
            outs,
            [VMEM] * (len(pieces) + 7),
            [pltpu.VMEM((n_tensor, rows, channels), F32)],
            *pieces,
            step,
            start_all,
            factor,
            base,
            gram,
            folded,
            resid,
        )
        vel = vels[0]
    if small:
        drift = vels[0]
        for k in range(1, n_tensor):
            drift = drift + swap(vels[k], "tensor", k)
    else:
        drift = lax.psum_scatter(vel, "tensor", scatter_dimension=0, tiled=True)
    return (start_latent + earlier_sum(drift, True))[None]


def solution(mesh):
    return jax.shard_map(
        local,
        mesh=mesh,
        in_specs=(
            P(("groups", "tensor"), None),
            P(("groups", "tm")),
            P(("groups", "tm")),
            P("tm", None),
            P(None, "tensor"),
            P(None, "tensor"),
            P("tensor", None),
            P("tm", None),
        ),
        out_specs=P(("groups", "tm"), "tensor", None),
        check_vma=False,
    )
```

```python
import functools
import math

import jax
import jax.numpy as jnp
from jax import lax
from jax.experimental import pallas as pl
from jax.experimental.pallas import tpu as pltpu
from jax.sharding import PartitionSpec as P


HD = 128
LANES = 128
ITERS = 2
NORM_EPS = 1e-06
STEP_DIVISOR = 64.0
F32 = jnp.float32
BF16 = jnp.bfloat16
VMEM = pl.BlockSpec(memory_space=pltpu.VMEM)
SMEM = pl.BlockSpec(memory_space=pltpu.SMEM)
HBM = pl.BlockSpec(memory_space=pltpu.HBM)


def embedding_of(time_index, width):
    half_width = width // 2
    frequency = jnp.exp(
        -math.log(10000.0) * jnp.arange(half_width).astype(F32) / half_width
    )
    angles = time_index.astype(F32)[:, None] * frequency[None, :]
    return jnp.concatenate([jnp.cos(angles), jnp.sin(angles)], axis=1)


def is_small(axis):
    return lax.axis_size(axis) in (2, 4)


def swap(value, axis, k):
    n = lax.axis_size(axis)
    return lax.ppermute(value, axis, [(i, i ^ k) for i in range(n)])


def hub_route(value, k):
    n = lax.axis_size("tensor")
    pairs = [
        (t * n + z, t * n + (z ^ k) if t % 2 else (t ^ 2) * n + z)
        for t in range(lax.axis_size("tm"))
        for z in range(n)
    ]
    return lax.ppermute(value, ("tm", "tensor"), pairs)


def hub_earlier_sum(value):
    stacked = jnp.stack([swap(value, "tm", 1), value])
    total = stacked.astype(F32)
    for k in (2, 3, 1):
        total = total + hub_route(stacked, k).astype(F32)
    pair = (total[0] + total[1]).astype(BF16)
    straight, crossed = swap(pair, "tm", 2), swap(pair, "tm", 3)
    me = lax.axis_index("tm")
    odd, high = me % 2 == 1, me >= 2
    far = jnp.where(odd, straight, crossed).astype(F32)
    return jnp.where(high, far, 0.0) + jnp.where(odd, total[0], 0.0)


def gather_parts(value, axis):
    if is_small(axis):
        return [value] + [swap(value, axis, k) for k in range(1, lax.axis_size(axis))]
    return [lax.all_gather(value, axis, axis=0, tiled=True)]


def gather_weight_parts(value, axis):
    n = lax.axis_size(axis)
    if n != 4:
        return gather_parts(value, axis)
    far = swap(value, axis, 2)
    near = swap(value, axis, 1)
    return [value, near, far, swap(far, axis, 1)]


def place(axis, parts, k):
    if parts == 1:
        return 0
    return lax.axis_index(axis) ^ k


def bdot(a, b):
    return jnp.dot(a, b, preferred_element_type=F32)


def bdot_t(a, b):
    return lax.dot_general(a, b, (((1,), (1,)), ((), ())), preferred_element_type=F32)


def split_terms(value, terms):
    out = []
    for _ in range(terms):
        piece = value.astype(BF16)
        out.append(piece)
        value = value - piece.astype(F32)
    return out


def run_copies(copies):
    for copy in copies:
        copy.start()
    return copies


def wait_copies(copies):
    for copy in copies:
        copy.wait()


def modulation_kernel(time_ref, weight_hbm, start_hbm, out_ref, weight_ref, start_ref, sems):
    rows = start_ref.shape[0]
    half = weight_ref.shape[0] // 2
    pairs = ((weight_hbm, weight_ref), (start_hbm, start_ref))
    copies = run_copies(
        [pltpu.make_async_copy(a, b, sems.at[i]) for i, (a, b) in enumerate(pairs)]
    )
    index = lax.broadcasted_iota(jnp.int32, (16, half), 1).astype(F32)
    angles = time_ref[0].astype(F32) * jnp.exp(-math.log(10000.0) * index / half)
    embedding = jnp.concatenate([jnp.cos(angles), jnp.sin(angles)], axis=1).astype(BF16)
    wait_copies(copies)
    result = bdot(embedding, weight_ref[...])
    out_ref[0:rows, :] = start_ref[...]
    for r in range(weight_ref.shape[1] // LANES):
        out_ref[rows + r : rows + r + 1, :] = result[0:1, r * LANES : (r + 1) * LANES]


def channel_columns(inw_ref, c, n):
    return inw_ref[:, :, c * LANES : (c + n) * LANES].reshape(-1, n * LANES)


def load_kernel(nm, weight_ref, qkv_hbm, inw_hbm, *refs):
    inws, refs = refs[: nm - 1], refs[nm - 1 :]
    qkv_ref, inw_ref, mean_ref, gram_ref, step_ref, sems = refs
    cols = qkv_ref.shape[1]
    copies = run_copies(
        [
            pltpu.make_async_copy(inw_hbm, inw_ref.at[place("tm", nm, 0)], sems.at[0]),
            pltpu.make_async_copy(qkv_hbm.at[:, pl.ds(0, cols)], qkv_ref, sems.at[1]),
        ]
    )
    step_ref[...] = jnp.full(step_ref.shape, weight_ref[0].astype(F32) * (1.0 / STEP_DIVISOR))
    for k in range(1, nm):
        inw_ref[place("tm", nm, k)] = inws[k - 1][...]
    copies[0].wait()
    channels, width = mean_ref.shape[0], inw_ref.shape[2]
    chunks = width // LANES
    total = jnp.zeros((channels, LANES), F32)
    for c in range(chunks):
        total = total + channel_columns(inw_ref, c, 1).astype(F32)
    mean = jnp.sum(total, axis=1, keepdims=True) * (1.0 / width)
    mean_b = jnp.broadcast_to(mean, mean_ref.shape)
    mean_ref[...] = mean_b
    gram = jnp.zeros((channels, channels), F32)
    for c in range(0, chunks, 6):
        piece = channel_columns(inw_ref, c, 6)
        gram = gram + bdot_t(piece, piece)
    mean_c = jnp.broadcast_to(mean, (channels, channels))
    gram = gram * (1.0 / width) - mean_c * mean_c.T
    for i, term in enumerate(split_terms(gram, 3)):
        gram_ref[i * channels : (i + 1) * channels, :] = term
    copies[1].wait()


def attend(x, factors, base, gram, head_count):
    twice = jnp.concatenate([x, x], axis=1)
    thrice = jnp.concatenate([twice, x], axis=1)
    heads = [slice(h * 3 * HD, (h + 1) * 3 * HD) for h in range(head_count)]
    quadratic = bdot(thrice, gram[...])
    raw = [bdot(twice, factors[:, cols]) for cols in heads]
    spread = jnp.sum(quadratic * x.astype(F32), axis=1, keepdims=True)
    scale = lax.rsqrt(jnp.maximum(spread, 0.0) + NORM_EPS)
    qkv = [(r * scale + base[0:1, cols]).astype(BF16) for r, cols in zip(raw, heads)]
    scores = [bdot_t(p[:, :HD], p[:, HD : 2 * HD]) * (1.0 / math.sqrt(HD)) for p in qkv]
    tops = [jnp.max(s, axis=1, keepdims=True) for s in scores]
    weights = [jnp.exp(s - t) for s, t in zip(scores, tops)]
    sums = [jnp.sum(w, axis=1, keepdims=True) for w in weights]
    probs = [(w / n).astype(BF16) for w, n in zip(weights, sums)]
    outs = [bdot(w, p[:, 2 * HD :]).astype(BF16) for w, p in zip(probs, qkv)]
    return outs[0] if head_count == 1 else jnp.concatenate(outs, axis=1)


def setup_kernel(nt, nm, block, *refs):
    msgs, refs = refs[:nt], refs[nt:]
    inw_ref, mean_ref, near_ref, qkv_hbm, out_w_hbm = refs[:5]
    refs = refs[5:]
    factor_ref, base_ref, start_ref, gate_ref, out_w_ref = refs[:5]
    start_s, mod_s, gate_s, z_s, qkv_s, sems = refs[5:]
    near = near_ref.shape[1] // block
    count = factor_ref.shape[1] // block
    copies = run_copies(
        [
            pltpu.make_async_copy(
                qkv_hbm.at[:, pl.ds(n * block, block)],
                qkv_s.at[:, pl.ds((n - near) * block, block)],
                sems.at[n - near],
            )
            for n in range(near, count)
        ]
        + [pltpu.make_async_copy(out_w_hbm, out_w_ref, sems.at[count - near])]
    )
    for k, msg in enumerate(msgs):
        at = place("tensor", nt, k)
        start_s[at] = msg[0 : start_s.shape[1], :]
        mod_s[at, 0 : msg.shape[0] - start_s.shape[1], :] = msg[start_s.shape[1] :, :]
    channels, width = mean_ref.shape[0], z_s.shape[1]
    chunks = width // LANES
    per = 3 * chunks // nt

    def mod_row(r):
        return mod_s[r // per, r % per : r % per + 1, :]

    mean = mean_ref[...]
    first = jnp.zeros((channels + 16, block), F32)
    group = 6
    for g in range(0, chunks, group):
        for c in range(g, g + group):
            cols = slice(c * LANES, (c + 1) * LANES)
            centered = channel_columns(inw_ref, c, 1).astype(F32) - mean
            z_s[0:channels, cols] = (centered * (1.0 + mod_row(chunks + c))).astype(BF16)
            shift = jnp.broadcast_to(mod_row(c), (16, LANES)).astype(BF16)
            z_s[channels : channels + 16, cols] = shift
        cols = slice(g * LANES, (g + group) * LANES)
        first = first + bdot(z_s[:, cols], near_ref[cols, 0:block])

    def keep(result, n):
        at = slice(n * block, (n + 1) * block)
        high, low = split_terms(result[0:channels], 2)
        factor_ref[0:channels, at] = high
        factor_ref[channels : 2 * channels, at] = low
        base_ref[:, at] = result[channels : channels + 8]

    keep(first, 0)
    for p in range(nm):
        for r in range(chunks // nm):
            gate_s[p, r : r + 1, :] = mod_row(2 * chunks + p * (chunks // nm) + r)
        gate_ref[p] = gate_s[p].T
    start_ref[...] = start_s[...].reshape(start_ref.shape)

    for n in range(1, count):
        if n < near:
            weight = near_ref[:, n * block : (n + 1) * block]
        else:
            copies[n - near].wait()
            weight = qkv_s[:, (n - near) * block : (n - near + 1) * block]
        keep(bdot(z_s[...], weight), n)
    copies[count - near].wait()


def fold_parts(nm, first, heads, gate_ref, out_w_ref, inw_ref):
    folded, resid = 0.0, 0.0
    for i, head_ref in enumerate(heads):
        size, _ = head_ref.shape
        at = place("tm", nm, first + i)
        cols = pl.ds(pl.multiple_of(at * size, LANES), size)
        gate = gate_ref[at]
        gated = []
        for r in range(size // LANES):
            rows = head_ref[r * LANES : (r + 1) * LANES, :].astype(F32)
            gated.append((rows * gate[:, r : r + 1]).astype(BF16))
        folded = folded + bdot(out_w_ref[:, cols], jnp.concatenate(gated, axis=0))
        inw = inw_ref[:, :, cols].reshape(-1, size)
        resid = resid + bdot(inw, head_ref[...])
    return folded, resid


def attend_kernel(nm, early, head_count, *refs):
    heads, refs = refs[:early], refs[early:]
    start_ref, factor_ref, base_ref, gram_ref, gate_ref, out_w_ref, inw_ref = refs[:7]
    att_ref, fold_ref, resid_ref = refs[7:]
    x = start_ref[...].astype(BF16)
    fold_ref[...], resid_ref[...] = fold_parts(nm, 0, heads, gate_ref, out_w_ref, inw_ref)
    att_ref[...] = attend(x, factor_ref, base_ref, gram_ref, head_count)


def add_own_rows(result, residual, rows):
    first = lax.axis_index("tensor") * rows
    at = lax.broadcasted_iota(jnp.int32, result.shape, 0)
    return result + jnp.where((at >= first) & (at < first + rows), residual, 0.0)


def fold_kernel(nm, late, rows, *refs):
    heads, refs = refs[:late], refs[late:]
    step_ref, gate_ref, out_w_ref, inw_ref, fold_in, resid_in, att_ref, start_ref = refs[:8]
    fold_ref, resid_ref, vel_ref = refs[8:]
    channels = resid_in.shape[0]
    total, resid = fold_in[...], resid_in[...]
    if late:
        more = fold_parts(nm, nm - late, heads, gate_ref, out_w_ref, inw_ref)
        total, resid = total + more[0], resid + more[1]
    folded = total.astype(BF16)
    fold_ref[...] = folded
    for i, term in enumerate(split_terms(resid, 2)):
        resid_ref[i * channels : (i + 1) * channels, :] = term
    x = start_ref[...].astype(BF16)
    vel = bdot(att_ref[...], folded)
    residual = bdot(jnp.concatenate([x, x], axis=1), resid_ref[...])
    vel_ref[...] = (add_own_rows(vel, residual, rows) * step_ref[0:1, :]).astype(vel_ref.dtype)


def iterate_kernel(nparts, rows, head_count, split, *refs):
    parts, refs = refs[:nparts], refs[nparts:]
    step_ref, start_ref, factor_ref, base_ref, gram_ref, fold_ref, resid_ref = refs[:7]
    outs = refs[7:-1]
    vel_s = refs[-1]
    guess = start_ref[...]
    for part in parts:
        guess = guess + part[...].astype(F32)
    x = guess.astype(BF16)
    attended = attend(x, factor_ref, base_ref, gram_ref, head_count)
    vel = bdot(attended, fold_ref[...])
    residual = bdot(jnp.concatenate([x, x], axis=1), resid_ref[...])
    vel = add_own_rows(vel, residual, rows) * step_ref[0:1, :]
    if not split:
        outs[0][...] = vel.astype(outs[0].dtype)
        return
    vel_s[...] = vel.reshape(vel_s.shape)
    for k in range(len(outs)):
        outs[k][...] = vel_s[lax.axis_index("tensor") ^ k]


def shape_of(shape, dtype):
    return jax.ShapeDtypeStruct(shape, dtype)


def call(kernel, outs, in_specs, scratch, *args, cost=4 * 2**20, limit=8):
    args = [
        pltpu.with_memory_space_constraint(arg, pltpu.HBM) if spec is HBM else arg
        for arg, spec in zip(args, in_specs)
    ]
    return pl.pallas_call(
        kernel,
        out_shape=outs,
        in_specs=in_specs,
        out_specs=[VMEM] * len(outs),
        scratch_shapes=scratch,
        compiler_params=pltpu.CompilerParams(vmem_limit_bytes=limit * 2**20),
        cost_estimate=pl.CostEstimate(flops=0, bytes_accessed=cost, transcendentals=0),
    )(*args)


def sum_earlier(parts, inclusive):
    me = lax.axis_index("tm")
    total = parts[0].astype(F32) if inclusive else jnp.zeros(parts[0].shape, F32)
    for k in range(1, len(parts)):
        total = total + jnp.where((me ^ k) < me, parts[k].astype(F32), 0.0)
    return total


def earlier_sum(value, inclusive):
    if is_small("tm"):
        return sum_earlier(gather_parts(value, "tm"), inclusive)
    everything = lax.all_gather(value, "tm").astype(F32)
    index = jnp.arange(everything.shape[0]).reshape((-1,) + (1,) * value.ndim)
    me = lax.axis_index("tm")
    keep = index <= me if inclusive else index < me
    return jnp.sum(jnp.where(keep, everything, 0.0), axis=0)


def local(
    start_latent,
    time_index,
    step_weight,
    in_weight,
    mod_weight,
    qkv_weight,
    out_weight,
    head_weight,
):
    rows, channels = start_latent.shape
    n_tensor = lax.axis_size("tensor")
    tokens = rows * n_tensor
    width = in_weight.shape[1]
    chunks = width // LANES
    head_count = qkv_weight.shape[1] // (3 * HD)
    span = out_weight.shape[0]

    inw_parts = gather_weight_parts(in_weight, "tm")
    small = is_small("tensor") and mod_weight.shape[1] % LANES == 0
    if small:
        mod_rows = mod_weight.shape[1] // LANES
        message = call(
            modulation_kernel,
            [shape_of((rows + mod_rows, LANES), F32)],
            [SMEM, HBM, HBM],
            [
                pltpu.VMEM(mod_weight.shape, BF16),
                pltpu.VMEM(start_latent.shape, F32),
                pltpu.SemaphoreType.DMA((2,)),
            ],
            time_index,
            mod_weight,
            start_latent,
        )[0]
        messages = gather_parts(message, "tensor")
        block_rows = rows
    else:
        embedding = embedding_of(time_index, mod_weight.shape[0]).astype(BF16)
        mod_part = jnp.dot(embedding, mod_weight, preferred_element_type=F32)
        modulation = lax.all_gather(mod_part, "tensor", axis=1, tiled=True)
        start_all = lax.all_gather(start_latent, "tensor", axis=0, tiled=True)
        messages = [jnp.concatenate([start_all, modulation.reshape(-1, LANES)], axis=0)]
        block_rows = tokens
    nt, nm = len(messages), len(inw_parts)
    mod_rows = messages[0].shape[0] - block_rows
    padded = -(-mod_rows // 8) * 8
    span_cols = qkv_weight.shape[1]
    gate_rows = -(-(chunks // nm) // 8) * 8
    block = 4 * LANES if span_cols % (4 * LANES) == 0 else span_cols
    near = max(1, span_cols // block // 3)
    far = max(1, span_cols // block - near)
    qkv_near, inw_all, mean, gram, step = call(
        functools.partial(load_kernel, nm),
        [
            shape_of((width, near * block), BF16),
            shape_of((nm, channels // nm, width), BF16),
            shape_of((channels, LANES), F32),
            shape_of((3 * channels, channels), BF16),
            shape_of((8, LANES), F32),
        ],
        [SMEM, HBM, HBM] + [VMEM] * (nm - 1),
        [pltpu.SemaphoreType.DMA((2,))],
        step_weight,
        qkv_weight,
        *inw_parts,
        limit=16,
    )
    factor, base, start_all, gate, out_near = call(
        functools.partial(setup_kernel, nt, nm, block),
        [
            shape_of((2 * channels, span_cols), BF16),
            shape_of((8, span_cols), F32),
            shape_of((tokens, channels), F32),
            shape_of((nm, LANES, gate_rows), F32),
            shape_of(out_weight.shape, BF16),
        ],
        [VMEM] * (nt + 3) + [HBM, HBM],
        [
            pltpu.VMEM((nt, block_rows, channels), F32),
            pltpu.VMEM((nt, padded, LANES), F32),
            pltpu.VMEM((nm, gate_rows, LANES), F32),
            pltpu.VMEM((channels + 16, width), BF16),
            pltpu.VMEM((width, far * block), BF16),
            pltpu.SemaphoreType.DMA((far + 1,)),
        ],
        *messages,
        inw_all,
        mean,
        qkv_near,
        qkv_weight,
        out_weight,
        limit=32,
    )
    head_parts = gather_weight_parts(head_weight, "tm")
    late = 1 if nm > 1 else 0
    early = nm - late
    attended, fold_part, resid_part = call(
        functools.partial(attend_kernel, nm, early, head_count),
        [
            shape_of((tokens, head_count * HD), BF16),
            shape_of((span, channels), F32),
            shape_of((channels, channels), F32),
        ],
        [VMEM] * (early + 7),
        [],
        *head_parts[:early],
        start_all,
        factor,
        base,
        gram,
        gate,
        out_near,
        inw_all,
        limit=16,
    )
    folded, resid, vel = call(
        functools.partial(fold_kernel, nm, late, rows),
        [
            shape_of((span, channels), BF16),
            shape_of((2 * channels, channels), BF16),
            shape_of((tokens, channels), BF16),
        ],
        [VMEM] * (late + 8),
        [],
        *head_parts[early:],
        step,
        gate,
        out_near,
        inw_all,
        fold_part,
        resid_part,
        attended,
        start_all,
        limit=16,
    )
    small = is_small("tensor")
    for iteration in range(1, ITERS):
        last = iteration + 1 == ITERS
        hub = lax.axis_size("tm") == 4 and lax.axis_size("tensor") == 4
        earlier = None if hub else earlier_sum(vel, False)
        if hub:
            pieces = [hub_earlier_sum(vel)]
        elif small:
            pieces = gather_parts(earlier.astype(BF16), "tensor")
        else:
            pieces = [lax.psum(earlier, "tensor")]
        split = last and small
        if split:
            outs = [shape_of((rows, channels), F32)] * n_tensor
        else:
            outs = [shape_of((tokens, channels), F32 if last else BF16)]
        vels = call(
            functools.partial(iterate_kernel, len(pieces), rows, head_count, split),
            outs,
            [VMEM] * (len(pieces) + 7),
            [pltpu.VMEM((n_tensor, rows, channels), F32)],
            *pieces,
            step,
            start_all,
            factor,
            base,
            gram,
            folded,
            resid,
        )
        vel = vels[0]
    if small:
        drift = vels[0]
        for k in range(1, n_tensor):
            drift = drift + swap(vels[k], "tensor", k)
    else:
        drift = lax.psum_scatter(vel, "tensor", scatter_dimension=0, tiled=True)
    return (start_latent + earlier_sum(drift, True))[None]


def solution(mesh):
    return jax.shard_map(
        local,
        mesh=mesh,
        in_specs=(
            P(("groups", "tensor"), None),
            P(("groups", "tm")),
            P(("groups", "tm")),
            P("tm", None),
            P(None, "tensor"),
            P(None, "tensor"),
            P("tensor", None),
            P("tm", None),
        ),
        out_specs=P(("groups", "tm"), "tensor", None),
        check_vma=False,
    )
```

```python
import functools
import math

import jax
import jax.numpy as jnp
from jax import lax
from jax.experimental import pallas as pl
from jax.experimental.pallas import tpu as pltpu
from jax.sharding import PartitionSpec as P


HD = 128
LANES = 128
ITERS = 2
NORM_EPS = 1e-06
STEP_DIVISOR = 64.0
F32 = jnp.float32
BF16 = jnp.bfloat16
VMEM = pl.BlockSpec(memory_space=pltpu.VMEM)
SMEM = pl.BlockSpec(memory_space=pltpu.SMEM)
HBM = pl.BlockSpec(memory_space=pltpu.HBM)


def embedding_of(time_index, width):
    half_width = width // 2
    frequency = jnp.exp(
        -math.log(10000.0) * jnp.arange(half_width).astype(F32) / half_width
    )
    angles = time_index.astype(F32)[:, None] * frequency[None, :]
    return jnp.concatenate([jnp.cos(angles), jnp.sin(angles)], axis=1)


def is_small(axis):
    return lax.axis_size(axis) in (2, 4)


def swap(value, axis, k):
    n = lax.axis_size(axis)
    return lax.ppermute(value, axis, [(i, i ^ k) for i in range(n)])


def gather_parts(value, axis):
    if is_small(axis):
        return [value] + [swap(value, axis, k) for k in range(1, lax.axis_size(axis))]
    return [lax.all_gather(value, axis, axis=0, tiled=True)]


def gather_weight_parts(value, axis):
    n = lax.axis_size(axis)
    if n != 4:
        return gather_parts(value, axis)
    far = swap(value, axis, 2)
    near = swap(value, axis, 1)
    return [value, near, far, swap(far, axis, 1)]


def place(axis, parts, k):
    if parts == 1:
        return 0
    return lax.axis_index(axis) ^ k


def bdot(a, b):
    return jnp.dot(a, b, preferred_element_type=F32)


def bdot_t(a, b):
    return lax.dot_general(a, b, (((1,), (1,)), ((), ())), preferred_element_type=F32)


def split_terms(value, terms):
    out = []
    for _ in range(terms):
        piece = value.astype(BF16)
        out.append(piece)
        value = value - piece.astype(F32)
    return out


def run_copies(copies):
    for copy in copies:
        copy.start()
    return copies


def wait_copies(copies):
    for copy in copies:
        copy.wait()


def modulation_kernel(
    time_ref, weight_hbm, start_hbm, qkv_hbm, inw_hbm, out_ref, qkv_ref, inw_ref, weight_ref, start_ref, sems
):
    rows = start_ref.shape[0]
    half = weight_ref.shape[0] // 2
    pairs = (
        (weight_hbm, weight_ref),
        (start_hbm, start_ref),
        (inw_hbm, inw_ref),
        (qkv_hbm.at[:, pl.ds(0, qkv_ref.shape[1])], qkv_ref),
    )
    copies = run_copies(
        [pltpu.make_async_copy(a, b, sems.at[i]) for i, (a, b) in enumerate(pairs)]
    )
    index = lax.broadcasted_iota(jnp.int32, (16, half), 1).astype(F32)
    angles = time_ref[0].astype(F32) * jnp.exp(-math.log(10000.0) * index / half)
    embedding = jnp.concatenate([jnp.cos(angles), jnp.sin(angles)], axis=1).astype(BF16)
    wait_copies(copies[:2])
    result = bdot(embedding, weight_ref[...])
    out_ref[0:rows, :] = start_ref[...]
    for r in range(weight_ref.shape[1] // LANES):
        out_ref[rows + r : rows + r + 1, :] = result[0:1, r * LANES : (r + 1) * LANES]
    wait_copies(copies[2:])


def channel_columns(inw_ref, c, n):
    return inw_ref[:, :, c * LANES : (c + n) * LANES].reshape(-1, n * LANES)


def prepare_kernel(nm, weight_ref, *refs):
    inws, refs = refs[:nm], refs[nm:]
    inw_ref, mean_ref, gram_ref, step_ref = refs
    step_ref[...] = jnp.full(step_ref.shape, weight_ref[0].astype(F32) * (1.0 / STEP_DIVISOR))
    for k in range(nm):
        inw_ref[place("tm", nm, k)] = inws[k][...]
    channels, width = mean_ref.shape[0], inw_ref.shape[2]
    chunks = width // LANES
    total = jnp.zeros((channels, LANES), F32)
    for c in range(chunks):
        total = total + channel_columns(inw_ref, c, 1).astype(F32)
    mean = jnp.sum(total, axis=1, keepdims=True) * (1.0 / width)
    mean_b = jnp.broadcast_to(mean, mean_ref.shape)
    mean_ref[...] = mean_b
    gram = jnp.zeros((channels, channels), F32)
    for c in range(0, chunks, 6):
        piece = channel_columns(inw_ref, c, 6)
        gram = gram + bdot_t(piece, piece)
    mean_c = jnp.broadcast_to(mean, (channels, channels))
    gram = gram * (1.0 / width) - mean_c * mean_c.T
    for i, term in enumerate(split_terms(gram, 3)):
        gram_ref[i * channels : (i + 1) * channels, :] = term


def attend(x, factors, base, gram, head_count):
    twice = jnp.concatenate([x, x], axis=1)
    thrice = jnp.concatenate([twice, x], axis=1)
    heads = [slice(h * 3 * HD, (h + 1) * 3 * HD) for h in range(head_count)]
    quadratic = bdot(thrice, gram[...])
    raw = [bdot(twice, factors[:, cols]) for cols in heads]
    spread = jnp.sum(quadratic * x.astype(F32), axis=1, keepdims=True)
    scale = lax.rsqrt(jnp.maximum(spread, 0.0) + NORM_EPS)
    qkv = [(r * scale + base[0:1, cols]).astype(BF16) for r, cols in zip(raw, heads)]
    scores = [bdot_t(p[:, :HD], p[:, HD : 2 * HD]) * (1.0 / math.sqrt(HD)) for p in qkv]
    tops = [jnp.max(s, axis=1, keepdims=True) for s in scores]
    weights = [jnp.exp(s - t) for s, t in zip(scores, tops)]
    sums = [jnp.sum(w, axis=1, keepdims=True) for w in weights]
    probs = [(w / n).astype(BF16) for w, n in zip(weights, sums)]
    outs = [bdot(w, p[:, 2 * HD :]).astype(BF16) for w, p in zip(probs, qkv)]
    return outs[0] if head_count == 1 else jnp.concatenate(outs, axis=1)


def setup_kernel(nt, nm, block, *refs):
    msgs, refs = refs[:nt], refs[nt:]
    inw_ref, mean_ref, near_ref, qkv_hbm, out_w_hbm = refs[:5]
    refs = refs[5:]
    factor_ref, base_ref, start_ref, gate_ref, out_w_ref = refs[:5]
    start_s, mod_s, gate_s, z_s, qkv_s, sems = refs[5:]
    near = near_ref.shape[1] // block
    count = factor_ref.shape[1] // block
    copies = run_copies(
        [
            pltpu.make_async_copy(
                qkv_hbm.at[:, pl.ds(n * block, block)],
                qkv_s.at[:, pl.ds((n - near) * block, block)],
                sems.at[n - near],
            )
            for n in range(near, count)
        ]
        + [pltpu.make_async_copy(out_w_hbm, out_w_ref, sems.at[count - near])]
    )
    for k, msg in enumerate(msgs):
        at = place("tensor", nt, k)
        start_s[at] = msg[0 : start_s.shape[1], :]
        mod_s[at, 0 : msg.shape[0] - start_s.shape[1], :] = msg[start_s.shape[1] :, :]
    channels, width = mean_ref.shape[0], z_s.shape[1]
    chunks = width // LANES
    per = 3 * chunks // nt

    def mod_row(r):
        return mod_s[r // per, r % per : r % per + 1, :]

    mean = mean_ref[...]
    first = jnp.zeros((channels + 16, block), F32)
    group = 6
    for g in range(0, chunks, group):
        for c in range(g, g + group):
            cols = slice(c * LANES, (c + 1) * LANES)
            centered = channel_columns(inw_ref, c, 1).astype(F32) - mean
            z_s[0:channels, cols] = (centered * (1.0 + mod_row(chunks + c))).astype(BF16)
            shift = jnp.broadcast_to(mod_row(c), (16, LANES)).astype(BF16)
            z_s[channels : channels + 16, cols] = shift
        cols = slice(g * LANES, (g + group) * LANES)
        first = first + bdot(z_s[:, cols], near_ref[cols, 0:block])

    def keep(result, n):
        at = slice(n * block, (n + 1) * block)
        high, low = split_terms(result[0:channels], 2)
        factor_ref[0:channels, at] = high
        factor_ref[channels : 2 * channels, at] = low
        base_ref[:, at] = result[channels : channels + 8]

    keep(first, 0)
    for p in range(nm):
        for r in range(chunks // nm):
            gate_s[p, r : r + 1, :] = mod_row(2 * chunks + p * (chunks // nm) + r)
        gate_ref[p] = gate_s[p].T
    start_ref[...] = start_s[...].reshape(start_ref.shape)

    for n in range(1, count):
        if n < near:
            weight = near_ref[:, n * block : (n + 1) * block]
        else:
            copies[n - near].wait()
            weight = qkv_s[:, (n - near) * block : (n - near + 1) * block]
        keep(bdot(z_s[...], weight), n)
    copies[count - near].wait()


def fold_parts(nm, first, heads, gate_ref, out_w_ref, inw_ref):
    folded, resid = 0.0, 0.0
    for i, head_ref in enumerate(heads):
        size, _ = head_ref.shape
        at = place("tm", nm, first + i)
        cols = pl.ds(pl.multiple_of(at * size, LANES), size)
        gate = gate_ref[at]
        gated = []
        for r in range(size // LANES):
            rows = head_ref[r * LANES : (r + 1) * LANES, :].astype(F32)
            gated.append((rows * gate[:, r : r + 1]).astype(BF16))
        folded = folded + bdot(out_w_ref[:, cols], jnp.concatenate(gated, axis=0))
        inw = inw_ref[:, :, cols].reshape(-1, size)
        resid = resid + bdot(inw, head_ref[...])
    return folded, resid


def add_own_rows(result, residual, rows):
    first = lax.axis_index("tensor") * rows
    at = lax.broadcasted_iota(jnp.int32, result.shape, 0)
    return result + jnp.where((at >= first) & (at < first + rows), residual, 0.0)


def first_kernel(nm, rows, head_count, *refs):
    heads, refs = refs[:nm], refs[nm:]
    step_ref, start_ref, factor_ref, base_ref, gram_ref, gate_ref, out_w_ref, inw_ref = refs[:8]
    fold_ref, resid_ref, vel_ref = refs[8:]
    x = start_ref[...].astype(BF16)
    total, resid = fold_parts(nm, 0, heads, gate_ref, out_w_ref, inw_ref)
    attended = attend(x, factor_ref, base_ref, gram_ref, head_count)
    channels = resid.shape[0]
    folded = total.astype(BF16)
    fold_ref[...] = folded
    for i, term in enumerate(split_terms(resid, 2)):
        resid_ref[i * channels : (i + 1) * channels, :] = term
    vel = bdot(attended, folded)
    residual = bdot(jnp.concatenate([x, x], axis=1), resid_ref[...])
    vel_ref[...] = (add_own_rows(vel, residual, rows) * step_ref[0:1, :]).astype(vel_ref.dtype)


def iterate_kernel(nparts, rows, head_count, split, *refs):
    parts, refs = refs[:nparts], refs[nparts:]
    step_ref, start_ref, factor_ref, base_ref, gram_ref, fold_ref, resid_ref = refs[:7]
    outs = refs[7:-1]
    vel_s = refs[-1]
    guess = start_ref[...]
    for part in parts:
        guess = guess + part[...].astype(F32)
    x = guess.astype(BF16)
    attended = attend(x, factor_ref, base_ref, gram_ref, head_count)
    vel = bdot(attended, fold_ref[...])
    residual = bdot(jnp.concatenate([x, x], axis=1), resid_ref[...])
    vel = add_own_rows(vel, residual, rows) * step_ref[0:1, :]
    if not split:
        outs[0][...] = vel.astype(outs[0].dtype)
        return
    vel_s[...] = vel.reshape(vel_s.shape)
    for k in range(len(outs)):
        outs[k][...] = vel_s[lax.axis_index("tensor") ^ k]


def shape_of(shape, dtype):
    return jax.ShapeDtypeStruct(shape, dtype)


def call(kernel, outs, in_specs, scratch, *args, cost=4 * 2**20, limit=8):
    args = [
        pltpu.with_memory_space_constraint(arg, pltpu.HBM) if spec is HBM else arg
        for arg, spec in zip(args, in_specs)
    ]
    return pl.pallas_call(
        kernel,
        out_shape=outs,
        in_specs=in_specs,
        out_specs=[VMEM] * len(outs),
        scratch_shapes=scratch,
        compiler_params=pltpu.CompilerParams(vmem_limit_bytes=limit * 2**20),
        cost_estimate=pl.CostEstimate(flops=0, bytes_accessed=cost, transcendentals=0),
    )(*args)


def sum_earlier(parts, inclusive):
    me = lax.axis_index("tm")
    total = parts[0].astype(F32) if inclusive else jnp.zeros(parts[0].shape, F32)
    for k in range(1, len(parts)):
        total = total + jnp.where((me ^ k) < me, parts[k].astype(F32), 0.0)
    return total


def earlier_sum(value, inclusive):
    if is_small("tm"):
        return sum_earlier(gather_parts(value, "tm"), inclusive)
    everything = lax.all_gather(value, "tm").astype(F32)
    index = jnp.arange(everything.shape[0]).reshape((-1,) + (1,) * value.ndim)
    me = lax.axis_index("tm")
    keep = index <= me if inclusive else index < me
    return jnp.sum(jnp.where(keep, everything, 0.0), axis=0)


def local(
    start_latent,
    time_index,
    step_weight,
    in_weight,
    mod_weight,
    qkv_weight,
    out_weight,
    head_weight,
):
    rows, channels = start_latent.shape
    n_tensor = lax.axis_size("tensor")
    tokens = rows * n_tensor
    width = in_weight.shape[1]
    chunks = width // LANES
    head_count = qkv_weight.shape[1] // (3 * HD)
    span = out_weight.shape[0]

    inw_parts = gather_weight_parts(in_weight, "tm")
    span_cols = qkv_weight.shape[1]
    block = 4 * LANES if span_cols % (4 * LANES) == 0 else span_cols
    near = max(1, span_cols // block // 3)
    far = max(1, span_cols // block - near)
    small = is_small("tensor") and mod_weight.shape[1] % LANES == 0
    if small:
        mod_rows = mod_weight.shape[1] // LANES
        message, qkv_near, inw_parts[0] = call(
            modulation_kernel,
            [
                shape_of((rows + mod_rows, LANES), F32),
                shape_of((width, near * block), BF16),
                shape_of(inw_parts[0].shape, BF16),
            ],
            [SMEM, HBM, HBM, HBM, HBM],
            [
                pltpu.VMEM(mod_weight.shape, BF16),
                pltpu.VMEM(start_latent.shape, F32),
                pltpu.SemaphoreType.DMA((4,)),
            ],
            time_index,
            mod_weight,
            start_latent,
            qkv_weight,
            inw_parts[0],
        )
        messages = gather_parts(message, "tensor")
        block_rows = rows
    else:
        embedding = embedding_of(time_index, mod_weight.shape[0]).astype(BF16)
        qkv_near = qkv_weight[:, : near * block]
        mod_part = jnp.dot(embedding, mod_weight, preferred_element_type=F32)
        modulation = lax.all_gather(mod_part, "tensor", axis=1, tiled=True)
        start_all = lax.all_gather(start_latent, "tensor", axis=0, tiled=True)
        messages = [jnp.concatenate([start_all, modulation.reshape(-1, LANES)], axis=0)]
        block_rows = tokens
    nt, nm = len(messages), len(inw_parts)
    mod_rows = messages[0].shape[0] - block_rows
    padded = -(-mod_rows // 8) * 8
    gate_rows = -(-(chunks // nm) // 8) * 8
    inw_all, mean, gram, step = call(
        functools.partial(prepare_kernel, nm),
        [
            shape_of((nm, channels // nm, width), BF16),
            shape_of((channels, LANES), F32),
            shape_of((3 * channels, channels), BF16),
            shape_of((8, LANES), F32),
        ],
        [SMEM] + [VMEM] * nm,
        [],
        step_weight,
        *inw_parts,
        limit=16,
    )
    factor, base, start_all, gate, out_near = call(
        functools.partial(setup_kernel, nt, nm, block),
        [
            shape_of((2 * channels, span_cols), BF16),
            shape_of((8, span_cols), F32),
            shape_of((tokens, channels), F32),
            shape_of((nm, LANES, gate_rows), F32),
            shape_of(out_weight.shape, BF16),
        ],
        [VMEM] * (nt + 3) + [HBM, HBM],
        [
            pltpu.VMEM((nt, block_rows, channels), F32),
            pltpu.VMEM((nt, padded, LANES), F32),
            pltpu.VMEM((nm, gate_rows, LANES), F32),
            pltpu.VMEM((channels + 16, width), BF16),
            pltpu.VMEM((width, far * block), BF16),
            pltpu.SemaphoreType.DMA((far + 1,)),
        ],
        *messages,
        inw_all,
        mean,
        qkv_near,
        qkv_weight,
        out_weight,
        limit=32,
    )
    head_parts = gather_weight_parts(head_weight, "tm")
    folded, resid, vel = call(
        functools.partial(first_kernel, nm, rows, head_count),
        [
            shape_of((span, channels), BF16),
            shape_of((2 * channels, channels), BF16),
            shape_of((tokens, channels), BF16),
        ],
        [VMEM] * (nm + 8),
        [],
        *head_parts,
        step,
        start_all,
        factor,
        base,
        gram,
        gate,
        out_near,
        inw_all,
        limit=16,
    )
    small = is_small("tensor")
    for iteration in range(1, ITERS):
        last = iteration + 1 == ITERS
        earlier = earlier_sum(vel, False)
        if small:
            pieces = gather_parts(earlier.astype(BF16), "tensor")
        else:
            pieces = [lax.psum(earlier, "tensor")]
        split = last and small
        if split:
            outs = [shape_of((rows, channels), F32)] * n_tensor
        else:
            outs = [shape_of((tokens, channels), F32 if last else BF16)]
        vels = call(
            functools.partial(iterate_kernel, len(pieces), rows, head_count, split),
            outs,
            [VMEM] * (len(pieces) + 7),
            [pltpu.VMEM((n_tensor, rows, channels), F32)],
            *pieces,
            step,
            start_all,
            factor,
            base,
            gram,
            folded,
            resid,
        )
        vel = vels[0]
    if small:
        drift = vels[0]
        for k in range(1, n_tensor):
            drift = drift + swap(vels[k], "tensor", k)
    else:
        drift = lax.psum_scatter(vel, "tensor", scatter_dimension=0, tiled=True)
    return (start_latent + earlier_sum(drift, True))[None]


def solution(mesh):
    return jax.shard_map(
        local,
        mesh=mesh,
        in_specs=(
            P(("groups", "tensor"), None),
            P(("groups", "tm")),
            P(("groups", "tm")),
            P("tm", None),
            P(None, "tensor"),
            P(None, "tensor"),
            P("tensor", None),
            P("tm", None),
        ),
        out_specs=P(("groups", "tm"), "tensor", None),
        check_vma=False,
    )
```

```python
import functools
import math

import jax
import jax.numpy as jnp
from jax import lax
from jax.experimental import pallas as pl
from jax.experimental.pallas import tpu as pltpu
from jax.sharding import PartitionSpec as P


HD = 128
LANES = 128
ITERS = 2
NORM_EPS = 1e-06
STEP_DIVISOR = 64.0
F32 = jnp.float32
BF16 = jnp.bfloat16
VMEM = pl.BlockSpec(memory_space=pltpu.VMEM)
SMEM = pl.BlockSpec(memory_space=pltpu.SMEM)
HBM = pl.BlockSpec(memory_space=pltpu.HBM)


def embedding_of(time_index, width):
    half_width = width // 2
    frequency = jnp.exp(
        -math.log(10000.0) * jnp.arange(half_width).astype(F32) / half_width
    )
    angles = time_index.astype(F32)[:, None] * frequency[None, :]
    return jnp.concatenate([jnp.cos(angles), jnp.sin(angles)], axis=1)


def is_small(axis):
    return lax.axis_size(axis) in (2, 4)


def swap(value, axis, k):
    n = lax.axis_size(axis)
    return lax.ppermute(value, axis, [(i, i ^ k) for i in range(n)])


def gather_parts(value, axis):
    if is_small(axis):
        return [value] + [swap(value, axis, k) for k in range(1, lax.axis_size(axis))]
    return [lax.all_gather(value, axis, axis=0, tiled=True)]


def gather_weight_parts(value, axis):
    n = lax.axis_size(axis)
    if n != 4:
        return gather_parts(value, axis)
    far = swap(value, axis, 2)
    near = swap(value, axis, 1)
    return [value, near, far, swap(far, axis, 1)]


def place(axis, parts, k):
    if parts == 1:
        return 0
    return lax.axis_index(axis) ^ k


def bdot(a, b):
    return jnp.dot(a, b, preferred_element_type=F32)


def bdot_t(a, b):
    return lax.dot_general(a, b, (((1,), (1,)), ((), ())), preferred_element_type=F32)


def split_terms(value, terms):
    out = []
    for _ in range(terms):
        piece = value.astype(BF16)
        out.append(piece)
        value = value - piece.astype(F32)
    return out


def run_copies(copies):
    for copy in copies:
        copy.start()
    return copies


def wait_copies(copies):
    for copy in copies:
        copy.wait()


def modulation_kernel(
    time_ref, weight_hbm, start_hbm, qkv_hbm, inw_hbm, out_ref, qkv_ref, inw_ref, weight_ref, start_ref, out_s, sems
):
    rows = start_ref.shape[0]
    half = weight_ref.shape[0] // 2
    pairs = (
        (weight_hbm, weight_ref),
        (start_hbm, start_ref),
        (inw_hbm, inw_ref),
        (qkv_hbm.at[:, pl.ds(0, qkv_ref.shape[1])], qkv_ref),
    )
    copies = run_copies(
        [pltpu.make_async_copy(a, b, sems.at[i]) for i, (a, b) in enumerate(pairs)]
    )
    index = lax.broadcasted_iota(jnp.int32, (16, half), 1).astype(F32)
    angles = time_ref[0].astype(F32) * jnp.exp(-math.log(10000.0) * index / half)
    embedding = jnp.concatenate([jnp.cos(angles), jnp.sin(angles)], axis=1).astype(BF16)
    wait_copies(copies[:2])
    result = bdot(embedding, weight_ref[...])
    out_s[0:rows, :] = start_ref[...]
    for r in range(weight_ref.shape[1] // LANES):
        out_s[rows + r : rows + r + 1, :] = result[0:1, r * LANES : (r + 1) * LANES]
    out_ref[...] = out_s[...].astype(BF16)
    wait_copies(copies[2:])


def channel_columns(inw_ref, c, n):
    return inw_ref[:, :, c * LANES : (c + n) * LANES].reshape(-1, n * LANES)


def prepare_kernel(nm, weight_ref, *refs):
    inws, refs = refs[:nm], refs[nm:]
    inw_ref, mean_ref, gram_ref, step_ref = refs
    step_ref[...] = jnp.full(step_ref.shape, weight_ref[0].astype(F32) * (1.0 / STEP_DIVISOR))
    for k in range(nm):
        inw_ref[place("tm", nm, k)] = inws[k][...]
    channels, width = mean_ref.shape[0], inw_ref.shape[2]
    chunks = width // LANES
    total = jnp.zeros((channels, LANES), F32)
    for c in range(chunks):
        total = total + channel_columns(inw_ref, c, 1).astype(F32)
    mean = jnp.sum(total, axis=1, keepdims=True) * (1.0 / width)
    mean_b = jnp.broadcast_to(mean, mean_ref.shape)
    mean_ref[...] = mean_b
    gram = jnp.zeros((channels, channels), F32)
    for c in range(0, chunks, 6):
        piece = channel_columns(inw_ref, c, 6)
        gram = gram + bdot_t(piece, piece)
    mean_c = jnp.broadcast_to(mean, (channels, channels))
    gram = gram * (1.0 / width) - mean_c * mean_c.T
    for i, term in enumerate(split_terms(gram, 3)):
        gram_ref[i * channels : (i + 1) * channels, :] = term


def attend(x, factors, base, gram, head_count):
    twice = jnp.concatenate([x, x], axis=1)
    thrice = jnp.concatenate([twice, x], axis=1)
    heads = [slice(h * 3 * HD, (h + 1) * 3 * HD) for h in range(head_count)]
    quadratic = bdot(thrice, gram[...])
    raw = [bdot(twice, factors[:, cols]) for cols in heads]
    spread = jnp.sum(quadratic * x.astype(F32), axis=1, keepdims=True)
    scale = lax.rsqrt(jnp.maximum(spread, 0.0) + NORM_EPS)
    qkv = [(r * scale + base[0:1, cols]).astype(BF16) for r, cols in zip(raw, heads)]
    scores = [bdot_t(p[:, :HD], p[:, HD : 2 * HD]) * (1.0 / math.sqrt(HD)) for p in qkv]
    tops = [jnp.max(s, axis=1, keepdims=True) for s in scores]
    weights = [jnp.exp(s - t) for s, t in zip(scores, tops)]
    sums = [jnp.sum(w, axis=1, keepdims=True) for w in weights]
    probs = [(w / n).astype(BF16) for w, n in zip(weights, sums)]
    outs = [bdot(w, p[:, 2 * HD :]).astype(BF16) for w, p in zip(probs, qkv)]
    return outs[0] if head_count == 1 else jnp.concatenate(outs, axis=1)


def setup_kernel(nt, nm, block, *refs):
    msgs, refs = refs[:nt], refs[nt:]
    inw_ref, mean_ref, near_ref, qkv_hbm, out_w_hbm = refs[:5]
    refs = refs[5:]
    factor_ref, base_ref, start_ref, gate_ref, out_w_ref = refs[:5]
    start_s, mod_s, gate_s, z_s, qkv_s, sems = refs[5:]
    near = near_ref.shape[1] // block
    count = factor_ref.shape[1] // block
    copies = run_copies(
        [
            pltpu.make_async_copy(
                qkv_hbm.at[:, pl.ds(n * block, block)],
                qkv_s.at[:, pl.ds((n - near) * block, block)],
                sems.at[n - near],
            )
            for n in range(near, count)
        ]
        + [pltpu.make_async_copy(out_w_hbm, out_w_ref, sems.at[count - near])]
    )
    for k, msg in enumerate(msgs):
        at = place("tensor", nt, k)
        start_s[at] = msg[0 : start_s.shape[1], :].astype(F32)
        mod_s[at, 0 : msg.shape[0] - start_s.shape[1], :] = msg[start_s.shape[1] :, :].astype(F32)
    channels, width = mean_ref.shape[0], z_s.shape[1]
    chunks = width // LANES
    per = 3 * chunks // nt

    def mod_row(r):
        return mod_s[r // per, r % per : r % per + 1, :]

    mean = mean_ref[...]
    first = jnp.zeros((channels + 16, block), F32)
    group = 6
    for g in range(0, chunks, group):
        for c in range(g, g + group):
            cols = slice(c * LANES, (c + 1) * LANES)
            centered = channel_columns(inw_ref, c, 1).astype(F32) - mean
            z_s[0:channels, cols] = (centered * (1.0 + mod_row(chunks + c))).astype(BF16)
            shift = jnp.broadcast_to(mod_row(c), (16, LANES)).astype(BF16)
            z_s[channels : channels + 16, cols] = shift
        cols = slice(g * LANES, (g + group) * LANES)
        first = first + bdot(z_s[:, cols], near_ref[cols, 0:block])

    def keep(result, n):
        at = slice(n * block, (n + 1) * block)
        high, low = split_terms(result[0:channels], 2)
        factor_ref[0:channels, at] = high
        factor_ref[channels : 2 * channels, at] = low
        base_ref[:, at] = result[channels : channels + 8]

    keep(first, 0)
    for p in range(nm):
        for r in range(chunks // nm):
            gate_s[p, r : r + 1, :] = mod_row(2 * chunks + p * (chunks // nm) + r)
        gate_ref[p] = gate_s[p].T
    start_ref[...] = start_s[...].reshape(start_ref.shape)

    for n in range(1, count):
        if n < near:
            weight = near_ref[:, n * block : (n + 1) * block]
        else:
            copies[n - near].wait()
            weight = qkv_s[:, (n - near) * block : (n - near + 1) * block]
        keep(bdot(z_s[...], weight), n)
    copies[count - near].wait()


def fold_parts(nm, first, heads, gate_ref, out_w_ref, inw_ref):
    folded, resid = 0.0, 0.0
    for i, head_ref in enumerate(heads):
        size, _ = head_ref.shape
        at = place("tm", nm, first + i)
        cols = pl.ds(pl.multiple_of(at * size, LANES), size)
        gate = gate_ref[at]
        gated = []
        for r in range(size // LANES):
            rows = head_ref[r * LANES : (r + 1) * LANES, :].astype(F32)
            gated.append((rows * gate[:, r : r + 1]).astype(BF16))
        folded = folded + bdot(out_w_ref[:, cols], jnp.concatenate(gated, axis=0))
        inw = inw_ref[:, :, cols].reshape(-1, size)
        resid = resid + bdot(inw, head_ref[...])
    return folded, resid


def attend_kernel(nm, early, head_count, *refs):
    heads, refs = refs[:early], refs[early:]
    start_ref, factor_ref, base_ref, gram_ref, gate_ref, out_w_ref, inw_ref = refs[:7]
    att_ref, fold_ref, resid_ref = refs[7:]
    x = start_ref[...].astype(BF16)
    fold_ref[...], resid_ref[...] = fold_parts(nm, 0, heads, gate_ref, out_w_ref, inw_ref)
    att_ref[...] = attend(x, factor_ref, base_ref, gram_ref, head_count)


def add_own_rows(result, residual, rows):
    first = lax.axis_index("tensor") * rows
    at = lax.broadcasted_iota(jnp.int32, result.shape, 0)
    return result + jnp.where((at >= first) & (at < first + rows), residual, 0.0)


def fold_kernel(nm, late, rows, *refs):
    heads, refs = refs[:late], refs[late:]
    step_ref, gate_ref, out_w_ref, inw_ref, fold_in, resid_in, att_ref, start_ref = refs[:8]
    fold_ref, resid_ref, vel_ref = refs[8:]
    channels = resid_in.shape[0]
    total, resid = fold_in[...], resid_in[...]
    if late:
        more = fold_parts(nm, nm - late, heads, gate_ref, out_w_ref, inw_ref)
        total, resid = total + more[0], resid + more[1]
    folded = total.astype(BF16)
    fold_ref[...] = folded
    for i, term in enumerate(split_terms(resid, 2)):
        resid_ref[i * channels : (i + 1) * channels, :] = term
    x = start_ref[...].astype(BF16)
    vel = bdot(att_ref[...], folded)
    residual = bdot(jnp.concatenate([x, x], axis=1), resid_ref[...])
    vel_ref[...] = (add_own_rows(vel, residual, rows) * step_ref[0:1, :]).astype(vel_ref.dtype)


def iterate_kernel(nparts, rows, head_count, split, *refs):
    parts, refs = refs[:nparts], refs[nparts:]
    step_ref, start_ref, factor_ref, base_ref, gram_ref, fold_ref, resid_ref = refs[:7]
    outs = refs[7:-1]
    vel_s = refs[-1]
    guess = start_ref[...]
    for part in parts:
        guess = guess + part[...].astype(F32)
    x = guess.astype(BF16)
    attended = attend(x, factor_ref, base_ref, gram_ref, head_count)
    vel = bdot(attended, fold_ref[...])
    residual = bdot(jnp.concatenate([x, x], axis=1), resid_ref[...])
    vel = add_own_rows(vel, residual, rows) * step_ref[0:1, :]
    if not split:
        outs[0][...] = vel.astype(outs[0].dtype)
        return
    vel_s[...] = vel.reshape(vel_s.shape)
    for k in range(len(outs)):
        outs[k][...] = vel_s[lax.axis_index("tensor") ^ k].astype(outs[k].dtype)


def shape_of(shape, dtype):
    return jax.ShapeDtypeStruct(shape, dtype)


def call(kernel, outs, in_specs, scratch, *args, cost=4 * 2**20, limit=8):
    args = [
        pltpu.with_memory_space_constraint(arg, pltpu.HBM) if spec is HBM else arg
        for arg, spec in zip(args, in_specs)
    ]
    return pl.pallas_call(
        kernel,
        out_shape=outs,
        in_specs=in_specs,
        out_specs=[VMEM] * len(outs),
        scratch_shapes=scratch,
        compiler_params=pltpu.CompilerParams(vmem_limit_bytes=limit * 2**20),
        cost_estimate=pl.CostEstimate(flops=0, bytes_accessed=cost, transcendentals=0),
    )(*args)


def sum_earlier(parts, inclusive):
    me = lax.axis_index("tm")
    total = parts[0].astype(F32) if inclusive else jnp.zeros(parts[0].shape, F32)
    for k in range(1, len(parts)):
        total = total + jnp.where((me ^ k) < me, parts[k].astype(F32), 0.0)
    return total


def earlier_sum(value, inclusive):
    if is_small("tm"):
        parts = gather_parts(value.astype(BF16), "tm")
        return sum_earlier([value] + parts[1:], inclusive)
    everything = lax.all_gather(value, "tm").astype(F32)
    index = jnp.arange(everything.shape[0]).reshape((-1,) + (1,) * value.ndim)
    me = lax.axis_index("tm")
    keep = index <= me if inclusive else index < me
    return jnp.sum(jnp.where(keep, everything, 0.0), axis=0)


def local(
    start_latent,
    time_index,
    step_weight,
    in_weight,
    mod_weight,
    qkv_weight,
    out_weight,
    head_weight,
):
    rows, channels = start_latent.shape
    n_tensor = lax.axis_size("tensor")
    tokens = rows * n_tensor
    width = in_weight.shape[1]
    chunks = width // LANES
    head_count = qkv_weight.shape[1] // (3 * HD)
    span = out_weight.shape[0]

    inw_parts = gather_weight_parts(in_weight, "tm")
    span_cols = qkv_weight.shape[1]
    block = 4 * LANES if span_cols % (4 * LANES) == 0 else span_cols
    near = max(1, span_cols // block // 3)
    far = max(1, span_cols // block - near)
    small = is_small("tensor") and mod_weight.shape[1] % LANES == 0
    if small:
        mod_rows = mod_weight.shape[1] // LANES
        message, qkv_near, inw_parts[0] = call(
            modulation_kernel,
            [
                shape_of((rows + mod_rows, LANES), BF16),
                shape_of((width, near * block), BF16),
                shape_of(inw_parts[0].shape, BF16),
            ],
            [SMEM, HBM, HBM, HBM, HBM],
            [
                pltpu.VMEM(mod_weight.shape, BF16),
                pltpu.VMEM(start_latent.shape, F32),
                pltpu.VMEM((rows + mod_rows, LANES), F32),
                pltpu.SemaphoreType.DMA((4,)),
            ],
            time_index,
            mod_weight,
            start_latent,
            qkv_weight,
            inw_parts[0],
        )
        messages = gather_parts(message, "tensor")
        block_rows = rows
    else:
        embedding = embedding_of(time_index, mod_weight.shape[0]).astype(BF16)
        qkv_near = qkv_weight[:, : near * block]
        mod_part = jnp.dot(embedding, mod_weight, preferred_element_type=F32)
        modulation = lax.all_gather(mod_part, "tensor", axis=1, tiled=True)
        start_all = lax.all_gather(start_latent, "tensor", axis=0, tiled=True)
        messages = [jnp.concatenate([start_all, modulation.reshape(-1, LANES)], axis=0)]
        block_rows = tokens
    nt, nm = len(messages), len(inw_parts)
    mod_rows = messages[0].shape[0] - block_rows
    padded = -(-mod_rows // 8) * 8
    gate_rows = -(-(chunks // nm) // 8) * 8
    inw_all, mean, gram, step = call(
        functools.partial(prepare_kernel, nm),
        [
            shape_of((nm, channels // nm, width), BF16),
            shape_of((channels, LANES), F32),
            shape_of((3 * channels, channels), BF16),
            shape_of((8, LANES), F32),
        ],
        [SMEM] + [VMEM] * nm,
        [],
        step_weight,
        *inw_parts,
        limit=16,
    )
    factor, base, start_all, gate, out_near = call(
        functools.partial(setup_kernel, nt, nm, block),
        [
            shape_of((2 * channels, span_cols), BF16),
            shape_of((8, span_cols), F32),
            shape_of((tokens, channels), F32),
            shape_of((nm, LANES, gate_rows), F32),
            shape_of(out_weight.shape, BF16),
        ],
        [VMEM] * (nt + 3) + [HBM, HBM],
        [
            pltpu.VMEM((nt, block_rows, channels), F32),
            pltpu.VMEM((nt, padded, LANES), F32),
            pltpu.VMEM((nm, gate_rows, LANES), F32),
            pltpu.VMEM((channels + 16, width), BF16),
            pltpu.VMEM((width, far * block), BF16),
            pltpu.SemaphoreType.DMA((far + 1,)),
        ],
        *messages,
        inw_all,
        mean,
        qkv_near,
        qkv_weight,
        out_weight,
        limit=32,
    )
    head_parts = gather_weight_parts(head_weight, "tm")
    late = 1 if nm > 1 else 0
    early = nm - late
    attended, fold_part, resid_part = call(
        functools.partial(attend_kernel, nm, early, head_count),
        [
            shape_of((tokens, head_count * HD), BF16),
            shape_of((span, channels), F32),
            shape_of((channels, channels), F32),
        ],
        [VMEM] * (early + 7),
        [],
        *head_parts[:early],
        start_all,
        factor,
        base,
        gram,
        gate,
        out_near,
        inw_all,
        limit=16,
    )
    folded, resid, vel = call(
        functools.partial(fold_kernel, nm, late, rows),
        [
            shape_of((span, channels), BF16),
            shape_of((2 * channels, channels), BF16),
            shape_of((tokens, channels), BF16),
        ],
        [VMEM] * (late + 8),
        [],
        *head_parts[early:],
        step,
        gate,
        out_near,
        inw_all,
        fold_part,
        resid_part,
        attended,
        start_all,
        limit=16,
    )
    small = is_small("tensor")
    for iteration in range(1, ITERS):
        last = iteration + 1 == ITERS
        earlier = earlier_sum(vel, False)
        if small:
            pieces = gather_parts(earlier.astype(BF16), "tensor")
        else:
            pieces = [lax.psum(earlier, "tensor")]
        split = last and small
        if split:
            outs = [shape_of((rows, channels), BF16 if k else F32) for k in range(n_tensor)]
        else:
            outs = [shape_of((tokens, channels), F32 if last else BF16)]
        vels = call(
            functools.partial(iterate_kernel, len(pieces), rows, head_count, split),
            outs,
            [VMEM] * (len(pieces) + 7),
            [pltpu.VMEM((n_tensor, rows, channels), F32)],
            *pieces,
            step,
            start_all,
            factor,
            base,
            gram,
            folded,
            resid,
        )
        vel = vels[0]
    if small:
        drift = vels[0]
        for k in range(1, n_tensor):
            drift = drift + swap(vels[k], "tensor", k).astype(F32)
    else:
        drift = lax.psum_scatter(vel, "tensor", scatter_dimension=0, tiled=True)
    return (start_latent + earlier_sum(drift, True))[None]


def solution(mesh):
    return jax.shard_map(
        local,
        mesh=mesh,
        in_specs=(
            P(("groups", "tensor"), None),
            P(("groups", "tm")),
            P(("groups", "tm")),
            P("tm", None),
            P(None, "tensor"),
            P(None, "tensor"),
            P("tensor", None),
            P("tm", None),
        ),
        out_specs=P(("groups", "tm"), "tensor", None),
        check_vma=False,
    )
```

```python
import functools
import math

import jax
import jax.numpy as jnp
from jax import lax
from jax.experimental import pallas as pl
from jax.experimental.pallas import tpu as pltpu
from jax.sharding import PartitionSpec as P


HD = 128
LANES = 128
ITERS = 2
NORM_EPS = 1e-06
STEP_DIVISOR = 64.0
F32 = jnp.float32
BF16 = jnp.bfloat16
VMEM = pl.BlockSpec(memory_space=pltpu.VMEM)
SMEM = pl.BlockSpec(memory_space=pltpu.SMEM)
HBM = pl.BlockSpec(memory_space=pltpu.HBM)


def embedding_of(time_index, width):
    half_width = width // 2
    frequency = jnp.exp(
        -math.log(10000.0) * jnp.arange(half_width).astype(F32) / half_width
    )
    angles = time_index.astype(F32)[:, None] * frequency[None, :]
    return jnp.concatenate([jnp.cos(angles), jnp.sin(angles)], axis=1)


def is_small(axis):
    return lax.axis_size(axis) in (2, 4)


def swap(value, axis, k):
    n = lax.axis_size(axis)
    return lax.ppermute(value, axis, [(i, i ^ k) for i in range(n)])


def gather_parts(value, axis):
    if is_small(axis):
        return [value] + [swap(value, axis, k) for k in range(1, lax.axis_size(axis))]
    return [lax.all_gather(value, axis, axis=0, tiled=True)]


def gather_weight_parts(value, axis):
    n = lax.axis_size(axis)
    if n != 4:
        return gather_parts(value, axis)
    far = swap(value, axis, 2)
    near = swap(value, axis, 1)
    return [value, near, far, swap(far, axis, 1)]


def place(axis, parts, k):
    if parts == 1:
        return 0
    return lax.axis_index(axis) ^ k


def bdot(a, b):
    return jnp.dot(a, b, preferred_element_type=F32)


def bdot_t(a, b):
    return lax.dot_general(a, b, (((1,), (1,)), ((), ())), preferred_element_type=F32)


def split_terms(value, terms):
    out = []
    for _ in range(terms):
        piece = value.astype(BF16)
        out.append(piece)
        value = value - piece.astype(F32)
    return out


def run_copies(copies):
    for copy in copies:
        copy.start()
    return copies


def wait_copies(copies):
    for copy in copies:
        copy.wait()


def modulation_kernel(
    time_ref, weight_hbm, start_hbm, qkv_hbm, inw_hbm, out_ref, qkv_ref, inw_ref, weight_ref, start_ref, sems
):
    rows = start_ref.shape[0]
    half = weight_ref.shape[0] // 2
    pairs = (
        (weight_hbm, weight_ref),
        (start_hbm, start_ref),
        (inw_hbm, inw_ref),
        (qkv_hbm.at[:, pl.ds(0, qkv_ref.shape[1])], qkv_ref),
    )
    copies = run_copies(
        [pltpu.make_async_copy(a, b, sems.at[i]) for i, (a, b) in enumerate(pairs)]
    )
    index = lax.broadcasted_iota(jnp.int32, (16, half), 1).astype(F32)
    angles = time_ref[0].astype(F32) * jnp.exp(-math.log(10000.0) * index / half)
    embedding = jnp.concatenate([jnp.cos(angles), jnp.sin(angles)], axis=1).astype(BF16)
    wait_copies(copies[:2])
    result = bdot(embedding, weight_ref[...])
    out_ref[0:rows, :] = start_ref[...]
    for r in range(weight_ref.shape[1] // LANES):
        out_ref[rows + r : rows + r + 1, :] = result[0:1, r * LANES : (r + 1) * LANES]
    wait_copies(copies[2:])


def channel_columns(inw_ref, c, n):
    return inw_ref[:, :, c * LANES : (c + n) * LANES].reshape(-1, n * LANES)


def prepare_kernel(nm, weight_ref, *refs):
    inws, refs = refs[:nm], refs[nm:]
    inw_ref, mean_ref, gram_ref, step_ref = refs
    step_ref[...] = jnp.full(step_ref.shape, weight_ref[0].astype(F32) * (1.0 / STEP_DIVISOR))
    for k in range(nm):
        inw_ref[place("tm", nm, k)] = inws[k][...]
    channels, width = mean_ref.shape[0], inw_ref.shape[2]
    chunks = width // LANES
    total = jnp.zeros((channels, LANES), F32)
    for c in range(chunks):
        total = total + channel_columns(inw_ref, c, 1).astype(F32)
    mean = jnp.sum(total, axis=1, keepdims=True) * (1.0 / width)
    mean_b = jnp.broadcast_to(mean, mean_ref.shape)
    mean_ref[...] = mean_b
    gram = jnp.zeros((channels, channels), F32)
    for c in range(0, chunks, 6):
        piece = channel_columns(inw_ref, c, 6)
        gram = gram + bdot_t(piece, piece)
    mean_c = jnp.broadcast_to(mean, (channels, channels))
    gram = gram * (1.0 / width) - mean_c * mean_c.T
    for i, term in enumerate(split_terms(gram, 3)):
        gram_ref[i * channels : (i + 1) * channels, :] = term


def attend(x, factors, base, gram, head_count):
    twice = jnp.concatenate([x, x], axis=1)
    thrice = jnp.concatenate([twice, x], axis=1)
    heads = [slice(h * 3 * HD, (h + 1) * 3 * HD) for h in range(head_count)]
    quadratic = bdot(thrice, gram[...])
    raw = [bdot(twice, factors[:, cols]) for cols in heads]
    spread = jnp.sum(quadratic * x.astype(F32), axis=1, keepdims=True)
    scale = lax.rsqrt(jnp.maximum(spread, 0.0) + NORM_EPS)
    qkv = [(r * scale + base[0:1, cols]).astype(BF16) for r, cols in zip(raw, heads)]
    scores = [bdot_t(p[:, :HD], p[:, HD : 2 * HD]) * (1.0 / math.sqrt(HD)) for p in qkv]
    tops = [jnp.max(s, axis=1, keepdims=True) for s in scores]
    weights = [jnp.exp(s - t) for s, t in zip(scores, tops)]
    sums = [jnp.sum(w, axis=1, keepdims=True) for w in weights]
    probs = [(w / n).astype(BF16) for w, n in zip(weights, sums)]
    outs = [bdot(w, p[:, 2 * HD :]).astype(BF16) for w, p in zip(probs, qkv)]
    return outs[0] if head_count == 1 else jnp.concatenate(outs, axis=1)


def setup_kernel(nt, nm, block, *refs):
    msgs, refs = refs[:nt], refs[nt:]
    inw_ref, mean_ref, near_ref, qkv_hbm, out_w_hbm = refs[:5]
    refs = refs[5:]
    factor_ref, base_ref, start_ref, gate_ref, out_w_ref = refs[:5]
    start_s, mod_s, gate_s, z_s, qkv_s, sems = refs[5:]
    near = near_ref.shape[1] // block
    count = factor_ref.shape[1] // block
    copies = run_copies(
        [
            pltpu.make_async_copy(
                qkv_hbm.at[:, pl.ds(n * block, block)],
                qkv_s.at[:, pl.ds((n - near) * block, block)],
                sems.at[n - near],
            )
            for n in range(near, count)
        ]
        + [pltpu.make_async_copy(out_w_hbm, out_w_ref, sems.at[count - near])]
    )
    for k, msg in enumerate(msgs):
        at = place("tensor", nt, k)
        start_s[at] = msg[0 : start_s.shape[1], :]
        mod_s[at, 0 : msg.shape[0] - start_s.shape[1], :] = msg[start_s.shape[1] :, :]
    channels, width = mean_ref.shape[0], z_s.shape[1]
    chunks = width // LANES
    per = 3 * chunks // nt

    def mod_row(r):
        return mod_s[r // per, r % per : r % per + 1, :]

    mean = mean_ref[...]
    first = jnp.zeros((channels + 16, block), F32)
    group = 6
    for g in range(0, chunks, group):
        for c in range(g, g + group):
            cols = slice(c * LANES, (c + 1) * LANES)
            centered = channel_columns(inw_ref, c, 1).astype(F32) - mean
            z_s[0:channels, cols] = (centered * (1.0 + mod_row(chunks + c))).astype(BF16)
            shift = jnp.broadcast_to(mod_row(c), (16, LANES)).astype(BF16)
            z_s[channels : channels + 16, cols] = shift
        cols = slice(g * LANES, (g + group) * LANES)
        first = first + bdot(z_s[:, cols], near_ref[cols, 0:block])

    def keep(result, n):
        at = slice(n * block, (n + 1) * block)
        high, low = split_terms(result[0:channels], 2)
        factor_ref[0:channels, at] = high
        factor_ref[channels : 2 * channels, at] = low
        base_ref[:, at] = result[channels : channels + 8]

    keep(first, 0)
    for p in range(nm):
        for r in range(chunks // nm):
            gate_s[p, r : r + 1, :] = mod_row(2 * chunks + p * (chunks // nm) + r)
        gate_ref[p] = gate_s[p].T
    start_ref[...] = start_s[...].reshape(start_ref.shape)

    for n in range(1, count):
        if n < near:
            weight = near_ref[:, n * block : (n + 1) * block]
        else:
            copies[n - near].wait()
            weight = qkv_s[:, (n - near) * block : (n - near + 1) * block]
        keep(bdot(z_s[...], weight), n)
    copies[count - near].wait()


def fold_parts(nm, first, heads, gate_ref, out_w_ref, inw_ref):
    folded, resid = 0.0, 0.0
    for i, head_ref in enumerate(heads):
        size, _ = head_ref.shape
        at = place("tm", nm, first + i)
        cols = pl.ds(pl.multiple_of(at * size, LANES), size)
        gate = gate_ref[at]
        gated = []
        for r in range(size // LANES):
            rows = head_ref[r * LANES : (r + 1) * LANES, :].astype(F32)
            gated.append((rows * gate[:, r : r + 1]).astype(BF16))
        folded = folded + bdot(out_w_ref[:, cols], jnp.concatenate(gated, axis=0))
        inw = inw_ref[:, :, cols].reshape(-1, size)
        resid = resid + bdot(inw, head_ref[...])
    return folded, resid


def attend_kernel(nm, early, head_count, *refs):
    heads, refs = refs[:early], refs[early:]
    start_ref, factor_ref, base_ref, gram_ref, gate_ref, out_w_ref, inw_ref = refs[:7]
    att_ref, fold_ref, resid_ref = refs[7:]
    x = start_ref[...].astype(BF16)
    fold_ref[...], resid_ref[...] = fold_parts(nm, 0, heads, gate_ref, out_w_ref, inw_ref)
    att_ref[...] = attend(x, factor_ref, base_ref, gram_ref, head_count)


def add_own_rows(result, residual, rows):
    first = lax.axis_index("tensor") * rows
    at = lax.broadcasted_iota(jnp.int32, result.shape, 0)
    return result + jnp.where((at >= first) & (at < first + rows), residual, 0.0)


def fold_kernel(nm, late, rows, *refs):
    heads, refs = refs[:late], refs[late:]
    step_ref, gate_ref, out_w_ref, inw_ref, fold_in, resid_in, att_ref, start_ref = refs[:8]
    fold_ref, resid_ref, vel_ref = refs[8:]
    channels = resid_in.shape[0]
    total, resid = fold_in[...], resid_in[...]
    if late:
        more = fold_parts(nm, nm - late, heads, gate_ref, out_w_ref, inw_ref)
        total, resid = total + more[0], resid + more[1]
    folded = total.astype(BF16)
    fold_ref[...] = folded
    for i, term in enumerate(split_terms(resid, 2)):
        resid_ref[i * channels : (i + 1) * channels, :] = term
    x = start_ref[...].astype(BF16)
    vel = bdot(att_ref[...], folded)
    residual = bdot(jnp.concatenate([x, x], axis=1), resid_ref[...])
    vel_ref[...] = (add_own_rows(vel, residual, rows) * step_ref[0:1, :]).astype(vel_ref.dtype)


def iterate_kernel(nparts, rows, head_count, split, *refs):
    parts, refs = refs[:nparts], refs[nparts:]
    step_ref, start_ref, factor_ref, base_ref, gram_ref, fold_ref, resid_ref = refs[:7]
    outs = refs[7:-1]
    vel_s = refs[-1]
    guess = start_ref[...]
    for part in parts:
        guess = guess + part[...].astype(F32)
    x = guess.astype(BF16)
    attended = attend(x, factor_ref, base_ref, gram_ref, head_count)
    vel = bdot(attended, fold_ref[...])
    residual = bdot(jnp.concatenate([x, x], axis=1), resid_ref[...])
    vel = add_own_rows(vel, residual, rows) * step_ref[0:1, :]
    if not split:
        outs[0][...] = vel.astype(outs[0].dtype)
        return
    vel_s[...] = vel.reshape(vel_s.shape)
    for k in range(len(outs)):
        outs[k][...] = vel_s[lax.axis_index("tensor") ^ k]


def shape_of(shape, dtype):
    return jax.ShapeDtypeStruct(shape, dtype)


def call(kernel, outs, in_specs, scratch, *args, cost=4 * 2**20, limit=8):
    args = [
        pltpu.with_memory_space_constraint(arg, pltpu.HBM) if spec is HBM else arg
        for arg, spec in zip(args, in_specs)
    ]
    return pl.pallas_call(
        kernel,
        out_shape=outs,
        in_specs=in_specs,
        out_specs=[VMEM] * len(outs),
        scratch_shapes=scratch,
        compiler_params=pltpu.CompilerParams(vmem_limit_bytes=limit * 2**20),
        cost_estimate=pl.CostEstimate(flops=0, bytes_accessed=cost, transcendentals=0),
    )(*args)


def sum_earlier(parts, inclusive):
    me = lax.axis_index("tm")
    total = parts[0].astype(F32) if inclusive else jnp.zeros(parts[0].shape, F32)
    for k in range(1, len(parts)):
        total = total + jnp.where((me ^ k) < me, parts[k].astype(F32), 0.0)
    return total


def earlier_sum(value, inclusive):
    if is_small("tm"):
        return sum_earlier(gather_parts(value, "tm"), inclusive)
    everything = lax.all_gather(value, "tm").astype(F32)
    index = jnp.arange(everything.shape[0]).reshape((-1,) + (1,) * value.ndim)
    me = lax.axis_index("tm")
    keep = index <= me if inclusive else index < me
    return jnp.sum(jnp.where(keep, everything, 0.0), axis=0)


def local(
    start_latent,
    time_index,
    step_weight,
    in_weight,
    mod_weight,
    qkv_weight,
    out_weight,
    head_weight,
):
    rows, channels = start_latent.shape
    n_tensor = lax.axis_size("tensor")
    tokens = rows * n_tensor
    width = in_weight.shape[1]
    chunks = width // LANES
    head_count = qkv_weight.shape[1] // (3 * HD)
    span = out_weight.shape[0]

    inw_parts = gather_weight_parts(in_weight, "tm")
    span_cols = qkv_weight.shape[1]
    block = 4 * LANES if span_cols % (4 * LANES) == 0 else span_cols
    near = max(1, span_cols // block // 3)
    far = max(1, span_cols // block - near)
    small = is_small("tensor") and mod_weight.shape[1] % LANES == 0
    if small:
        mod_rows = mod_weight.shape[1] // LANES
        message, qkv_near, inw_parts[0] = call(
            modulation_kernel,
            [
                shape_of((rows + mod_rows, LANES), F32),
                shape_of((width, near * block), BF16),
                shape_of(inw_parts[0].shape, BF16),
            ],
            [SMEM, HBM, HBM, HBM, HBM],
            [
                pltpu.VMEM(mod_weight.shape, BF16),
                pltpu.VMEM(start_latent.shape, F32),
                pltpu.SemaphoreType.DMA((4,)),
            ],
            time_index,
            mod_weight,
            start_latent,
            qkv_weight,
            inw_parts[0],
        )
        messages = gather_parts(message, "tensor")
        block_rows = rows
    else:
        embedding = embedding_of(time_index, mod_weight.shape[0]).astype(BF16)
        qkv_near = qkv_weight[:, : near * block]
        mod_part = jnp.dot(embedding, mod_weight, preferred_element_type=F32)
        modulation = lax.all_gather(mod_part, "tensor", axis=1, tiled=True)
        start_all = lax.all_gather(start_latent, "tensor", axis=0, tiled=True)
        messages = [jnp.concatenate([start_all, modulation.reshape(-1, LANES)], axis=0)]
        block_rows = tokens
    nt, nm = len(messages), len(inw_parts)
    mod_rows = messages[0].shape[0] - block_rows
    padded = -(-mod_rows // 8) * 8
    gate_rows = -(-(chunks // nm) // 8) * 8
    inw_all, mean, gram, step = call(
        functools.partial(prepare_kernel, nm),
        [
            shape_of((nm, channels // nm, width), BF16),
            shape_of((channels, LANES), F32),
            shape_of((3 * channels, channels), BF16),
            shape_of((8, LANES), F32),
        ],
        [SMEM] + [VMEM] * nm,
        [],
        step_weight,
        *inw_parts,
        limit=16,
    )
    factor, base, start_all, gate, out_near = call(
        functools.partial(setup_kernel, nt, nm, block),
        [
            shape_of((2 * channels, span_cols), BF16),
            shape_of((8, span_cols), F32),
            shape_of((tokens, channels), F32),
            shape_of((nm, LANES, gate_rows), F32),
            shape_of(out_weight.shape, BF16),
        ],
        [VMEM] * (nt + 3) + [HBM, HBM],
        [
            pltpu.VMEM((nt, block_rows, channels), F32),
            pltpu.VMEM((nt, padded, LANES), F32),
            pltpu.VMEM((nm, gate_rows, LANES), F32),
            pltpu.VMEM((channels + 16, width), BF16),
            pltpu.VMEM((width, far * block), BF16),
            pltpu.SemaphoreType.DMA((far + 1,)),
        ],
        *messages,
        inw_all,
        mean,
        qkv_near,
        qkv_weight,
        out_weight,
        limit=32,
    )
    head_parts = gather_weight_parts(head_weight, "tm")
    late = 1 if nm > 1 else 0
    early = nm - late
    attended, fold_part, resid_part = call(
        functools.partial(attend_kernel, nm, early, head_count),
        [
            shape_of((tokens, head_count * HD), BF16),
            shape_of((span, channels), F32),
            shape_of((channels, channels), F32),
        ],
        [VMEM] * (early + 7),
        [],
        *head_parts[:early],
        start_all,
        factor,
        base,
        gram,
        gate,
        out_near,
        inw_all,
        limit=16,
    )
    folded, resid, vel = call(
        functools.partial(fold_kernel, nm, late, rows),
        [
            shape_of((span, channels), BF16),
            shape_of((2 * channels, channels), BF16),
            shape_of((tokens, channels), BF16),
        ],
        [VMEM] * (late + 8),
        [],
        *head_parts[early:],
        step,
        gate,
        out_near,
        inw_all,
        fold_part,
        resid_part,
        attended,
        start_all,
        limit=16,
    )
    small = is_small("tensor")
    for iteration in range(1, ITERS):
        last = iteration + 1 == ITERS
        earlier = earlier_sum(vel, False)
        if small:
            pieces = gather_parts(earlier.astype(BF16), "tensor")
        else:
            pieces = [lax.psum(earlier, "tensor")]
        split = last and small
        if split:
            outs = [shape_of((rows, channels), F32)] * n_tensor
        else:
            outs = [shape_of((tokens, channels), F32 if last else BF16)]
        vels = call(
            functools.partial(iterate_kernel, len(pieces), rows, head_count, split),
            outs,
            [VMEM] * (len(pieces) + 7),
            [pltpu.VMEM((n_tensor, rows, channels), F32)],
            *pieces,
            step,
            start_all,
            factor,
            base,
            gram,
            folded,
            resid,
        )
        vel = vels[0]
    if small:
        drift = vels[0]
        for k in range(1, n_tensor):
            drift = drift + swap(vels[k], "tensor", k)
    else:
        drift = lax.psum_scatter(vel, "tensor", scatter_dimension=0, tiled=True)
    return (start_latent + earlier_sum(drift, True))[None]


def solution(mesh):
    return jax.shard_map(
        local,
        mesh=mesh,
        in_specs=(
            P(("groups", "tensor"), None),
            P(("groups", "tm")),
            P(("groups", "tm")),
            P("tm", None),
            P(None, "tensor"),
            P(None, "tensor"),
            P("tensor", None),
            P("tm", None),
        ),
        out_specs=P(("groups", "tm"), "tensor", None),
        check_vma=False,
    )
```

```python
import functools
import math

import jax
import jax.numpy as jnp
from jax import lax
from jax.experimental import pallas as pl
from jax.experimental.pallas import tpu as pltpu
from jax.sharding import PartitionSpec as P


HD = 128
LANES = 128
ITERS = 2
NORM_EPS = 1e-06
STEP_DIVISOR = 64.0
F32 = jnp.float32
BF16 = jnp.bfloat16
VMEM = pl.BlockSpec(memory_space=pltpu.VMEM)
SMEM = pl.BlockSpec(memory_space=pltpu.SMEM)
HBM = pl.BlockSpec(memory_space=pltpu.HBM)


def embedding_of(time_index, width):
    half_width = width // 2
    frequency = jnp.exp(
        -math.log(10000.0) * jnp.arange(half_width).astype(F32) / half_width
    )
    angles = time_index.astype(F32)[:, None] * frequency[None, :]
    return jnp.concatenate([jnp.cos(angles), jnp.sin(angles)], axis=1)


def is_small(axis):
    return lax.axis_size(axis) in (2, 4)


def swap(value, axis, k):
    n = lax.axis_size(axis)
    return lax.ppermute(value, axis, [(i, i ^ k) for i in range(n)])


def gather_parts(value, axis):
    if is_small(axis):
        return [value] + [swap(value, axis, k) for k in range(1, lax.axis_size(axis))]
    return [lax.all_gather(value, axis, axis=0, tiled=True)]


def gather_weight_parts(value, axis):
    n = lax.axis_size(axis)
    if n != 4:
        return gather_parts(value, axis)
    far = swap(value, axis, 2)
    near = swap(value, axis, 1)
    return [value, near, far, swap(far, axis, 1)]


def place(axis, parts, k):
    if parts == 1:
        return 0
    return lax.axis_index(axis) ^ k


def bdot(a, b):
    return jnp.dot(a, b, preferred_element_type=F32)


def bdot_t(a, b):
    return lax.dot_general(a, b, (((1,), (1,)), ((), ())), preferred_element_type=F32)


def split_terms(value, terms):
    out = []
    for _ in range(terms):
        piece = value.astype(BF16)
        out.append(piece)
        value = value - piece.astype(F32)
    return out


def run_copies(copies):
    for copy in copies:
        copy.start()
    return copies


def wait_copies(copies):
    for copy in copies:
        copy.wait()


def modulation_kernel(
    time_ref, weight_hbm, start_hbm, qkv_hbm, inw_hbm, out_ref, qkv_ref, inw_ref, weight_ref, start_ref, out_s, sems
):
    rows = start_ref.shape[0]
    half = weight_ref.shape[0] // 2
    pairs = (
        (weight_hbm, weight_ref),
        (start_hbm, start_ref),
        (inw_hbm, inw_ref),
        (qkv_hbm.at[:, pl.ds(0, qkv_ref.shape[1])], qkv_ref),
    )
    copies = run_copies(
        [pltpu.make_async_copy(a, b, sems.at[i]) for i, (a, b) in enumerate(pairs)]
    )
    index = lax.broadcasted_iota(jnp.int32, (16, half), 1).astype(F32)
    angles = time_ref[0].astype(F32) * jnp.exp(-math.log(10000.0) * index / half)
    embedding = jnp.concatenate([jnp.cos(angles), jnp.sin(angles)], axis=1).astype(BF16)
    wait_copies(copies[:2])
    result = bdot(embedding, weight_ref[...])
    out_s[0:rows, :] = start_ref[...]
    for r in range(weight_ref.shape[1] // LANES):
        out_s[rows + r : rows + r + 1, :] = result[0:1, r * LANES : (r + 1) * LANES]
    out_ref[...] = out_s[...].astype(BF16)
    wait_copies(copies[2:])


def channel_columns(inw_ref, c, n):
    return inw_ref[:, :, c * LANES : (c + n) * LANES].reshape(-1, n * LANES)


def prepare_kernel(nm, weight_ref, *refs):
    inws, refs = refs[:nm], refs[nm:]
    inw_ref, mean_ref, gram_ref, step_ref = refs
    step_ref[...] = jnp.full(step_ref.shape, weight_ref[0].astype(F32) * (1.0 / STEP_DIVISOR))
    for k in range(nm):
        inw_ref[place("tm", nm, k)] = inws[k][...]
    channels, width = mean_ref.shape[0], inw_ref.shape[2]
    chunks = width // LANES
    total = jnp.zeros((channels, LANES), F32)
    for c in range(chunks):
        total = total + channel_columns(inw_ref, c, 1).astype(F32)
    mean = jnp.sum(total, axis=1, keepdims=True) * (1.0 / width)
    mean_b = jnp.broadcast_to(mean, mean_ref.shape)
    mean_ref[...] = mean_b
    gram = jnp.zeros((channels, channels), F32)
    for c in range(0, chunks, 6):
        piece = channel_columns(inw_ref, c, 6)
        gram = gram + bdot_t(piece, piece)
    mean_c = jnp.broadcast_to(mean, (channels, channels))
    gram = gram * (1.0 / width) - mean_c * mean_c.T
    for i, term in enumerate(split_terms(gram, 3)):
        gram_ref[i * channels : (i + 1) * channels, :] = term


def attend(x, factors, base, gram, head_count):
    twice = jnp.concatenate([x, x], axis=1)
    thrice = jnp.concatenate([twice, x], axis=1)
    heads = [slice(h * 3 * HD, (h + 1) * 3 * HD) for h in range(head_count)]
    quadratic = bdot(thrice, gram[...])
    raw = [bdot(twice, factors[:, cols]) for cols in heads]
    spread = jnp.sum(quadratic * x.astype(F32), axis=1, keepdims=True)
    scale = lax.rsqrt(jnp.maximum(spread, 0.0) + NORM_EPS)
    qkv = [(r * scale + base[0:1, cols]).astype(BF16) for r, cols in zip(raw, heads)]
    scores = [bdot_t(p[:, :HD], p[:, HD : 2 * HD]) * (1.0 / math.sqrt(HD)) for p in qkv]
    tops = [jnp.max(s, axis=1, keepdims=True) for s in scores]
    weights = [jnp.exp(s - t) for s, t in zip(scores, tops)]
    sums = [jnp.sum(w, axis=1, keepdims=True) for w in weights]
    probs = [(w / n).astype(BF16) for w, n in zip(weights, sums)]
    outs = [bdot(w, p[:, 2 * HD :]).astype(BF16) for w, p in zip(probs, qkv)]
    return outs[0] if head_count == 1 else jnp.concatenate(outs, axis=1)


def setup_kernel(nt, nm, block, *refs):
    msgs, refs = refs[:nt], refs[nt:]
    inw_ref, mean_ref, near_ref, _, qkv_hbm = refs[:5]
    refs = refs[5:]
    factor_ref, base_ref, start_ref, gate_ref = refs[:4]
    start_s, mod_s, gate_s, z_s, qkv_s, sems = refs[4:]
    near = near_ref.shape[1] // block
    count = factor_ref.shape[1] // block
    half = z_s.shape[1] // 2
    copies = run_copies(
        [
            pltpu.make_async_copy(
                qkv_hbm.at[pl.ds(p * half, half), pl.ds(n * block, block)],
                qkv_s.at[pl.ds(p * half, half), pl.ds((n - near) * block, block)],
                sems.at[2 * (n - near) + p],
            )
            for n in range(near, count)
            for p in range(2)
        ]
    )
    for k, msg in enumerate(msgs):
        at = place("tensor", nt, k)
        start_s[at] = msg[0 : start_s.shape[1], :].astype(F32)
        mod_s[at, 0 : msg.shape[0] - start_s.shape[1], :] = msg[start_s.shape[1] :, :].astype(F32)
    channels, width = mean_ref.shape[0], z_s.shape[1]
    chunks = width // LANES
    per = 3 * chunks // nt

    def mod_row(r):
        return mod_s[r // per, r % per : r % per + 1, :]

    mean = mean_ref[...]
    first = jnp.zeros((channels + 16, block), F32)
    group = 6
    for g in range(0, chunks, group):
        for c in range(g, g + group):
            cols = slice(c * LANES, (c + 1) * LANES)
            centered = channel_columns(inw_ref, c, 1).astype(F32) - mean
            z_s[0:channels, cols] = (centered * (1.0 + mod_row(chunks + c))).astype(BF16)
            shift = jnp.broadcast_to(mod_row(c), (16, LANES)).astype(BF16)
            z_s[channels : channels + 16, cols] = shift
        cols = slice(g * LANES, (g + group) * LANES)
        first = first + bdot(z_s[:, cols], near_ref[cols, 0:block])

    def keep(result, n):
        at = slice(n * block, (n + 1) * block)
        high, low = split_terms(result[0:channels], 2)
        factor_ref[0:channels, at] = high
        factor_ref[channels : 2 * channels, at] = low
        base_ref[:, at] = result[channels : channels + 8]

    keep(first, 0)
    for p in range(nm):
        for r in range(chunks // nm):
            gate_s[p, r : r + 1, :] = mod_row(2 * chunks + p * (chunks // nm) + r)
        gate_ref[p] = gate_s[p].T
    start_ref[...] = start_s[...].reshape(start_ref.shape)

    for n in range(1, count):
        at = slice((n - near) * block, (n - near + 1) * block)
        result = 0.0
        for p in range(2):
            rows_at = slice(p * half, (p + 1) * half)
            if n < near:
                weight = near_ref[rows_at, n * block : (n + 1) * block]
            else:
                copies[2 * (n - near) + p].wait()
                weight = qkv_s[rows_at, at]
            result = result + bdot(z_s[:, rows_at], weight)
        keep(result, n)


def fold_parts(nm, first, heads, gate_ref, out_w_ref, inw_ref):
    folded, resid = 0.0, 0.0
    for i, head_ref in enumerate(heads):
        size, _ = head_ref.shape
        at = place("tm", nm, first + i)
        cols = pl.ds(pl.multiple_of(at * size, LANES), size)
        gate = gate_ref[at]
        gated = []
        for r in range(size // LANES):
            rows = head_ref[r * LANES : (r + 1) * LANES, :].astype(F32)
            gated.append((rows * gate[:, r : r + 1]).astype(BF16))
        folded = folded + bdot(out_w_ref[:, cols], jnp.concatenate(gated, axis=0))
        inw = inw_ref[:, :, cols].reshape(-1, size)
        resid = resid + bdot(inw, head_ref[...])
    return folded, resid


def attend_kernel(nm, early, head_count, *refs):
    heads, refs = refs[:early], refs[early:]
    start_ref, factor_ref, base_ref, gram_ref, gate_ref, out_w_ref, inw_ref = refs[:7]
    att_ref, fold_ref, resid_ref = refs[7:]
    x = start_ref[...].astype(BF16)
    fold_ref[...], resid_ref[...] = fold_parts(nm, 0, heads, gate_ref, out_w_ref, inw_ref)
    att_ref[...] = attend(x, factor_ref, base_ref, gram_ref, head_count)


def add_own_rows(result, residual, rows):
    first = lax.axis_index("tensor") * rows
    at = lax.broadcasted_iota(jnp.int32, result.shape, 0)
    return result + jnp.where((at >= first) & (at < first + rows), residual, 0.0)


def fold_kernel(nm, late, rows, *refs):
    heads, refs = refs[:late], refs[late:]
    step_ref, gate_ref, out_w_ref, inw_ref, fold_in, resid_in, att_ref, start_ref = refs[:8]
    fold_ref, resid_ref, vel_ref = refs[8:]
    channels = resid_in.shape[0]
    total, resid = fold_in[...], resid_in[...]
    if late:
        more = fold_parts(nm, nm - late, heads, gate_ref, out_w_ref, inw_ref)
        total, resid = total + more[0], resid + more[1]
    folded = total.astype(BF16)
    fold_ref[...] = folded
    for i, term in enumerate(split_terms(resid, 2)):
        resid_ref[i * channels : (i + 1) * channels, :] = term
    x = start_ref[...].astype(BF16)
    vel = bdot(att_ref[...], folded)
    residual = bdot(jnp.concatenate([x, x], axis=1), resid_ref[...])
    vel_ref[...] = (add_own_rows(vel, residual, rows) * step_ref[0:1, :]).astype(vel_ref.dtype)


def iterate_kernel(nparts, rows, head_count, split, *refs):
    parts, refs = refs[:nparts], refs[nparts:]
    step_ref, start_ref, factor_ref, base_ref, gram_ref, fold_ref, resid_ref = refs[:7]
    outs = refs[7:-1]
    vel_s = refs[-1]
    guess = start_ref[...]
    for part in parts:
        guess = guess + part[...].astype(F32)
    x = guess.astype(BF16)
    attended = attend(x, factor_ref, base_ref, gram_ref, head_count)
    vel = bdot(attended, fold_ref[...])
    residual = bdot(jnp.concatenate([x, x], axis=1), resid_ref[...])
    vel = add_own_rows(vel, residual, rows) * step_ref[0:1, :]
    if not split:
        outs[0][...] = vel.astype(outs[0].dtype)
        return
    vel_s[...] = vel.reshape(vel_s.shape)
    for k in range(len(outs)):
        outs[k][...] = vel_s[lax.axis_index("tensor") ^ k].astype(outs[k].dtype)


def shape_of(shape, dtype):
    return jax.ShapeDtypeStruct(shape, dtype)


def call(kernel, outs, in_specs, scratch, *args, cost=4 * 2**20, limit=8):
    args = [
        pltpu.with_memory_space_constraint(arg, pltpu.HBM) if spec is HBM else arg
        for arg, spec in zip(args, in_specs)
    ]
    return pl.pallas_call(
        kernel,
        out_shape=outs,
        in_specs=in_specs,
        out_specs=[VMEM] * len(outs),
        scratch_shapes=scratch,
        compiler_params=pltpu.CompilerParams(vmem_limit_bytes=limit * 2**20),
        cost_estimate=pl.CostEstimate(flops=0, bytes_accessed=cost, transcendentals=0),
    )(*args)


def sum_earlier(parts, inclusive):
    me = lax.axis_index("tm")
    total = parts[0].astype(F32) if inclusive else jnp.zeros(parts[0].shape, F32)
    for k in range(1, len(parts)):
        total = total + jnp.where((me ^ k) < me, parts[k].astype(F32), 0.0)
    return total


def earlier_sum(value, inclusive):
    if is_small("tm"):
        parts = gather_parts(value.astype(BF16), "tm")
        return sum_earlier([value] + parts[1:], inclusive)
    everything = lax.all_gather(value, "tm").astype(F32)
    index = jnp.arange(everything.shape[0]).reshape((-1,) + (1,) * value.ndim)
    me = lax.axis_index("tm")
    keep = index <= me if inclusive else index < me
    return jnp.sum(jnp.where(keep, everything, 0.0), axis=0)


def local(
    start_latent,
    time_index,
    step_weight,
    in_weight,
    mod_weight,
    qkv_weight,
    out_weight,
    head_weight,
):
    rows, channels = start_latent.shape
    n_tensor = lax.axis_size("tensor")
    tokens = rows * n_tensor
    width = in_weight.shape[1]
    chunks = width // LANES
    head_count = qkv_weight.shape[1] // (3 * HD)
    span = out_weight.shape[0]

    inw_parts = gather_weight_parts(in_weight, "tm")
    span_cols = qkv_weight.shape[1]
    block = 4 * LANES if span_cols % (4 * LANES) == 0 else span_cols
    near = max(1, span_cols // block // 3)
    far = max(1, span_cols // block - near)
    small = is_small("tensor") and mod_weight.shape[1] % LANES == 0
    if small:
        mod_rows = mod_weight.shape[1] // LANES
        message, qkv_near, inw_parts[0] = call(
            modulation_kernel,
            [
                shape_of((rows + mod_rows, LANES), BF16),
                shape_of((width, near * block), BF16),
                shape_of(inw_parts[0].shape, BF16),
            ],
            [SMEM, HBM, HBM, HBM, HBM],
            [
                pltpu.VMEM(mod_weight.shape, BF16),
                pltpu.VMEM(start_latent.shape, F32),
                pltpu.VMEM((rows + mod_rows, LANES), F32),
                pltpu.SemaphoreType.DMA((4,)),
            ],
            time_index,
            mod_weight,
            start_latent,
            qkv_weight,
            inw_parts[0],
        )
        messages = gather_parts(message, "tensor")
        block_rows = rows
    else:
        embedding = embedding_of(time_index, mod_weight.shape[0]).astype(BF16)
        qkv_near = qkv_weight[:, : near * block]
        mod_part = jnp.dot(embedding, mod_weight, preferred_element_type=F32)
        modulation = lax.all_gather(mod_part, "tensor", axis=1, tiled=True)
        start_all = lax.all_gather(start_latent, "tensor", axis=0, tiled=True)
        messages = [jnp.concatenate([start_all, modulation.reshape(-1, LANES)], axis=0)]
        block_rows = tokens
    nt, nm = len(messages), len(inw_parts)
    mod_rows = messages[0].shape[0] - block_rows
    padded = -(-mod_rows // 8) * 8
    gate_rows = -(-(chunks // nm) // 8) * 8
    inw_all, mean, gram, step = call(
        functools.partial(prepare_kernel, nm),
        [
            shape_of((nm, channels // nm, width), BF16),
            shape_of((channels, LANES), F32),
            shape_of((3 * channels, channels), BF16),
            shape_of((8, LANES), F32),
        ],
        [SMEM] + [VMEM] * nm,
        [],
        step_weight,
        *inw_parts,
        limit=16,
    )
    factor, base, start_all, gate = call(
        functools.partial(setup_kernel, nt, nm, block),
        [
            shape_of((2 * channels, span_cols), BF16),
            shape_of((8, span_cols), F32),
            shape_of((tokens, channels), F32),
            shape_of((nm, LANES, gate_rows), F32),
        ],
        [VMEM] * (nt + 4) + [HBM],
        [
            pltpu.VMEM((nt, block_rows, channels), F32),
            pltpu.VMEM((nt, padded, LANES), F32),
            pltpu.VMEM((nm, gate_rows, LANES), F32),
            pltpu.VMEM((channels + 16, width), BF16),
            pltpu.VMEM((width, far * block), BF16),
            pltpu.SemaphoreType.DMA((2 * far,)),
        ],
        *messages,
        inw_all,
        mean,
        qkv_near,
        out_weight,
        qkv_weight,
        limit=32,
    )
    head_parts = gather_weight_parts(head_weight, "tm")
    late = 1 if nm > 1 else 0
    early = nm - late
    attended, fold_part, resid_part = call(
        functools.partial(attend_kernel, nm, early, head_count),
        [
            shape_of((tokens, head_count * HD), BF16),
            shape_of((span, channels), F32),
            shape_of((channels, channels), F32),
        ],
        [VMEM] * (early + 7),
        [],
        *head_parts[:early],
        start_all,
        factor,
        base,
        gram,
        gate,
        out_weight,
        inw_all,
        limit=16,
    )
    folded, resid, vel = call(
        functools.partial(fold_kernel, nm, late, rows),
        [
            shape_of((span, channels), BF16),
            shape_of((2 * channels, channels), BF16),
            shape_of((tokens, channels), BF16),
        ],
        [VMEM] * (late + 8),
        [],
        *head_parts[early:],
        step,
        gate,
        out_weight,
        inw_all,
        fold_part,
        resid_part,
        attended,
        start_all,
        limit=16,
    )
    small = is_small("tensor")
    for iteration in range(1, ITERS):
        last = iteration + 1 == ITERS
        earlier = earlier_sum(vel, False)
        if small:
            pieces = gather_parts(earlier.astype(BF16), "tensor")
        else:
            pieces = [lax.psum(earlier, "tensor")]
        split = last and small
        if split:
            outs = [shape_of((rows, channels), BF16 if k else F32) for k in range(n_tensor)]
        else:
            outs = [shape_of((tokens, channels), F32 if last else BF16)]
        vels = call(
            functools.partial(iterate_kernel, len(pieces), rows, head_count, split),
            outs,
            [VMEM] * (len(pieces) + 7),
            [pltpu.VMEM((n_tensor, rows, channels), F32)],
            *pieces,
            step,
            start_all,
            factor,
            base,
            gram,
            folded,
            resid,
        )
        vel = vels[0]
    if small:
        drift = vels[0]
        for k in range(1, n_tensor):
            drift = drift + swap(vels[k], "tensor", k).astype(F32)
    else:
        drift = lax.psum_scatter(vel, "tensor", scatter_dimension=0, tiled=True)
    return (start_latent + earlier_sum(drift, True))[None]


def solution(mesh):
    return jax.shard_map(
        local,
        mesh=mesh,
        in_specs=(
            P(("groups", "tensor"), None),
            P(("groups", "tm")),
            P(("groups", "tm")),
            P("tm", None),
            P(None, "tensor"),
            P(None, "tensor"),
            P("tensor", None),
            P("tm", None),
        ),
        out_specs=P(("groups", "tm"), "tensor", None),
        check_vma=False,
    )
```
